128 devices in a mesh: gx: 8 (over z_lo, y), gy: 16 (over x, z_hi, core).
Axes of the slice: x: 4, y: 4, z: 4 (z_hi: 2, z_lo: 2; z = z_hi * 2 + z_lo), core: 2. Of those that a mesh axis runs over, the one named last changes fastest.
Arguments:
- initial_state: float32 [3, 256, 49152], P(None, 'gx', 'gy'), may hold values from -6 to 6
- beam_dir: float32 [3, 512], P(None, ('gx', 'gy')), may hold values from -4 to 4
- gate_obs: float32 [3, 128, 128, 32], P(None, ('gx', 'gy')), may hold values from -6 to 6
- slot_beam: int32 [128, 128, 32], P(('gx', 'gy')), may hold values from -1 to 3, as said below
- slot_cell: int32 [128, 128, 32], P(('gx', 'gy')), may hold values from 0 to 98303, as said below
Outputs:
- gradient: float32 [3, 256, 49152], P(None, 'gx', 'gy')
The draws below stay inside these ranges and needn't reach their ends.
Inputs may be any that keep to these rules, and one draw needn't show every extreme that they name: `slot_beam`: each of an owner's 4 beams fills exactly 512 slots over all of that owner's lists. In every list the used slots come first. Each owner's list for one common tile is full, so that tile receives 32 used slots from every owner. `slot_cell`: A cell index within the tile, of 32 x 32 x 96 cells with the streamwise index slowest and the vertical fastest; empty slots also hold a valid index.
All inputs are finite; a program needn't handle non-finite values.
Results may differ from the reference program's by a relative error of at most 0.00015.
Values sent between devices are 32-bit elements; how exact they have to be, the bound alone decides.
A program may use at most 128 MiB of HBM per device.

```python
import jax
import jax.numpy as jnp
from jax import lax

CX = 32
CY = 32
NZ = 96
STEPS = 3
GATES = 512
BEAMS_DEV = 4
CAP = 32
BEAMS = 512
NX = 256
NY = 512
N_GX = 8
N_GY = 16
DEVICES = 128


def slot_layout(key):
    peers = N_GX * N_GY
    half = CAP // 2
    base = jax.random.fold_in(key, 7001)
    favoured = jax.random.randint(jax.random.fold_in(base, 1), (), 0, peers).astype(jnp.int32)
    owner_keys = jax.random.split(jax.random.fold_in(base, 2), peers)

    def one_owner(owner_key):
        key_order, key_shift, key_gates = jax.random.split(owner_key, 3)
        order = jax.random.permutation(key_order, peers).astype(jnp.int32)
        position = jnp.argmax(order == favoured)
        order = order.at[position].set(order[0]).at[0].set(favoured)
        shifts = jax.random.randint(key_shift, (peers // 2,), -half, half + 1).astype(jnp.int32).at[0].set(half)
        counts = jnp.zeros((peers,), jnp.int32).at[order[0::2]].set(half + shifts).at[order[1::2]].set(half - shifts)
        starts = jnp.cumsum(counts) - counts
        slots = jnp.arange(CAP, dtype=jnp.int32)[None, :]
        live = slots < counts[:, None]
        gate = jnp.minimum(starts[:, None] + slots, peers * half - 1)
        gate_order = jax.random.permutation(key_gates, peers * half).astype(jnp.int32)
        return jnp.where(live, gate_order[gate] // GATES, -1).astype(jnp.int32)
    return jax.vmap(one_owner)(owner_keys)


def draw_slot_beam(key, part):
    return slot_layout(key)


def draw_slot_cell(key, part):
    peers = N_GX * N_GY
    return jax.random.randint(jax.random.fold_in(key, 7002), (peers, peers, CAP), 0, CX * CY * NZ).astype(jnp.int32)


def levels(rng, extent, cuts, least, high):
    level = 1.0
    for dim, blocks in cuts:
        draws = jax.random.uniform(jax.random.fold_in(jax.random.fold_in(rng, 6), dim), (blocks,), jnp.float32, least / len(cuts), high / len(cuts))
        level = level * jnp.repeat(jnp.exp(draws), extent[dim] // blocks).reshape((-1,) + (1,) * (len(extent) - 1 - dim))
    return level


def scatter_about(stream_key, shape, spread, reach, shards=(), kind=jnp.bfloat16):
    level = levels(stream_key, shape, shards, -0.22, 0.18) if shards else 1.0
    entries = jax.random.normal(stream_key, shape, jnp.float32) * spread * level
    return jnp.minimum(jnp.maximum(entries, -reach), reach).astype(kind)


def setup_inputs(seed: int = 0) -> dict:
    key_of = jax.random.split(jax.random.key(seed), 6)
    return {
        "initial_state": scatter_about(key_of[0], (3, NX, NY * NZ), 1.0, 6.0, ((1, 8), (2, 16)), jnp.float32),
        "beam_dir": scatter_about(key_of[1], (3, BEAMS), 0.7, 4.0, ((1, 128),), jnp.float32),
        "gate_obs": scatter_about(key_of[2], (STEPS, DEVICES, DEVICES, CAP), 1.0, 6.0, ((1, 128),), jnp.float32),
        "slot_beam": draw_slot_beam(jax.random.fold_in(key_of[5], 71), 0),
        "slot_cell": draw_slot_cell(jax.random.fold_in(key_of[5], 71), 0),
    }


TIME_STEP = 0.2
VISCOSITY = 0.5

def step_core(padded):
    centre = padded[:, 1:-1, NZ:-NZ]
    fore_cell = padded[:, 2:, NZ:-NZ]
    back_cell = padded[:, :-2, NZ:-NZ]
    right_cell = padded[:, 1:-1, 2 * NZ:]
    left_cell = padded[:, 1:-1, :-2 * NZ]
    level = lax.broadcasted_iota(jnp.int32, centre.shape, 2) % NZ
    upper_cell = jnp.where(level < NZ - 1, jnp.roll(centre, -1, axis=2), 0.0)
    lower_cell = jnp.where(level > 0, jnp.roll(centre, 1, axis=2), 0.0)
    laplace = fore_cell + back_cell + right_cell + left_cell + upper_cell + lower_cell - 6.0 * centre
    advect = centre[0:1] * (fore_cell - back_cell) * 0.5
    advect = advect + centre[1:2] * (right_cell - left_cell) * 0.5
    advect = advect + centre[2:3] * (upper_cell - lower_cell) * 0.5
    return centre + TIME_STEP * (VISCOSITY * laplace - advect)

def advance(state):
    return step_core(jnp.pad(state, ((0, 0), (1, 1), (NZ, NZ))))

def reference(initial_state, beam_dir, gate_obs, slot_beam, slot_cell):
    peers = N_GX * N_GY
    row_len = CY * NZ
    owner = jnp.arange(peers, dtype=jnp.int32)[:, None, None]
    tile = jnp.arange(peers, dtype=jnp.int32)[None, :, None]
    x_index = tile // N_GY * CX + slot_cell // row_len
    y_index = tile % N_GY * row_len + slot_cell % row_len
    used = slot_beam >= 0
    beam_ids = jnp.where(used, owner * BEAMS_DEV + slot_beam, peers * BEAMS_DEV).astype(jnp.int32)
    safe_ids = jnp.minimum(beam_ids, peers * BEAMS_DEV - 1)
    slot_dir = jnp.where(used[None], beam_dir[:, safe_ids], 0.0)
    flat_ids = beam_ids.reshape(-1)
    count = peers * BEAMS_DEV + 1

    def beam_mean(values):
        sums = jax.ops.segment_sum(values.reshape(-1), flat_ids, num_segments=count)
        return (sums / GATES)[flat_ids].reshape(values.shape)
    centred = [jnp.where(used, gate_obs[moment] - beam_mean(gate_obs[moment]), 0.0) for moment in range(STEPS)]

    def forcing(state, moment):
        seen = lax.optimization_barrier(jnp.sum(slot_dir * state[:, x_index, y_index], axis=0))
        misfit = jnp.where(used, seen - beam_mean(seen) - centred[moment], 0.0)
        return jnp.zeros_like(state).at[:, x_index, y_index].add(slot_dir * misfit)
    states = [initial_state]
    for moment in range(STEPS):
        states.append(advance(states[-1]))
    adjoint = forcing(states[STEPS], STEPS - 1)
    for moment in range(STEPS - 1, -1, -1):
        unused_out, pull = jax.vjp(advance, states[moment])
        adjoint = pull(adjoint)[0]
        if moment > 0:
            adjoint = adjoint + forcing(states[moment], moment - 1)
    return adjoint
```

```python
import functools

import jax
import jax.numpy as jnp
from jax import lax
from jax.experimental import pallas as pl
from jax.experimental.pallas import tpu as pltpu
from jax.sharding import PartitionSpec as P

NZ = 96
LANES = 128
GATES = 512
BEAMS = 4
STEPS = 3
TIME_STEP = 0.2
VISCOSITY = 0.5
CX = 32
CY = 32
HALO = 5
EDGE = 512
ROWS = 64
TOP = 16
WIDE = CY + 2 * HALO
COPIES = 2
MESH = pl.DeviceIdType.MESH
VMEM = pl.BlockSpec(memory_space=pltpu.VMEM)
SMEM = pl.BlockSpec(memory_space=pltpu.SMEM)
LIMIT = 60 * 1024 * 1024


def f32(*shape):
    return jax.ShapeDtypeStruct(shape, jnp.float32)


def at_mesh(peer, width):
    return (peer // width, lax.rem(peer, width))


def swap_kernel(state, msg, ylo, yhi, xlo, xhi, cll, clh, chl, chh, got, send, recv, list_send, list_recv, own):
    n_gx, n_gy = lax.axis_size("gx"), lax.axis_size("gy")
    count = n_gx * n_gy
    gx, gy = lax.axis_index("gx"), lax.axis_index("gy")
    me = gx * n_gy + gy
    barrier = pltpu.get_barrier_semaphore()

    def hail(i, carry):
        pl.semaphore_signal(barrier, inc=1, device_id=at_mesh(lax.rem(me + i, count), n_gy), device_id_type=MESH)
        return carry

    lax.fori_loop(1, count, hail, 0)
    pl.semaphore_wait(barrier, count - 1)
    row = CY * NZ
    low, high = pl.ds(0, EDGE), pl.ds(row - EDGE, EDGE)
    first, last = pl.ds(0, 8), pl.ds(CX - 8, 8)
    moves = [
        (state.at[:, last, :], xlo, 1, 0),
        (state.at[:, first, :], xhi, n_gx - 1, 0),
        (state.at[:, :, high], ylo, 0, 1),
        (state.at[:, :, low], yhi, 0, n_gy - 1),
        (state.at[:, last, high], cll, 1, 1),
        (state.at[:, last, low], clh, 1, n_gy - 1),
        (state.at[:, first, high], chl, n_gx - 1, 1),
        (state.at[:, first, low], chh, n_gx - 1, n_gy - 1),
    ]
    copies = []
    for i, (src, dst, dx, dy) in enumerate(moves):
        copy = pltpu.make_async_remote_copy(
            src_ref=src, dst_ref=dst, send_sem=send.at[i], recv_sem=recv.at[i],
            device_id=(lax.rem(gx + dx, n_gx), lax.rem(gy + dy, n_gy)), device_id_type=MESH,
        )
        copy.start()
        copies.append(copy)

    def post(i, carry):
        peer = lax.rem(me + i, count)
        pltpu.make_async_remote_copy(
            src_ref=msg.at[peer], dst_ref=got.at[me], send_sem=list_send, recv_sem=list_recv,
            device_id=at_mesh(peer, n_gy), device_id_type=MESH,
        ).start()
        return carry

    lax.fori_loop(1, count, post, 0)
    mine = pltpu.make_async_copy(msg.at[me], got.at[me], own)
    mine.start()
    mine.wait()
    for copy in copies:
        copy.wait()
    rest = pl.ds(0, count - 1)
    pltpu.make_async_remote_copy(
        src_ref=msg.at[rest], dst_ref=got.at[rest], send_sem=list_send, recv_sem=list_recv,
        device_id=at_mesh(lax.rem(me + 1, count), n_gy), device_id_type=MESH,
    ).wait()


def swap(state, msg):
    count = msg.shape[0]
    row = CY * NZ
    return pl.pallas_call(
        swap_kernel,
        out_shape=[
            f32(3, CX, EDGE), f32(3, CX, EDGE), f32(3, 8, row), f32(3, 8, row),
            f32(3, 8, EDGE), f32(3, 8, EDGE), f32(3, 8, EDGE), f32(3, 8, EDGE), f32(count, 2, LANES),
        ],
        in_specs=[VMEM] * 2,
        out_specs=[VMEM] * 9,
        scratch_shapes=[
            pltpu.SemaphoreType.DMA((8,)), pltpu.SemaphoreType.DMA((8,)),
            pltpu.SemaphoreType.DMA, pltpu.SemaphoreType.DMA, pltpu.SemaphoreType.DMA,
        ],
        compiler_params=pltpu.CompilerParams(collective_id=0, has_side_effects=True, vmem_limit_bytes=LIMIT),
        name="swap",
    )(state, msg)


def inside_flags():
    n_gx, n_gy = lax.axis_size("gx"), lax.axis_size("gy")
    gx, gy = lax.axis_index("gx"), lax.axis_index("gy")
    return (gx > 0, gx < n_gx - 1, gy > 0, gy < n_gy - 1)


def keep_rows(start, flags):
    lane = lax.broadcasted_iota(jnp.int32, (8, LANES), 1)
    keep = lane < NZ
    if start < TOP:
        keep = keep & flags[0]
    if start >= TOP + CX:
        keep = keep & flags[1]
    return keep


def keep_layer(y, lo, hi, flags):
    return ((y >= lo) | flags[2]) & ((y < hi) | flags[3])


def shift_up(v):
    return pltpu.roll(v, LANES - 1, 1)


def shift_down(v):
    return pltpu.roll(v, 1, 1)


def step_block(src, y, r):
    rows, fore, back = pl.ds(r, 8), pl.ds(r + 1, 8), pl.ds(r - 1, 8)
    centre = [src[c, y, rows, :] for c in range(3)]
    out = []
    for c in range(3):
        v = centre[c]
        f, b = src[c, y, fore, :], src[c, y, back, :]
        rt, lf = src[c, y + 1, rows, :], src[c, y - 1, rows, :]
        up, dn = shift_up(v), shift_down(v)
        lap = f + b + rt + lf + up + dn - 6.0 * v
        adv = centre[0] * (f - b) + centre[1] * (rt - lf) + centre[2] * (up - dn)
        out.append(v + (TIME_STEP * VISCOSITY) * lap - (0.5 * TIME_STEP) * adv)
    return out


def pull_block(src, sy, adj, y, r):
    rows, fore, back = pl.ds(r, 8), pl.ds(r + 1, 8), pl.ds(r - 1, 8)
    a = [adj[c, y, rows, :] for c in range(3)]
    v2 = src[2, sy, rows, :]
    u_f, u_b = src[0, sy, fore, :], src[0, sy, back, :]
    v_r, v_l = src[1, sy + 1, rows, :], src[1, sy - 1, rows, :]
    v_c = [src[c, sy, rows, :] for c in range(3)]
    out = []
    for c in range(3):
        f, b = adj[c, y, fore, :], adj[c, y, back, :]
        rt, lf = adj[c, y + 1, rows, :], adj[c, y - 1, rows, :]
        up, dn = shift_up(a[c]), shift_down(a[c])
        lap = f + b + rt + lf + up + dn - 6.0 * a[c]
        w = v2 * a[c]
        flow = (u_f * f - u_b * b) + (v_r * rt - v_l * lf) + (shift_up(w) - shift_down(w))
        out.append(a[c] + (TIME_STEP * VISCOSITY) * lap + (0.5 * TIME_STEP) * flow)
    grads = [jnp.zeros_like(a[0])] * 3
    for k in range(3):
        f, b = src[k, sy, fore, :], src[k, sy, back, :]
        rt, lf = src[k, sy + 1, rows, :], src[k, sy - 1, rows, :]
        grads[0] = grads[0] + a[k] * (f - b)
        grads[1] = grads[1] + a[k] * (rt - lf)
        grads[2] = grads[2] + a[k] * (shift_up(v_c[k]) - shift_down(v_c[k]))
    return [out[c] - (0.5 * TIME_STEP) * grads[c] for c in range(3)]


def regroup(block, quantity):
    lane = lax.broadcasted_iota(jnp.int32, (32, LANES), 1)
    out = None
    for k in range(4):
        piece = block[32 * k : 32 * k + 32, :]
        turn = (32 * (k - quantity)) % LANES
        if turn:
            piece = pltpu.roll(piece, turn, 1)
        out = piece if out is None else jnp.where(lane >= 32 * k, piece, out)
    return out


def same_list():
    a = lax.broadcasted_iota(jnp.int32, (LANES, LANES), 0) // 32
    b = lax.broadcasted_iota(jnp.int32, (LANES, LANES), 1) // 32
    return (a == b).astype(jnp.float32)


def diagonal():
    g = lax.broadcasted_iota(jnp.int32, (32, LANES), 0)
    lane = lax.broadcasted_iota(jnp.int32, (32, LANES), 1)
    return (lane % 32) == g


def forward_kernel(
    state, ylo, yhi, xlo, xhi, cll, clh, chl, chh, got,
    w0, w1, w2, resid, slots, packed, part,
    tab_a, tab_b, acc_a, acc_b, index, sem,
):
    flags = inside_flags()
    row = CY * NZ
    g0, g1 = got[:, 0, :], got[:, 1, :]
    cell = regroup(g0, 0).astype(jnp.int32)
    x = ((cell >> 10) * 171) >> 9
    rem = cell - x * row
    y = ((rem >> 5) * 171) >> 9
    z = rem - y * NZ
    lane = lax.broadcasted_iota(jnp.int32, (32, LANES), 1)
    packed[...] = (y * CX + x) * LANES + ((lane - z) & (LANES - 1))
    to_scalar = pltpu.make_async_copy(packed, index, sem)
    to_scalar.start()
    for j in range(4):
        slots[j] = regroup(g1, j)

    blank = jnp.zeros((ROWS, LANES), jnp.float32)

    def clear(i, carry):
        for c in range(3):
            w0[c, i] = blank
        return carry

    lax.fori_loop(0, WIDE, clear, 0)

    def put(c, yy, at, size, ref, rows, lanes, flag):
        v = ref[c, rows, lanes]
        if flag is not None:
            v = jnp.where(flag, v, 0.0)
        w0[c, yy, pl.ds(at, size), pl.ds(0, NZ)] = v

    for c in range(3):
        for yy in range(CY):
            lanes = pl.ds(yy * NZ, NZ)
            put(c, yy + HALO, TOP, CX, state, slice(None), lanes, None)
            put(c, yy + HALO, TOP - 8, 8, xlo, slice(None), lanes, flags[0])
            put(c, yy + HALO, TOP + CX, 8, xhi, slice(None), lanes, flags[1])
        for i in range(HALO):
            lanes = pl.ds(EDGE - (HALO - i) * NZ, NZ)
            put(c, i, TOP, CX, ylo, slice(None), lanes, flags[2])
            put(c, i, TOP - 8, 8, cll, slice(None), lanes, flags[0] & flags[2])
            put(c, i, TOP + CX, 8, chl, slice(None), lanes, flags[1] & flags[2])
            lanes = pl.ds(i * NZ, NZ)
            yy = i + HALO + CY
            put(c, yy, TOP, CX, yhi, slice(None), lanes, flags[3])
            put(c, yy, TOP - 8, 8, clh, slice(None), lanes, flags[0] & flags[3])
            put(c, yy, TOP + CX, 8, chh, slice(None), lanes, flags[1] & flags[3])

    def advance(src, dst, lo, hi):
        def layer(yy, carry):
            good = keep_layer(yy, HALO, HALO + CY, flags)
            for r in range(TOP - 8, TOP + CX + 8, 8):
                keep = keep_rows(r, flags) & good
                for c, v in enumerate(step_block(src, yy, r)):
                    dst[c, yy, pl.ds(r, 8), :] = jnp.where(keep, v, 0.0)
            return carry

        lax.fori_loop(lo, hi, layer, 0)

    advance(w0, w1, 1, WIDE - 1)
    advance(w1, w2, 2, WIDE - 2)

    def tables(yy, carry):
        for r in range(TOP, TOP + CX, 8):
            at = (yy * CX + (r - TOP)) * 8
            for c, v in enumerate(step_block(w2, yy + HALO, r)):
                tab_a[pl.ds(at + c, 8, stride=8), :] = v
                tab_a[pl.ds(at + 3 + c, 8, stride=8), :] = w2[c, yy + HALO, pl.ds(r, 8), :]
                tab_b[pl.ds(at + c, 8, stride=8), :] = w1[c, yy + HALO, pl.ds(r, 8), :]
        return carry

    lax.fori_loop(0, CY, tables, 0)
    to_scalar.wait()

    lane8 = lax.broadcasted_iota(jnp.int32, (8, LANES), 1)

    def pick(g, carry):
        a = jnp.zeros((8, LANES), jnp.float32)
        b = jnp.zeros((8, LANES), jnp.float32)
        for j in range(LANES):
            code = index[g, j]
            at = pl.multiple_of((code >> 7) * 8, 8)
            turn = code & (LANES - 1)
            here = lane8 == j
            a = jnp.where(here, pltpu.roll(tab_a[pl.ds(at, 8), :], turn, 1), a)
            b = jnp.where(here, pltpu.roll(tab_b[pl.ds(at, 8), :], turn, 1), b)
        at = pl.multiple_of(g * 8, 8)
        acc_a[pl.ds(at, 8), :] = a
        acc_b[pl.ds(at, 8), :] = b
        return carry

    lax.fori_loop(0, 32, pick, 0)

    ones = same_list()
    diag = diagonal()
    beam = slots[0]
    values = []
    for n in range(STEPS):
        ref, base = ((acc_b, 0), (acc_a, 3), (acc_a, 0))[n]
        seen = sum(slots[1 + c] * ref[pl.ds(base + c, 32, stride=8), :] for c in range(3))
        r = jnp.where(beam >= 0.0, seen - regroup(g0, 1 + n), 0.0)
        resid[n] = r
        for b in range(BEAMS):
            values.append(jnp.where(beam == float(b), r, 0.0))
    stacked = jnp.concatenate(values, axis=0)
    sums = jnp.dot(stacked, ones, precision=lax.Precision.HIGHEST, preferred_element_type=jnp.float32)
    part[...] = jnp.zeros_like(part)
    for i in range(STEPS * BEAMS):
        block = jnp.where(diag, sums[32 * i : 32 * i + 32, :], 0.0)
        part[pl.ds(i, 1), :] = jnp.sum(block, axis=0, keepdims=True)


def forward(state, halos, got):
    wide = f32(3, WIDE, ROWS, LANES)
    return pl.pallas_call(
        forward_kernel,
        out_shape=[
            wide, wide, wide, f32(STEPS, 32, LANES), f32(4, 32, LANES),
            jax.ShapeDtypeStruct((32, LANES), jnp.int32), f32(16, LANES),
        ],
        in_specs=[VMEM] * 10,
        out_specs=[VMEM] * 7,
        scratch_shapes=[
            pltpu.VMEM((CX * CY * 8, LANES), jnp.float32), pltpu.VMEM((CX * CY * 8, LANES), jnp.float32),
            pltpu.VMEM((256, LANES), jnp.float32), pltpu.VMEM((256, LANES), jnp.float32),
            pltpu.SMEM((32, LANES), jnp.int32), pltpu.SemaphoreType.DMA,
        ],
        compiler_params=pltpu.CompilerParams(vmem_limit_bytes=LIMIT),
        name="forward",
    )(state, *halos, got)


def sum_kernel(part, total, inbox_a, inbox_b, half, send_a, recv_a, send_b, recv_b):
    gx, gy = lax.axis_index("gx"), lax.axis_index("gy")
    q = (gx // 4) * 4 + lax.rem(gy, 4)
    p = lax.rem(gx, 4) * 4 + gy // 4

    def near(d):
        to = lax.rem(q + d, 8)
        return ((to // 4) * 4 + lax.rem(gx, 4), (gy // 4) * 4 + lax.rem(to, 4))

    def far(d):
        to = lax.rem(p + d, 16)
        return ((gx // 4) * 4 + to // 4, lax.rem(to, 4) * 4 + lax.rem(gy, 4))

    barrier = pltpu.get_barrier_semaphore()
    for d in range(1, 8):
        pl.semaphore_signal(barrier, inc=1, device_id=near(d), device_id_type=MESH)
    for d in range(1, 16):
        pl.semaphore_signal(barrier, inc=1, device_id=far(d), device_id_type=MESH)
    pl.semaphore_wait(barrier, 22)

    def spread(src, inbox, send, recv, where_to, peers):
        copies = []
        for d in range(1, peers):
            copy = pltpu.make_async_remote_copy(
                src_ref=src, dst_ref=inbox.at[d - 1], send_sem=send.at[d - 1], recv_sem=recv.at[d - 1],
                device_id=where_to(d), device_id_type=MESH,
            )
            copy.start()
            copies.append(copy)
        for copy in copies:
            copy.wait()

    spread(part, inbox_a, send_a, recv_a, near, 8)
    acc = part[...]
    for d in range(7):
        acc = acc + inbox_a[d]
    half[...] = acc
    spread(half, inbox_b, send_b, recv_b, far, 16)
    for d in range(15):
        acc = acc + inbox_b[d]
    total[...] = acc


def sum_all(part):
    return pl.pallas_call(
        sum_kernel,
        out_shape=f32(16, LANES),
        in_specs=[VMEM],
        out_specs=VMEM,
        scratch_shapes=[
            pltpu.VMEM((7, 16, LANES), jnp.float32), pltpu.VMEM((15, 16, LANES), jnp.float32),
            pltpu.VMEM((16, LANES), jnp.float32),
            pltpu.SemaphoreType.DMA((7,)), pltpu.SemaphoreType.DMA((7,)),
            pltpu.SemaphoreType.DMA((15,)), pltpu.SemaphoreType.DMA((15,)),
        ],
        compiler_params=pltpu.CompilerParams(collective_id=1, has_side_effects=True),
        name="sum_all",
    )(part)


def scatter_kernel(index, total, resid, slots, f3, f2, f1, xl, xh, vals_a, vals_b, *sums):
    ones = same_list()
    diag = diagonal()
    rows = [jnp.where(diag, total[pl.ds(i, 1), :], 0.0) for i in range(STEPS * BEAMS)]
    means = jnp.dot(
        jnp.concatenate(rows, axis=0), ones, precision=lax.Precision.HIGHEST, preferred_element_type=jnp.float32
    ) * (1.0 / GATES)
    beam = slots[0]
    vals_a[...] = jnp.zeros_like(vals_a)
    vals_b[...] = jnp.zeros_like(vals_b)
    for n in range(STEPS):
        at = 32 * BEAMS * n
        mean = jnp.zeros((32, LANES), jnp.float32)
        for b in range(BEAMS):
            mean = jnp.where(beam == float(b), means[at + 32 * b : at + 32 * b + 32, :], mean)
        misfit = jnp.where(beam >= 0.0, resid[n] - mean, 0.0)
        ref, base = ((vals_b, 0), (vals_a, 3), (vals_a, 0))[n]
        for c in range(3):
            ref[pl.ds(base + c, 32, stride=8), :] = slots[1 + c] * misfit

    blank = jnp.zeros((64, LANES), jnp.float32)

    def clear(i, carry):
        for ref in sums:
            ref[pl.ds(pl.multiple_of(i * 64, 64), 64), :] = blank
        return carry

    lax.fori_loop(0, CX * CY * 8 // 64, clear, 0)
    lane8 = lax.broadcasted_iota(jnp.int32, (8, LANES), 1)
    sum_a, sum_b = sums[:COPIES], sums[COPIES:]

    def place(g, carry):
        at = pl.multiple_of(g * 8, 8)
        va = vals_a[pl.ds(at, 8), :]
        vb = vals_b[pl.ds(at, 8), :]
        for j in range(LANES):
            code = index[g, j]
            to = pl.ds(pl.multiple_of((code >> 7) * 8, 8), 8)
            turn = (0 - code) & (LANES - 1)
            here = lane8 == ((j - code) & (LANES - 1))
            a, b = sum_a[j % COPIES], sum_b[j % COPIES]
            a[to, :] = a[to, :] + jnp.where(here, pltpu.roll(va, turn, 1), 0.0)
            b[to, :] = b[to, :] + jnp.where(here, pltpu.roll(vb, turn, 1), 0.0)
        return carry

    lax.fori_loop(0, 32, place, 0)

    def read(refs, start, stride):
        out = refs[0][pl.ds(start, 8, stride=stride), :]
        for ref in refs[1:]:
            out = out + ref[pl.ds(start, 8, stride=stride), :]
        return out

    plan = ((f3, sum_a, 0, 3, 0), (f2, sum_a, 3, 2, 3), (f1, sum_b, 0, 1, 5))

    def unpack(yy, carry):
        for r in range(0, CX, 8):
            for out, refs, base, depth, first in plan:
                for c in range(3):
                    out[c, yy, pl.ds(r, 8), :] = read(refs, (yy * CX + r) * 8 + base + c, 8)
        return carry

    lax.fori_loop(0, CY, unpack, 0)

    for out, refs, base, depth, first in plan:
        for c in range(3):
            for i in range(depth):
                for yy in range(0, CY, 8):
                    xl[c, first + i, pl.ds(yy, 8), :] = read(refs, (yy * CX + i) * 8 + base + c, CX * 8)
                    x = CX - depth + i
                    xh[c, first + i, pl.ds(yy, 8), :] = read(refs, (yy * CX + x) * 8 + base + c, CX * 8)


def scatter(index, total, resid, slots):
    table = pltpu.VMEM((CX * CY * 8, LANES), jnp.float32)
    field = f32(3, CY, CX, LANES)
    edge = f32(3, 6, CY, LANES)
    return pl.pallas_call(
        scatter_kernel,
        out_shape=[field, field, field, edge, edge],
        in_specs=[SMEM, VMEM, VMEM, VMEM],
        out_specs=[VMEM] * 5,
        scratch_shapes=[pltpu.VMEM((256, LANES), jnp.float32)] * 2 + [table] * (2 * COPIES),
        compiler_params=pltpu.CompilerParams(vmem_limit_bytes=LIMIT),
        name="scatter",
    )(index, total, resid, slots)


def rim_kernel(f3, f2, f1, xl, xh, ylo, yhi, xlo, xhi, cll, clh, chl, chh, send, recv):
    n_gx, n_gy = lax.axis_size("gx"), lax.axis_size("gy")
    gx, gy = lax.axis_index("gx"), lax.axis_index("gy")

    def to(dx, dy):
        return (lax.rem(gx + dx + n_gx, n_gx), lax.rem(gy + dy + n_gy, n_gy))

    barrier = pltpu.get_barrier_semaphore()
    for dx in (-1, 0, 1):
        for dy in (-1, 0, 1):
            if dx or dy:
                pl.semaphore_signal(barrier, inc=1, device_id=to(dx, dy), device_id_type=MESH)
    pl.semaphore_wait(barrier, 8)
    high, low = pl.ds(CY - 8, 8), pl.ds(0, 8)
    moves = []
    for f, depth, first in ((f3, 3, 0), (f2, 2, 3), (f1, 1, 5)):
        part = pl.ds(first, depth)
        moves += [
            (xh.at[:, part], xlo.at[:, part], 1, 0),
            (xl.at[:, part], xhi.at[:, part], -1, 0),
            (f.at[:, pl.ds(CY - depth, depth)], ylo.at[:, part], 0, 1),
            (f.at[:, pl.ds(0, depth)], yhi.at[:, part], 0, -1),
            (xh.at[:, part, high], cll.at[:, part], 1, 1),
            (xh.at[:, part, low], clh.at[:, part], 1, -1),
            (xl.at[:, part, high], chl.at[:, part], -1, 1),
            (xl.at[:, part, low], chh.at[:, part], -1, -1),
        ]
    copies = []
    for i, (src, dst, dx, dy) in enumerate(moves):
        copy = pltpu.make_async_remote_copy(
            src_ref=src, dst_ref=dst, send_sem=send.at[i], recv_sem=recv.at[i],
            device_id=to(dx, dy), device_id_type=MESH,
        )
        copy.start()
        copies.append(copy)
    for copy in copies:
        copy.wait()


def rims(fields, xl, xh):
    side, corner = f32(3, 6, CY, LANES), f32(3, 6, 8, LANES)
    return pl.pallas_call(
        rim_kernel,
        out_shape=[side] * 4 + [corner] * 4,
        in_specs=[VMEM] * 5,
        out_specs=[VMEM] * 8,
        scratch_shapes=[pltpu.SemaphoreType.DMA((24,)), pltpu.SemaphoreType.DMA((24,))],
        compiler_params=pltpu.CompilerParams(collective_id=2, has_side_effects=True, vmem_limit_bytes=LIMIT),
        name="rims",
    )(*fields, xl, xh)


def adjoint_kernel(w0, w1, w2, f3, f2, f1, ylo, yhi, xlo, xhi, cll, clh, chl, chh, out, a3, a2, a1):
    flags = inside_flags()
    blank = jnp.zeros((ROWS, LANES), jnp.float32)

    def clear(i, carry):
        for c in range(3):
            a3[c, i] = blank
            a2[c, i] = blank
            a1[c, i] = blank
        return carry

    lax.fori_loop(0, WIDE, clear, 0)

    def fill(dst, f, depth, first):
        def layer(yy, carry):
            for c in range(3):
                dst[c, yy + HALO, pl.ds(TOP, CX), :] = f[c, yy]
            return carry

        lax.fori_loop(0, CY, layer, 0)
        for c in range(3):
            for i in range(depth):
                k = first + i
                dst[c, HALO - depth + i, pl.ds(TOP, CX), :] = jnp.where(flags[2], ylo[c, k], 0.0)
                dst[c, HALO + CY + i, pl.ds(TOP, CX), :] = jnp.where(flags[3], yhi[c, k], 0.0)
        flat = dst.reshape(3, WIDE * ROWS, LANES)
        for c in range(3):
            for i in range(depth):
                k = first + i
                for ref, cl, ch, flag, x in (
                    (xlo, cll, clh, flags[0], TOP - depth + i),
                    (xhi, chl, chh, flags[1], TOP + CX + i),
                ):
                    for yy in range(0, CY, 8):
                        flat[c, pl.ds((yy + HALO) * ROWS + x, 8, stride=ROWS), :] = jnp.where(
                            flag, ref[c, k, pl.ds(yy, 8), :], 0.0
                        )
                    for j in range(depth):
                        dst[c, HALO - depth + j, pl.ds(x, 1), :] = jnp.where(
                            flag & flags[2], cl[c, k, pl.ds(8 - depth + j, 1), :], 0.0
                        )
                        dst[c, HALO + CY + j, pl.ds(x, 1), :] = jnp.where(
                            flag & flags[3], ch[c, k, pl.ds(j, 1), :], 0.0
                        )

    fill(a3, f3, 3, 0)
    fill(a2, f2, 2, 3)
    fill(a1, f1, 1, 5)

    def pull(src, adj, dst, reach):
        def layer(yy, carry):
            good = keep_layer(yy, HALO, HALO + CY, flags)
            for r in range(TOP - 8, TOP + CX + 8, 8):
                keep = keep_rows(r, flags) & good
                for c, v in enumerate(pull_block(src, yy, adj, yy, r)):
                    at = dst[c, yy, pl.ds(r, 8), :]
                    dst[c, yy, pl.ds(r, 8), :] = at + jnp.where(keep, v, 0.0)
            return carry

        lax.fori_loop(HALO - reach, HALO + CY + reach, layer, 0)

    pull(w2, a3, a2, 2)
    pull(w1, a2, a1, 1)
    for yy in range(CY):
        for r in range(0, CX, 8):
            for c, v in enumerate(pull_block(w0, yy + HALO, a1, yy + HALO, r + TOP)):
                out[c, pl.ds(r, 8), pl.ds(yy * NZ, NZ)] = v[:, :NZ]


def adjoint(wides, fields, edges):
    wide = pltpu.VMEM((3, WIDE, ROWS, LANES), jnp.float32)
    return pl.pallas_call(
        adjoint_kernel,
        out_shape=f32(3, CX, CY * NZ),
        in_specs=[VMEM] * 14,
        out_specs=VMEM,
        scratch_shapes=[wide] * 3,
        compiler_params=pltpu.CompilerParams(vmem_limit_bytes=LIMIT),
        name="adjoint",
    )(*wides, *fields, *edges)


def local(initial_state, beam_dir, gate_obs, slot_beam, slot_cell):
    beam = slot_beam[0]
    direction = jnp.zeros((3,) + beam.shape, jnp.float32)
    for b in range(BEAMS):
        direction = jnp.where((beam == b)[None], beam_dir[:, b][:, None, None], direction)
    msg = jnp.concatenate(
        [slot_cell[0].astype(jnp.float32), gate_obs[0, 0], gate_obs[1, 0], gate_obs[2, 0],
         beam.astype(jnp.float32), direction[0], direction[1], direction[2]], axis=1,
    ).reshape(-1, 2, LANES)
    *halos, got = swap(initial_state, msg)
    w0, w1, w2, resid, slots, index, part = forward(initial_state, halos, got)
    total = sum_all(part)
    f3, f2, f1, xl, xh = scatter(index, total, resid, slots)
    edges = rims((f3, f2, f1), xl, xh)
    return adjoint((w0, w1, w2), (f3, f2, f1), edges)


def solution(mesh):
    in_specs = (
        P(None, "gx", "gy"),
        P(None, ("gx", "gy")),
        P(None, ("gx", "gy"), None, None),
        P(("gx", "gy"), None, None),
        P(("gx", "gy"), None, None),
    )
    out_specs = P(None, "gx", "gy")
    return jax.shard_map(local, mesh=mesh, in_specs=in_specs, out_specs=out_specs, check_vma=False)
```

```python
import jax
import jax.numpy as jnp
from jax import lax
from jax.experimental import pallas as pl
from jax.experimental.pallas import tpu as pltpu
from jax.sharding import PartitionSpec as P

NZ = 96
LANES = 128
GATES = 512
BEAMS = 4
STEPS = 3
TIME_STEP = 0.2
VISCOSITY = 0.5
HALF = 0.5 * TIME_STEP
CX = 32
CY = 32
TOP = 8
ROWS = CX + 2 * TOP
WIDE = CY + 2
COPIES = 2
MIB = 1024 * 1024
MESH = pl.DeviceIdType.MESH
VMEM = pl.BlockSpec(memory_space=pltpu.VMEM)
SMEM = pl.BlockSpec(memory_space=pltpu.SMEM)
INNER = (TOP + 8, TOP + 16)
OUTER = (TOP, TOP + 24)


def f32(*shape):
    return jax.ShapeDtypeStruct(shape, jnp.float32)


def sizes():
    return lax.axis_size("gx"), lax.axis_size("gy"), lax.axis_index("gx"), lax.axis_index("gy")


def shift_up(v):
    return pltpu.roll(v, LANES - 1, 1)


def shift_down(v):
    return pltpu.roll(v, 1, 1)


def levels():
    return lax.broadcasted_iota(jnp.int32, (8, LANES), 1) < NZ


def step_block(src, y, r):
    rows, fore, back = pl.ds(r, 8), pl.ds(r + 1, 8), pl.ds(r - 1, 8)
    centre = [src[c, y, rows, :] for c in range(3)]
    less = [1.0 - v for v in centre]
    more = [1.0 + v for v in centre]
    out = []
    for c in range(3):
        v = centre[c]
        total = src[c, y, fore, :] * less[0] + src[c, y, back, :] * more[0]
        total += src[c, y + 1, rows, :] * less[1] + src[c, y - 1, rows, :] * more[1]
        total += shift_up(v) * less[2] + shift_down(v) * more[2]
        out.append((1.0 - 6.0 * HALF) * v + HALF * total)
    return out


def pull_block(src, adj, y, r):
    rows, fore, back = pl.ds(r, 8), pl.ds(r + 1, 8), pl.ds(r - 1, 8)
    near = []
    for c in range(3):
        v = src[c, y, rows, :]
        near.append((src[c, y, fore, :], src[c, y, back, :], src[c, y + 1, rows, :], src[c, y - 1, rows, :],
                     shift_up(v), shift_down(v)))
    factors = [1.0 + near[0][0], 1.0 - near[0][1], 1.0 + near[1][2], 1.0 - near[1][3],
               1.0 + near[2][4], 1.0 - near[2][5]]
    a = [adj[c, y, rows, :] for c in range(3)]
    out = []
    for c in range(3):
        total = adj[c, y, fore, :] * factors[0] + adj[c, y, back, :] * factors[1]
        total += adj[c, y + 1, rows, :] * factors[2] + adj[c, y - 1, rows, :] * factors[3]
        total += shift_up(a[c]) * factors[4] + shift_down(a[c]) * factors[5]
        for k in range(3):
            total -= a[k] * (near[k][2 * c] - near[k][2 * c + 1])
        out.append((1.0 - 6.0 * HALF) * a[c] + HALF * total)
    return out


def pack_rims(field, sides):
    flat = field.reshape(3, WIDE * ROWS, LANES)
    for c in range(3):
        for y in range(0, CY, 8):
            at = pl.ds(y, 8)
            sides[0, c, at, :] = flat[c, pl.ds((y + 1) * ROWS + TOP, 8, stride=ROWS), :]
            sides[1, c, at, :] = flat[c, pl.ds((y + 1) * ROWS + TOP + CX - 1, 8, stride=ROWS), :]
            sides[2, c, at, :] = field[c, 1, pl.ds(TOP + y, 8), :]
            sides[3, c, at, :] = field[c, CY, pl.ds(TOP + y, 8), :]


def unpack_rims(field, sides, n_gx, n_gy, gx, gy):
    flat = field.reshape(3, WIDE * ROWS, LANES)
    inside = (gx < n_gx - 1, gx > 0, gy < n_gy - 1, gy > 0)
    for c in range(3):
        for y in range(0, CY, 8):
            v = [jnp.where(inside[s], sides[s, c, pl.ds(y, 8), :], 0.0) for s in range(4)]
            flat[c, pl.ds((y + 1) * ROWS + TOP + CX, 8, stride=ROWS), :] = v[0]
            flat[c, pl.ds((y + 1) * ROWS + TOP - 1, 8, stride=ROWS), :] = v[1]
            field[c, CY + 1, pl.ds(TOP + y, 8), :] = v[2]
            field[c, 0, pl.ds(TOP + y, 8), :] = v[3]


def send_rims(sides, inbox, send, recv, n_gx, n_gy, gx, gy):
    targets = (
        (lax.rem(gx + n_gx - 1, n_gx), gy), (lax.rem(gx + 1, n_gx), gy),
        (gx, lax.rem(gy + n_gy - 1, n_gy)), (gx, lax.rem(gy + 1, n_gy)),
    )
    copies = []
    for s, target in enumerate(targets):
        copy = pltpu.make_async_remote_copy(
            src_ref=sides.at[s], dst_ref=inbox.at[s], send_sem=send.at[s], recv_sem=recv.at[s],
            device_id=target, device_id_type=MESH,
        )
        copy.start()
        copies.append(copy)
    return copies


def over_tile(body, inner):
    if inner:
        def layer(y, carry):
            for r in INNER:
                body(y, r)
            return carry

        lax.fori_loop(2, CY, layer, 0)
        return

    def layer(y, carry):
        for r in OUTER:
            body(y, r)
        return carry

    lax.fori_loop(1, CY + 1, layer, 0)
    for y in (1, CY):
        for r in INNER:
            body(y, r)


def regroup(block, quantity):
    lane = lax.broadcasted_iota(jnp.int32, (32, LANES), 1)
    out = None
    for k in range(4):
        piece = block[32 * k : 32 * k + 32, :]
        turn = (32 * (k - quantity)) % LANES
        if turn:
            piece = pltpu.roll(piece, turn, 1)
        out = piece if out is None else jnp.where(lane >= 32 * k, piece, out)
    return out


def forward_kernel(
    state, cell, obs, beam, beam_dir,
    w0, w1, w2, tab_a, tab_b, packed, slots, seen_obs,
    got, msg, sides, inbox, send, recv, list_send, list_recv, own,
):
    n_gx, n_gy, gx, gy = sizes()
    count = n_gx * n_gy
    me = gx * n_gy + gy
    barrier = pltpu.get_barrier_semaphore()

    def device(i):
        peer = lax.rem(me + i, count)
        return peer, (peer // n_gy, lax.rem(peer, n_gy))

    def hail(i, carry):
        pl.semaphore_signal(barrier, inc=1, device_id=device(i)[1], device_id_type=MESH)
        return carry

    lax.fori_loop(1, count, hail, 0)
    kind = beam[...]
    heads = [cell[...].astype(jnp.float32), obs[0], obs[1], obs[2]]
    tails = [kind.astype(jnp.float32)]
    for c in range(3):
        weight = jnp.zeros(kind.shape, jnp.float32)
        for b in range(BEAMS):
            weight = jnp.where(kind == b, beam_dir[c, b], weight)
        tails.append(weight)
    msg[:, 0, :] = jnp.concatenate(heads, axis=0).T
    msg[:, 1, :] = jnp.concatenate(tails, axis=0).T

    lane = lax.broadcasted_iota(jnp.int32, (CX, LANES), 1)
    for c in range(3):
        for y in range(0, CY, 4):
            t = [state[c, :, pl.ds(y * NZ + LANES * i, LANES)] for i in range(3)]
            planes = [
                t[0],
                pltpu.roll(jnp.where(lane >= 96, t[0], t[1]), 32, 1),
                pltpu.roll(jnp.where(lane >= 64, t[1], t[2]), 64, 1),
                pltpu.roll(t[2], 96, 1),
            ]
            for i, v in enumerate(planes):
                w0[c, y + 1 + i, pl.ds(TOP, CX), :] = jnp.where(lane < NZ, v, 0.0)
    pack_rims(w0, sides.at[0])
    pl.semaphore_wait(barrier, count - 1)

    where = (n_gx, n_gy, gx, gy)
    copies = send_rims(sides.at[0], inbox.at[0], send.at[0], recv.at[0], *where)

    def post(i, carry):
        peer, target = device(i)
        pltpu.make_async_remote_copy(
            src_ref=msg.at[peer], dst_ref=got.at[me], send_sem=list_send, recv_sem=list_recv,
            device_id=target, device_id_type=MESH,
        ).start()
        return carry

    lax.fori_loop(1, count, post, 0)
    mine = pltpu.make_async_copy(msg.at[me], got.at[me], own)
    mine.start()

    keep = levels()

    def advance(src, dst):
        def body(y, r):
            for c, v in enumerate(step_block(src, y, r)):
                dst[c, y, pl.ds(r, 8), :] = jnp.where(keep, v, 0.0)
        return body

    def tables(y, r):
        at = ((y - 1) * CX + (r - TOP)) * 8
        for c, v in enumerate(step_block(w2, y, r)):
            tab_a[pl.ds(at + c, 8, stride=8), :] = v
            tab_a[pl.ds(at + 3 + c, 8, stride=8), :] = w2[c, y, pl.ds(r, 8), :]
            tab_b[pl.ds(at + c, 8, stride=8), :] = w1[c, y, pl.ds(r, 8), :]

    for n, (src, body) in enumerate(((w0, advance(w0, w1)), (w1, advance(w1, w2)), (w2, tables))):
        if n:
            pack_rims(src, sides.at[n])
            copies = send_rims(sides.at[n], inbox.at[n], send.at[n], recv.at[n], *where)
        over_tile(body, True)
        for copy in copies:
            copy.wait()
        unpack_rims(src, inbox.at[n], *where)
        over_tile(body, False)

    mine.wait()
    rest = pl.ds(0, count - 1)
    pltpu.make_async_remote_copy(
        src_ref=msg.at[rest], dst_ref=got.at[rest], send_sem=list_send, recv_sem=list_recv,
        device_id=device(1)[1], device_id_type=MESH,
    ).wait()
    g0, g1 = got[:, 0, :], got[:, 1, :]
    where_to = regroup(g0, 0).astype(jnp.int32)
    x = ((where_to >> 10) * 171) >> 9
    rem = where_to - x * (CY * NZ)
    y = ((rem >> 5) * 171) >> 9
    z = rem - y * NZ
    lane = lax.broadcasted_iota(jnp.int32, (32, LANES), 1)
    packed[...] = (y * CX + x) * LANES + ((lane - z) & (LANES - 1))
    for j in range(4):
        slots[j] = regroup(g1, j)
    for n in range(STEPS):
        seen_obs[n] = regroup(g0, 1 + n)


def forward(state, cell, obs, beam, beam_dir):
    count = cell.shape[1]
    wide, table = f32(3, WIDE, ROWS, LANES), f32(CX * CY * 8, LANES)
    rim = pltpu.VMEM((STEPS, 4, 3, 32, LANES), jnp.float32)
    return pl.pallas_call(
        forward_kernel,
        out_shape=[wide, wide, wide, table, table, jax.ShapeDtypeStruct((32, LANES), jnp.int32), f32(4, 32, LANES), f32(STEPS, 32, LANES)],
        in_specs=[VMEM] * 4 + [SMEM],
        out_specs=[VMEM] * 8,
        scratch_shapes=[
            pltpu.VMEM((count, 2, LANES), jnp.float32), pltpu.VMEM((count, 2, LANES), jnp.float32), rim, rim,
            pltpu.SemaphoreType.DMA((STEPS, 4)), pltpu.SemaphoreType.DMA((STEPS, 4)),
            pltpu.SemaphoreType.DMA, pltpu.SemaphoreType.DMA, pltpu.SemaphoreType.DMA,
        ],
        compiler_params=pltpu.CompilerParams(collective_id=0, has_side_effects=True, vmem_limit_bytes=24 * MIB),
        name="forward",
    )(state, cell, obs, beam, beam_dir)


def same_list():
    a = lax.broadcasted_iota(jnp.int32, (LANES, LANES), 0) >> 5
    b = lax.broadcasted_iota(jnp.int32, (LANES, LANES), 1) >> 5
    return (a == b).astype(jnp.float32)


def diagonal():
    g = lax.broadcasted_iota(jnp.int32, (32, LANES), 0)
    lane = lax.broadcasted_iota(jnp.int32, (32, LANES), 1)
    return (lane & 31) == g


def list_sums(values):
    return jnp.dot(
        jnp.concatenate(values, axis=0), same_list(), precision=lax.Precision.HIGHEST,
        preferred_element_type=jnp.float32,
    )


def gather_kernel(
    index, tab_a, tab_b, slots, seen_obs,
    resid, part,
    acc_a, acc_b,
):
    part[...] = jnp.zeros_like(part)

    lane8 = lax.broadcasted_iota(jnp.int32, (8, LANES), 1)

    def pick(g, carry):
        a = jnp.zeros((8, LANES), jnp.float32)
        b = jnp.zeros((8, LANES), jnp.float32)
        for j in range(LANES):
            code = index[g, j]
            at = pl.multiple_of((code >> 7) * 8, 8)
            turn = code & (LANES - 1)
            here = lane8 == j
            a = jnp.where(here, pltpu.roll(tab_a[pl.ds(at, 8), :], turn, 1), a)
            b = jnp.where(here, pltpu.roll(tab_b[pl.ds(at, 8), :], turn, 1), b)
        at = pl.multiple_of(g * 8, 8)
        acc_a[pl.ds(at, 8), :] = a
        acc_b[pl.ds(at, 8), :] = b
        return carry

    lax.fori_loop(0, 32, pick, 0)

    diag = diagonal()
    beam = slots[0]
    values = []
    for n in range(STEPS):
        ref, base = ((acc_b, 0), (acc_a, 3), (acc_a, 0))[n]
        seen = sum(slots[1 + c] * ref[pl.ds(base + c, 32, stride=8), :] for c in range(3))
        r = seen - seen_obs[n]
        resid[n] = r
        for b in range(BEAMS):
            values.append(jnp.where(beam == float(b), r, 0.0))
    sums = list_sums(values)
    for i in range(STEPS * BEAMS):
        block = jnp.where(diag, sums[32 * i : 32 * i + 32, :], 0.0)
        part[pl.ds(i, 1), :] = jnp.sum(block, axis=0, keepdims=True)

def gather(index, tab_a, tab_b, slots, seen_obs):
    rows = pltpu.VMEM((256, LANES), jnp.float32)
    return pl.pallas_call(
        gather_kernel,
        out_shape=[f32(STEPS, 32, LANES), f32(16, LANES)],
        in_specs=[SMEM] + [VMEM] * 4,
        out_specs=[VMEM] * 2,
        scratch_shapes=[rows, rows],
        compiler_params=pltpu.CompilerParams(vmem_limit_bytes=16 * MIB),
        name="gather",
    )(index, tab_a, tab_b, slots, seen_obs)


def misfit_kernel(
    part, resid, slots, vals_a, vals_b, half, inbox_a, inbox_b, send_a, recv_a, send_b, recv_b
):
    gx, gy = lax.axis_index("gx"), lax.axis_index("gy")
    q = (gx // 4) * 4 + lax.rem(gy, 4)
    p = lax.rem(gx, 4) * 4 + gy // 4

    def near(d):
        to = lax.rem(q + d, 8)
        return ((to // 4) * 4 + lax.rem(gx, 4), (gy // 4) * 4 + lax.rem(to, 4))

    def far(d):
        to = lax.rem(p + d, 16)
        return ((gx // 4) * 4 + to // 4, lax.rem(to, 4) * 4 + lax.rem(gy, 4))

    barrier = pltpu.get_barrier_semaphore()
    for d in range(1, 8):
        pl.semaphore_signal(barrier, inc=1, device_id=near(d), device_id_type=MESH)
    for d in range(1, 16):
        pl.semaphore_signal(barrier, inc=1, device_id=far(d), device_id_type=MESH)

    vals_a[...] = jnp.zeros_like(vals_a)
    vals_b[...] = jnp.zeros_like(vals_b)
    diag = diagonal()
    beam = slots[0]
    pl.semaphore_wait(barrier, 22)

    def spread(src, inbox, send, recv, where_to, peers):
        copies = []
        for d in range(1, peers):
            copy = pltpu.make_async_remote_copy(
                src_ref=src, dst_ref=inbox.at[d - 1], send_sem=send.at[d - 1], recv_sem=recv.at[d - 1],
                device_id=where_to(d), device_id_type=MESH,
            )
            copy.start()
            copies.append(copy)
        for copy in copies:
            copy.wait()

    spread(part, inbox_a, send_a, recv_a, near, 8)
    acc = part[...]
    for d in range(7):
        acc = acc + inbox_a[d]
    half[...] = acc
    spread(half, inbox_b, send_b, recv_b, far, 16)
    for d in range(15):
        acc = acc + inbox_b[d]

    total = acc * (1.0 / GATES)
    means = list_sums([jnp.where(diag, total[i : i + 1, :], 0.0) for i in range(STEPS * BEAMS)])
    for n in range(STEPS):
        at = 32 * BEAMS * n
        mean = jnp.zeros((32, LANES), jnp.float32)
        for b in range(BEAMS):
            mean = jnp.where(beam == float(b), means[at + 32 * b : at + 32 * b + 32, :], mean)
        misfit = jnp.where(beam >= 0.0, resid[n] - mean, 0.0)
        ref, base = ((vals_b, 0), (vals_a, 3), (vals_a, 0))[n]
        for c in range(3):
            ref[pl.ds(base + c, 32, stride=8), :] = slots[1 + c] * misfit


def misfits(part, resid, slots):
    return pl.pallas_call(
        misfit_kernel,
        out_shape=[f32(256, LANES), f32(256, LANES)],
        in_specs=[VMEM] * 3,
        out_specs=[VMEM] * 2,
        scratch_shapes=[
            pltpu.VMEM((16, LANES), jnp.float32),
            pltpu.VMEM((7, 16, LANES), jnp.float32), pltpu.VMEM((15, 16, LANES), jnp.float32),
            pltpu.SemaphoreType.DMA((7,)), pltpu.SemaphoreType.DMA((7,)),
            pltpu.SemaphoreType.DMA((15,)), pltpu.SemaphoreType.DMA((15,)),
        ],
        compiler_params=pltpu.CompilerParams(collective_id=1, has_side_effects=True, vmem_limit_bytes=16 * MIB),
        name="misfits",
    )(part, resid, slots)


def scatter_kernel(index, vals_a, vals_b, f3, f2, f1, *sums):
    blank = jnp.zeros((64, LANES), jnp.float32)

    def clear(i, carry):
        for ref in sums:
            ref[pl.ds(pl.multiple_of(i * 64, 64), 64), :] = blank
        return carry

    lax.fori_loop(0, CX * CY * 8 // 64, clear, 0)
    lane8 = lax.broadcasted_iota(jnp.int32, (8, LANES), 1)
    sum_a, sum_b = sums[:COPIES], sums[COPIES:]

    def place(g, carry):
        at = pl.multiple_of(g * 8, 8)
        va = vals_a[pl.ds(at, 8), :]
        vb = vals_b[pl.ds(at, 8), :]
        for j in range(LANES):
            code = index[g, j]
            to = pl.ds(pl.multiple_of((code >> 7) * 8, 8), 8)
            turn = (0 - code) & (LANES - 1)
            here = lane8 == ((j - code) & (LANES - 1))
            a, b = sum_a[j % COPIES], sum_b[j % COPIES]
            a[to, :] = a[to, :] + jnp.where(here, pltpu.roll(va, turn, 1), 0.0)
            b[to, :] = b[to, :] + jnp.where(here, pltpu.roll(vb, turn, 1), 0.0)
        return carry

    lax.fori_loop(0, 32, place, 0)

    def unpack(y, carry):
        for r in range(0, CX, 8):
            for out, refs, base in ((f3, sum_a, 0), (f2, sum_a, 3), (f1, sum_b, 0)):
                for c in range(3):
                    at = pl.ds((y * CX + r) * 8 + base + c, 8, stride=8)
                    out[c, y, pl.ds(r, 8), :] = sum(ref[at, :] for ref in refs)
        return carry

    lax.fori_loop(0, CY, unpack, 0)


def scatter(index, vals_a, vals_b):
    table = pltpu.VMEM((CX * CY * 8, LANES), jnp.float32)
    field = f32(3, CY, CX, LANES)
    return pl.pallas_call(
        scatter_kernel,
        out_shape=[field, field, field],
        in_specs=[SMEM, VMEM, VMEM],
        out_specs=[VMEM] * 3,
        scratch_shapes=[table] * (2 * COPIES),
        compiler_params=pltpu.CompilerParams(vmem_limit_bytes=32 * MIB),
        name="scatter",
    )(index, vals_a, vals_b)


def adjoint_kernel(w0, w1, w2, f3, f2, f1, out, a3, a2, a1, sides, inbox, send, recv):
    n_gx, n_gy, gx, gy = sizes()
    where = (n_gx, n_gy, gx, gy)
    barrier = pltpu.get_barrier_semaphore()
    for target in (
        (lax.rem(gx + n_gx - 1, n_gx), gy), (lax.rem(gx + 1, n_gx), gy),
        (gx, lax.rem(gy + n_gy - 1, n_gy)), (gx, lax.rem(gy + 1, n_gy)),
    ):
        pl.semaphore_signal(barrier, inc=1, device_id=target, device_id_type=MESH)

    def fill(y, carry):
        for c in range(3):
            a3[c, y + 1, pl.ds(TOP, CX), :] = f3[c, y]
        return carry

    lax.fori_loop(0, CY, fill, 0)
    keep = levels()

    def pull(src, adj, dst, force):
        def body(y, r):
            for c, v in enumerate(pull_block(src, adj, y, r)):
                v = jnp.where(keep, v, 0.0)
                if force is not None:
                    v = v + force[c, y - 1, pl.ds(r - TOP, 8), :]
                dst[c, y, pl.ds(r, 8), :] = v
        return body

    for n, (src, adj, dst, force) in enumerate(((w2, a3, a2, f2), (w1, a2, a1, f1), (w0, a1, a3, None))):
        body = pull(src, adj, dst, force)
        pack_rims(adj, sides.at[n])
        if n == 0:
            pl.semaphore_wait(barrier, 4)
        copies = send_rims(sides.at[n], inbox.at[n], send.at[n], recv.at[n], *where)
        over_tile(body, True)
        for copy in copies:
            copy.wait()
        unpack_rims(adj, inbox.at[n], *where)
        over_tile(body, False)

    lane = lax.broadcasted_iota(jnp.int32, (CX, LANES), 1)
    for c in range(3):
        for y in range(0, CY, 4):
            v = [a3[c, y + 1 + i, pl.ds(TOP, CX), :] for i in range(4)]
            v = [v[0], pltpu.roll(v[1], 96, 1), pltpu.roll(v[2], 64, 1), pltpu.roll(v[3], 32, 1)]
            t = [
                jnp.where(lane < 96, v[0], v[1]),
                jnp.where(lane < 64, v[1], v[2]),
                jnp.where(lane < 32, v[2], v[3]),
            ]
            for i in range(3):
                out[c, :, pl.ds(y * NZ + LANES * i, LANES)] = t[i]


def adjoint(wides, fields):
    wide = pltpu.VMEM((3, WIDE, ROWS, LANES), jnp.float32)
    rim = pltpu.VMEM((STEPS, 4, 3, 32, LANES), jnp.float32)
    return pl.pallas_call(
        adjoint_kernel,
        out_shape=f32(3, CX, CY * NZ),
        in_specs=[VMEM] * 6,
        out_specs=VMEM,
        scratch_shapes=[wide] * 3 + [
            rim, rim, pltpu.SemaphoreType.DMA((STEPS, 4)), pltpu.SemaphoreType.DMA((STEPS, 4)),
        ],
        compiler_params=pltpu.CompilerParams(collective_id=2, has_side_effects=True, vmem_limit_bytes=24 * MIB),
        name="adjoint",
    )(*wides, *fields)


def local(initial_state, beam_dir, gate_obs, slot_beam, slot_cell):
    w0, w1, w2, tab_a, tab_b, index, slots, seen_obs = forward(
        initial_state, slot_cell[0].T, jnp.transpose(gate_obs[:, 0], (0, 2, 1)), slot_beam[0].T, beam_dir
    )
    resid, part = gather(index, tab_a, tab_b, slots, seen_obs)
    vals_a, vals_b = misfits(part, resid, slots)
    fields = scatter(index, vals_a, vals_b)
    return adjoint((w0, w1, w2), fields)


def solution(mesh):
    in_specs = (
        P(None, "gx", "gy"),
        P(None, ("gx", "gy")),
        P(None, ("gx", "gy"), None, None),
        P(("gx", "gy"), None, None),
        P(("gx", "gy"), None, None),
    )
    out_specs = P(None, "gx", "gy")
    return jax.shard_map(local, mesh=mesh, in_specs=in_specs, out_specs=out_specs, check_vma=False)
```

```python
import jax
import jax.numpy as jnp
from jax import lax
from jax.experimental import pallas as pl
from jax.experimental.pallas import tpu as pltpu
from jax.sharding import PartitionSpec as P

NZ = 96
LANES = 128
GATES = 512
BEAMS = 4
STEPS = 3
TIME_STEP = 0.2
VISCOSITY = 0.5
HALF = 0.5 * TIME_STEP
CX = 32
CY = 32
TOP = 8
ROWS = CX + 2 * TOP
WIDE = CY + 2
COPIES = 2
TILE = 16
UNROLL = 4
MIB = 1024 * 1024
MESH = pl.DeviceIdType.MESH
VMEM = pl.BlockSpec(memory_space=pltpu.VMEM)
SMEM = pl.BlockSpec(memory_space=pltpu.SMEM)


def f32(*shape):
    return jax.ShapeDtypeStruct(shape, jnp.float32)


def sizes():
    return lax.axis_size("gx"), lax.axis_size("gy"), lax.axis_index("gx"), lax.axis_index("gy")


def shift_up(v):
    return pltpu.roll(v, LANES - 1, 1)


def shift_down(v):
    return pltpu.roll(v, 1, 1)


def levels():
    return lax.broadcasted_iota(jnp.int32, (8, LANES), 1) < NZ


def step_block(src, y, r):
    rows, fore, back = pl.ds(r, 8), pl.ds(r + 1, 8), pl.ds(r - 1, 8)
    centre = [src[c, y, rows, :] for c in range(3)]
    less = [1.0 - v for v in centre]
    more = [1.0 + v for v in centre]
    out = []
    for c in range(3):
        v = centre[c]
        total = src[c, y, fore, :] * less[0] + src[c, y, back, :] * more[0]
        total += src[c, y + 1, rows, :] * less[1] + src[c, y - 1, rows, :] * more[1]
        total += shift_up(v) * less[2] + shift_down(v) * more[2]
        out.append((1.0 - 6.0 * HALF) * v + HALF * total)
    return out


def pull_block(src, adj, y, r):
    rows, fore, back = pl.ds(r, 8), pl.ds(r + 1, 8), pl.ds(r - 1, 8)
    near = []
    for c in range(3):
        v = src[c, y, rows, :]
        near.append((src[c, y, fore, :], src[c, y, back, :], src[c, y + 1, rows, :], src[c, y - 1, rows, :],
                     shift_up(v), shift_down(v)))
    factors = [1.0 + near[0][0], 1.0 - near[0][1], 1.0 + near[1][2], 1.0 - near[1][3],
               1.0 + near[2][4], 1.0 - near[2][5]]
    a = [adj[c, y, rows, :] for c in range(3)]
    out = []
    for c in range(3):
        total = adj[c, y, fore, :] * factors[0] + adj[c, y, back, :] * factors[1]
        total += adj[c, y + 1, rows, :] * factors[2] + adj[c, y - 1, rows, :] * factors[3]
        total += shift_up(a[c]) * factors[4] + shift_down(a[c]) * factors[5]
        for k in range(3):
            total -= a[k] * (near[k][2 * c] - near[k][2 * c + 1])
        out.append((1.0 - 6.0 * HALF) * a[c] + HALF * total)
    return out


def send_rims(sides, inbox, send, recv, n_gx, n_gy, gx, gy):
    targets = (
        (lax.rem(gx + n_gx - 1, n_gx), gy), (lax.rem(gx + 1, n_gx), gy),
        (gx, lax.rem(gy + n_gy - 1, n_gy)), (gx, lax.rem(gy + 1, n_gy)),
    )
    copies = []
    for s, target in enumerate(targets):
        copy = pltpu.make_async_remote_copy(
            src_ref=sides.at[s], dst_ref=inbox.at[s], send_sem=send.at[s], recv_sem=recv.at[s],
            device_id=target, device_id_type=MESH,
        )
        copy.start()
        copies.append(copy)
    return copies


def over_tile(body):
    def layer(y, carry):
        for r in range(TOP, TOP + CX, 8):
            body(y, r)
        return carry

    lax.fori_loop(1, CY + 1, layer, 0, unroll=UNROLL)


def clear_rims(fields):
    blank = jnp.zeros((8, LANES), jnp.float32)

    def layer(y, carry):
        for field in fields:
            for c in range(3):
                field[c, y, pl.ds(0, 8), :] = blank
                field[c, y, pl.ds(TOP + CX, 8), :] = blank
        return carry

    lax.fori_loop(1, CY + 1, layer, 0)
    for field in fields:
        for c in range(3):
            for y in (0, CY + 1):
                for r in range(TOP, TOP + CX, 8):
                    field[c, y, pl.ds(r, 8), :] = blank


def layer_at(field, side, depth, c, y):
    if side < 2:
        row = TOP - depth if side == 0 else TOP + CX - 1 + depth
        return field.reshape(3, WIDE * ROWS, LANES), (c, pl.ds((y + 1) * ROWS + row, 8, stride=ROWS), slice(None))
    return field, (c, 1 - depth if side == 2 else CY + depth, pl.ds(TOP + y, 8), slice(None))


OPPOSITE = (1, 0, 3, 2)


def inside_grid(n_gx, n_gy, gx, gy):
    return (gx > 0, gx < n_gx - 1, gy > 0, gy < n_gy - 1)


def pack_rims(field, sides):
    for s in range(4):
        for c in range(3):
            for y in range(0, CY, 8):
                ref, at = layer_at(field, s, 0, c, y)
                sides[s, c, pl.ds(y, 8), :] = ref[at]


def regroup(block, quantity):
    lane = lax.broadcasted_iota(jnp.int32, (32, LANES), 1)
    out = None
    for k in range(4):
        piece = block[32 * k : 32 * k + 32, :]
        turn = (32 * (k - quantity)) % LANES
        if turn:
            piece = pltpu.roll(piece, turn, 1)
        out = piece if out is None else jnp.where(lane >= 32 * k, piece, out)
    return out


def forward_kernel(
    state, cell, obs, beam, beam_dir,
    w0, w1, w2, table, take, give, slots, seen_obs,
    got, msg, sides, inbox, send, recv, list_send, list_recv, own,
):
    n_gx, n_gy, gx, gy = sizes()
    count = n_gx * n_gy
    me = gx * n_gy + gy
    barrier = pltpu.get_barrier_semaphore()

    def device(i):
        peer = lax.rem(me + i, count)
        return peer, (peer // n_gy, lax.rem(peer, n_gy))

    def hail(i, carry):
        pl.semaphore_signal(barrier, inc=1, device_id=device(i)[1], device_id_type=MESH)
        return carry

    lax.fori_loop(1, count, hail, 0)
    kind = beam[...]
    heads = [cell[...].astype(jnp.float32), obs[0], obs[1], obs[2]]
    tails = [kind.astype(jnp.float32)]
    for c in range(3):
        weight = jnp.zeros(kind.shape, jnp.float32)
        for b in range(BEAMS):
            weight = jnp.where(kind == b, beam_dir[c, b], weight)
        tails.append(weight)
    msg[:, 0, :] = jnp.concatenate(heads, axis=0).T
    msg[:, 1, :] = jnp.concatenate(tails, axis=0).T

    lane = lax.broadcasted_iota(jnp.int32, (CX, LANES), 1)
    for c in range(3):
        for y in range(0, CY, 4):
            t = [state[c, :, pl.ds(y * NZ + LANES * i, LANES)] for i in range(3)]
            planes = [
                t[0],
                pltpu.roll(jnp.where(lane >= 96, t[0], t[1]), 32, 1),
                pltpu.roll(jnp.where(lane >= 64, t[1], t[2]), 64, 1),
                pltpu.roll(t[2], 96, 1),
            ]
            for i, v in enumerate(planes):
                w0[c, y + 1 + i, pl.ds(TOP, CX), :] = jnp.where(lane < NZ, v, 0.0)
    pack_rims(w0, sides.at[0])
    clear_rims((w0, w1, w2))
    pl.semaphore_wait(barrier, count - 1)

    where = (n_gx, n_gy, gx, gy)
    copies = send_rims(sides.at[0], inbox.at[0], send.at[0], recv.at[0], *where)

    def post(i, carry):
        peer, target = device(i)
        pltpu.make_async_remote_copy(
            src_ref=msg.at[peer], dst_ref=got.at[me], send_sem=list_send, recv_sem=list_recv,
            device_id=target, device_id_type=MESH,
        ).start()
        return carry

    lax.fori_loop(1, count, post, 0)
    mine = pltpu.make_async_copy(msg.at[me], got.at[me], own)
    mine.start()

    keep = levels()

    def advance(src, dst):
        def body(y, r):
            for c, v in enumerate(step_block(src, y, r)):
                dst[c, y, pl.ds(r, 8), :] = jnp.where(keep, v, 0.0)
        return body

    cells = table.reshape(CX * CY * TILE, LANES)

    def tables(y, r):
        at = ((y - 1) * CX + (r - TOP)) * TILE
        for c, v in enumerate(step_block(w2, y, r)):
            cells[pl.ds(at + c, 8, stride=TILE), :] = v
            cells[pl.ds(at + 3 + c, 8, stride=TILE), :] = w2[c, y, pl.ds(r, 8), :]
            cells[pl.ds(at + 8 + c, 8, stride=TILE), :] = w1[c, y, pl.ds(r, 8), :]

    def target(dst, s, c, y):
        if dst is not None:
            return layer_at(dst, s, 0, c, y)
        if s < 2:
            return cells, (pl.ds((y * CX + (CX - 1) * s) * TILE + c, 8, stride=CX * TILE), slice(None))
        return cells, (pl.ds(((CY - 1) * (s - 2) * CX + y) * TILE + c, 8, stride=TILE), slice(None))

    inside = inside_grid(*where)

    def meet_rims(src, dst, n):
        for s in range(4):
            for y in range(0, CY, 8):
                rows = pl.ds(y, 8)
                speed = sides[n, s, s // 2, rows, :]
                factor = HALF * (1.0 - speed) if s % 2 else HALF * (1.0 + speed)
                for c in range(3):
                    v = jnp.where(inside[s], inbox[n, OPPOSITE[s], c, rows, :], 0.0)
                    ref, at = layer_at(src, s, 1, c, y)
                    ref[at] = v
                    ref, at = target(dst, s, c, y)
                    ref[at] = ref[at] + factor * v

    for n, (src, dst, body) in enumerate(((w0, w1, advance(w0, w1)), (w1, w2, advance(w1, w2)), (w2, None, tables))):
        if n:
            pack_rims(src, sides.at[n])
            copies = send_rims(sides.at[n], inbox.at[n], send.at[n], recv.at[n], *where)
        over_tile(body)
        for copy in copies:
            copy.wait()
        meet_rims(src, dst, n)

    mine.wait()
    rest = pl.ds(0, count - 1)
    pltpu.make_async_remote_copy(
        src_ref=msg.at[rest], dst_ref=got.at[rest], send_sem=list_send, recv_sem=list_recv,
        device_id=device(1)[1], device_id_type=MESH,
    ).wait()
    g0, g1 = got[:, 0, :], got[:, 1, :]
    where_to = regroup(g0, 0).astype(jnp.int32)
    x = ((where_to >> 10) * 171) >> 9
    rem = where_to - x * (CY * NZ)
    y = ((rem >> 5) * 171) >> 9
    z = rem - y * NZ
    lane = lax.broadcasted_iota(jnp.int32, (32, LANES), 1)
    at = (y * CX + x) * (TILE * LANES)
    take[...] = at + ((lane - z) & (LANES - 1))
    give[...] = at + ((z - lane) & (LANES - 1))
    for j in range(4):
        slots[j] = regroup(g1, j)
    for n in range(STEPS):
        seen_obs[n] = regroup(g0, 1 + n)


def forward(state, cell, obs, beam, beam_dir):
    count = cell.shape[1]
    wide, table = f32(3, WIDE, ROWS, LANES), f32(CX * CY, TILE, LANES)
    codes = jax.ShapeDtypeStruct((32, LANES), jnp.int32)
    rim = pltpu.VMEM((STEPS, 4, 3, 32, LANES), jnp.float32)
    return pl.pallas_call(
        forward_kernel,
        out_shape=[wide, wide, wide, table, codes, codes, f32(4, 32, LANES), f32(STEPS, 32, LANES)],
        in_specs=[VMEM] * 4 + [SMEM],
        out_specs=[VMEM] * 8,
        scratch_shapes=[
            pltpu.VMEM((count, 2, LANES), jnp.float32), pltpu.VMEM((count, 2, LANES), jnp.float32), rim, rim,
            pltpu.SemaphoreType.DMA((STEPS, 4)), pltpu.SemaphoreType.DMA((STEPS, 4)),
            pltpu.SemaphoreType.DMA, pltpu.SemaphoreType.DMA, pltpu.SemaphoreType.DMA,
        ],
        compiler_params=pltpu.CompilerParams(collective_id=0, has_side_effects=True, vmem_limit_bytes=24 * MIB),
        name="forward",
    )(state, cell, obs, beam, beam_dir)


def same_list():
    a = lax.broadcasted_iota(jnp.int32, (LANES, LANES), 0) >> 5
    b = lax.broadcasted_iota(jnp.int32, (LANES, LANES), 1) >> 5
    return (a == b).astype(jnp.float32)


def diagonal():
    g = lax.broadcasted_iota(jnp.int32, (32, LANES), 0)
    lane = lax.broadcasted_iota(jnp.int32, (32, LANES), 1)
    return (lane & 31) == g


def list_sums(values):
    return jnp.dot(
        jnp.concatenate(values, axis=0), same_list(), precision=lax.Precision.HIGHEST,
        preferred_element_type=jnp.float32,
    )


def gather_kernel(
    take, table, slots, seen_obs,
    vals_a, vals_b,
    acc_a, acc_b, resid, part, half, inbox_a, inbox_b, send_a, recv_a, send_b, recv_b,
):
    gx, gy = lax.axis_index("gx"), lax.axis_index("gy")
    q = (gx // 4) * 4 + lax.rem(gy, 4)
    p = lax.rem(gx, 4) * 4 + gy // 4

    def near(d):
        to = lax.rem(q + d, 8)
        return ((to // 4) * 4 + lax.rem(gx, 4), (gy // 4) * 4 + lax.rem(to, 4))

    def far(d):
        to = lax.rem(p + d, 16)
        return ((gx // 4) * 4 + to // 4, lax.rem(to, 4) * 4 + lax.rem(gy, 4))

    barrier = pltpu.get_barrier_semaphore()
    for d in range(1, 8):
        pl.semaphore_signal(barrier, inc=1, device_id=near(d), device_id_type=MESH)
    for d in range(1, 16):
        pl.semaphore_signal(barrier, inc=1, device_id=far(d), device_id_type=MESH)

    vals_a[...] = jnp.zeros_like(vals_a)
    vals_b[...] = jnp.zeros_like(vals_b)
    part[...] = jnp.zeros_like(part)

    lane8 = lax.broadcasted_iota(jnp.int32, (8, LANES), 1)

    def pick(g, carry):
        a = jnp.zeros((8, LANES), jnp.float32)
        b = jnp.zeros((8, LANES), jnp.float32)
        for j in range(LANES):
            code = take[g, j]
            tile = pltpu.roll(table[code >> 11], code & (LANES - 1), 1)
            here = lane8 == j
            a = jnp.where(here, tile[:8], a)
            b = jnp.where(here, tile[8:], b)
        at = pl.multiple_of(g * 8, 8)
        acc_a[pl.ds(at, 8), :] = a
        acc_b[pl.ds(at, 8), :] = b
        return carry

    lax.fori_loop(0, 32, pick, 0)

    diag = diagonal()
    beam = slots[0]
    values = []
    for n in range(STEPS):
        ref, base = ((acc_b, 0), (acc_a, 3), (acc_a, 0))[n]
        seen = sum(slots[1 + c] * ref[pl.ds(base + c, 32, stride=8), :] for c in range(3))
        r = seen - seen_obs[n]
        resid[n] = r
        for b in range(BEAMS):
            values.append(jnp.where(beam == float(b), r, 0.0))
    sums = list_sums(values)
    for i in range(STEPS * BEAMS):
        block = jnp.where(diag, sums[32 * i : 32 * i + 32, :], 0.0)
        part[pl.ds(i, 1), :] = jnp.sum(block, axis=0, keepdims=True)
    pl.semaphore_wait(barrier, 22)

    def spread(src, inbox, send, recv, where_to, peers):
        copies = []
        for d in range(1, peers):
            copy = pltpu.make_async_remote_copy(
                src_ref=src, dst_ref=inbox.at[d - 1], send_sem=send.at[d - 1], recv_sem=recv.at[d - 1],
                device_id=where_to(d), device_id_type=MESH,
            )
            copy.start()
            copies.append(copy)
        for copy in copies:
            copy.wait()

    spread(part, inbox_a, send_a, recv_a, near, 8)
    acc = part[...]
    for d in range(7):
        acc = acc + inbox_a[d]
    half[...] = acc
    spread(half, inbox_b, send_b, recv_b, far, 16)
    for d in range(15):
        acc = acc + inbox_b[d]

    total = acc * (1.0 / GATES)
    means = list_sums([jnp.where(diag, total[i : i + 1, :], 0.0) for i in range(STEPS * BEAMS)])
    for n in range(STEPS):
        at = 32 * BEAMS * n
        mean = jnp.zeros((32, LANES), jnp.float32)
        for b in range(BEAMS):
            mean = jnp.where(beam == float(b), means[at + 32 * b : at + 32 * b + 32, :], mean)
        misfit = jnp.where(beam >= 0.0, resid[n] - mean, 0.0)
        ref, base = ((vals_b, 0), (vals_a, 3), (vals_a, 0))[n]
        for c in range(3):
            ref[pl.ds(base + c, 32, stride=8), :] = slots[1 + c] * misfit


def gather(take, table, slots, seen_obs):
    rows = pltpu.VMEM((256, LANES), jnp.float32)
    block = pltpu.VMEM((16, LANES), jnp.float32)
    return pl.pallas_call(
        gather_kernel,
        out_shape=[f32(256, LANES), f32(256, LANES)],
        in_specs=[SMEM] + [VMEM] * 3,
        out_specs=[VMEM] * 2,
        scratch_shapes=[
            rows, rows, pltpu.VMEM((STEPS, 32, LANES), jnp.float32), block, block,
            pltpu.VMEM((7, 16, LANES), jnp.float32), pltpu.VMEM((15, 16, LANES), jnp.float32),
            pltpu.SemaphoreType.DMA((7,)), pltpu.SemaphoreType.DMA((7,)),
            pltpu.SemaphoreType.DMA((15,)), pltpu.SemaphoreType.DMA((15,)),
        ],
        compiler_params=pltpu.CompilerParams(collective_id=1, has_side_effects=True, vmem_limit_bytes=16 * MIB),
        name="gather",
    )(take, table, slots, seen_obs)


def scatter_kernel(give, vals_a, vals_b, f3, f2, f1, *sums):
    blank = jnp.zeros((64, LANES), jnp.float32)

    def clear(i, carry):
        for ref in sums:
            ref[pl.ds(pl.multiple_of(i * 64, 64), 64), :] = blank
        return carry

    lax.fori_loop(0, CX * CY * TILE // 64, clear, 0)
    lane8 = lax.broadcasted_iota(jnp.int32, (8, LANES), 1)

    def place(g, carry):
        at = pl.multiple_of(g * 8, 8)
        va = vals_a[pl.ds(at, 8), :]
        vb = vals_b[pl.ds(at, 8), :]
        for j in range(LANES):
            code = give[g, j]
            at = pl.multiple_of(code >> 7, TILE)
            turn = code & (LANES - 1)
            here = lane8 == j
            out = sums[j % COPIES]
            a, b = pl.ds(at, 8), pl.ds(at + 8, 8)
            out[a, :] = out[a, :] + pltpu.roll(jnp.where(here, va, 0.0), turn, 1)
            out[b, :] = out[b, :] + pltpu.roll(jnp.where(here, vb, 0.0), turn, 1)
        return carry

    lax.fori_loop(0, 32, place, 0)

    def unpack(y, carry):
        for r in range(0, CX, 8):
            for out, base in ((f3, 0), (f2, 3), (f1, 8)):
                for c in range(3):
                    at = pl.ds((y * CX + r) * TILE + base + c, 8, stride=TILE)
                    out[c, y, pl.ds(r, 8), :] = sum(ref[at, :] for ref in sums)
        return carry

    lax.fori_loop(0, CY, unpack, 0)


def scatter(give, vals_a, vals_b):
    table = pltpu.VMEM((CX * CY * TILE, LANES), jnp.float32)
    field = f32(3, CY, CX, LANES)
    return pl.pallas_call(
        scatter_kernel,
        out_shape=[field, field, field],
        in_specs=[SMEM, VMEM, VMEM],
        out_specs=[VMEM] * 3,
        scratch_shapes=[table] * COPIES,
        compiler_params=pltpu.CompilerParams(vmem_limit_bytes=32 * MIB),
        name="scatter",
    )(give, vals_a, vals_b)


def adjoint_kernel(w0, w1, w2, f3, f2, f1, out, a3, a2, a1, sides, inbox, send, recv):
    n_gx, n_gy, gx, gy = sizes()
    where = (n_gx, n_gy, gx, gy)
    barrier = pltpu.get_barrier_semaphore()
    for target in (
        (lax.rem(gx + n_gx - 1, n_gx), gy), (lax.rem(gx + 1, n_gx), gy),
        (gx, lax.rem(gy + n_gy - 1, n_gy)), (gx, lax.rem(gy + 1, n_gy)),
    ):
        pl.semaphore_signal(barrier, inc=1, device_id=target, device_id_type=MESH)

    def fill(y, carry):
        for c in range(3):
            a3[c, y + 1, pl.ds(TOP, CX), :] = f3[c, y]
        return carry

    lax.fori_loop(0, CY, fill, 0)
    clear_rims((a3, a2, a1))
    keep = levels()
    inside = inside_grid(*where)

    def meet_rims(src, dst, n):
        for s in range(4):
            for y in range(0, CY, 8):
                ref, at = layer_at(src, s, 1, s // 2, y)
                factor = HALF * (1.0 + ref[at]) if s % 2 else HALF * (1.0 - ref[at])
                for c in range(3):
                    v = jnp.where(inside[s], inbox[n, OPPOSITE[s], c, pl.ds(y, 8), :], 0.0)
                    ref, at = layer_at(dst, s, 0, c, y)
                    ref[at] = ref[at] + factor * v

    def pull(src, adj, dst, force):
        def body(y, r):
            for c, v in enumerate(pull_block(src, adj, y, r)):
                v = jnp.where(keep, v, 0.0)
                if force is not None:
                    v = v + force[c, y - 1, pl.ds(r - TOP, 8), :]
                dst[c, y, pl.ds(r, 8), :] = v
        return body

    for n, (src, adj, dst, force) in enumerate(((w2, a3, a2, f2), (w1, a2, a1, f1), (w0, a1, a3, None))):
        body = pull(src, adj, dst, force)
        pack_rims(adj, sides.at[n])
        if n == 0:
            pl.semaphore_wait(barrier, 4)
        copies = send_rims(sides.at[n], inbox.at[n], send.at[n], recv.at[n], *where)
        over_tile(body)
        for copy in copies:
            copy.wait()
        meet_rims(src, dst, n)

    lane = lax.broadcasted_iota(jnp.int32, (CX, LANES), 1)
    for c in range(3):
        for y in range(0, CY, 4):
            v = [a3[c, y + 1 + i, pl.ds(TOP, CX), :] for i in range(4)]
            v = [v[0], pltpu.roll(v[1], 96, 1), pltpu.roll(v[2], 64, 1), pltpu.roll(v[3], 32, 1)]
            t = [
                jnp.where(lane < 96, v[0], v[1]),
                jnp.where(lane < 64, v[1], v[2]),
                jnp.where(lane < 32, v[2], v[3]),
            ]
            for i in range(3):
                out[c, :, pl.ds(y * NZ + LANES * i, LANES)] = t[i]


def adjoint(wides, fields):
    wide = pltpu.VMEM((3, WIDE, ROWS, LANES), jnp.float32)
    rim = pltpu.VMEM((STEPS, 4, 3, 32, LANES), jnp.float32)
    return pl.pallas_call(
        adjoint_kernel,
        out_shape=f32(3, CX, CY * NZ),
        in_specs=[VMEM] * 6,
        out_specs=VMEM,
        scratch_shapes=[wide] * 3 + [
            rim, rim, pltpu.SemaphoreType.DMA((STEPS, 4)), pltpu.SemaphoreType.DMA((STEPS, 4)),
        ],
        compiler_params=pltpu.CompilerParams(collective_id=2, has_side_effects=True, vmem_limit_bytes=24 * MIB),
        name="adjoint",
    )(*wides, *fields)


def local(initial_state, beam_dir, gate_obs, slot_beam, slot_cell):
    w0, w1, w2, table, take, give, slots, seen_obs = forward(
        initial_state, slot_cell[0].T, jnp.transpose(gate_obs[:, 0], (0, 2, 1)), slot_beam[0].T, beam_dir
    )
    vals_a, vals_b = gather(take, table, slots, seen_obs)
    fields = scatter(give, vals_a, vals_b)
    return adjoint((w0, w1, w2), fields)


def solution(mesh):
    in_specs = (
        P(None, "gx", "gy"),
        P(None, ("gx", "gy")),
        P(None, ("gx", "gy"), None, None),
        P(("gx", "gy"), None, None),
        P(("gx", "gy"), None, None),
    )
    out_specs = P(None, "gx", "gy")
    return jax.shard_map(local, mesh=mesh, in_specs=in_specs, out_specs=out_specs, check_vma=False)
```

```python
import jax
import jax.numpy as jnp
from jax import lax
from jax.experimental import pallas as pl
from jax.experimental.pallas import tpu as pltpu
from jax.sharding import PartitionSpec as P

NZ = 96
LANES = 128
GATES = 512
BEAMS = 4
STEPS = 3
TIME_STEP = 0.2
VISCOSITY = 0.5
HALF = 0.5 * TIME_STEP
CX = 32
CY = 32
TOP = 8
ROWS = CX + 2 * TOP
WIDE = CY + 2
COPIES = 3
TILE = 8
UNROLL = 4
MIB = 1024 * 1024
MESH = pl.DeviceIdType.MESH
VMEM = pl.BlockSpec(memory_space=pltpu.VMEM)
SMEM = pl.BlockSpec(memory_space=pltpu.SMEM)


def f32(*shape):
    return jax.ShapeDtypeStruct(shape, jnp.float32)


def sizes():
    return lax.axis_size("gx"), lax.axis_size("gy"), lax.axis_index("gx"), lax.axis_index("gy")


def shift_up(v):
    return pltpu.roll(v, LANES - 1, 1)


def shift_down(v):
    return pltpu.roll(v, 1, 1)


def levels():
    return lax.broadcasted_iota(jnp.int32, (8, LANES), 1) < NZ


def step_block(src, y, r):
    rows, fore, back = pl.ds(r, 8), pl.ds(r + 1, 8), pl.ds(r - 1, 8)
    centre = [src[c, y, rows, :] for c in range(3)]
    less = [1.0 - v for v in centre]
    more = [1.0 + v for v in centre]
    out = []
    for c in range(3):
        v = centre[c]
        total = src[c, y, fore, :] * less[0] + src[c, y, back, :] * more[0]
        total += src[c, y + 1, rows, :] * less[1] + src[c, y - 1, rows, :] * more[1]
        total += shift_up(v) * less[2] + shift_down(v) * more[2]
        out.append((1.0 - 6.0 * HALF) * v + HALF * total)
    return out


def pull_block(src, adj, y, r):
    rows, fore, back = pl.ds(r, 8), pl.ds(r + 1, 8), pl.ds(r - 1, 8)
    near = []
    for c in range(3):
        v = src[c, y, rows, :]
        near.append((src[c, y, fore, :], src[c, y, back, :], src[c, y + 1, rows, :], src[c, y - 1, rows, :],
                     shift_up(v), shift_down(v)))
    factors = [1.0 + near[0][0], 1.0 - near[0][1], 1.0 + near[1][2], 1.0 - near[1][3],
               1.0 + near[2][4], 1.0 - near[2][5]]
    a = [adj[c, y, rows, :] for c in range(3)]
    out = []
    for c in range(3):
        total = adj[c, y, fore, :] * factors[0] + adj[c, y, back, :] * factors[1]
        total += adj[c, y + 1, rows, :] * factors[2] + adj[c, y - 1, rows, :] * factors[3]
        total += shift_up(a[c]) * factors[4] + shift_down(a[c]) * factors[5]
        for k in range(3):
            total -= a[k] * (near[k][2 * c] - near[k][2 * c + 1])
        out.append((1.0 - 6.0 * HALF) * a[c] + HALF * total)
    return out


def send_rims(sides, inbox, send, recv, n_gx, n_gy, gx, gy):
    targets = (
        (lax.rem(gx + n_gx - 1, n_gx), gy), (lax.rem(gx + 1, n_gx), gy),
        (gx, lax.rem(gy + n_gy - 1, n_gy)), (gx, lax.rem(gy + 1, n_gy)),
    )
    copies = []
    for s, target in enumerate(targets):
        copy = pltpu.make_async_remote_copy(
            src_ref=sides.at[s], dst_ref=inbox.at[s], send_sem=send.at[s], recv_sem=recv.at[s],
            device_id=target, device_id_type=MESH,
        )
        copy.start()
        copies.append(copy)
    return copies


def over_tile(body):
    def layer(y, carry):
        for r in range(TOP, TOP + CX, 8):
            body(y, r)
        return carry

    lax.fori_loop(1, CY + 1, layer, 0, unroll=UNROLL)


def clear_rims(fields):
    blank = jnp.zeros((8, LANES), jnp.float32)

    def layer(y, carry):
        for field in fields:
            for c in range(3):
                field[c, y, pl.ds(0, 8), :] = blank
                field[c, y, pl.ds(TOP + CX, 8), :] = blank
        return carry

    lax.fori_loop(1, CY + 1, layer, 0)
    for field in fields:
        for c in range(3):
            for y in (0, CY + 1):
                for r in range(TOP, TOP + CX, 8):
                    field[c, y, pl.ds(r, 8), :] = blank


def layer_at(field, side, depth, c, y):
    if side < 2:
        row = TOP - depth if side == 0 else TOP + CX - 1 + depth
        return field.reshape(3, WIDE * ROWS, LANES), (c, pl.ds((y + 1) * ROWS + row, 8, stride=ROWS), slice(None))
    return field, (c, 1 - depth if side == 2 else CY + depth, pl.ds(TOP + y, 8), slice(None))


OPPOSITE = (1, 0, 3, 2)


def inside_grid(n_gx, n_gy, gx, gy):
    return (gx > 0, gx < n_gx - 1, gy > 0, gy < n_gy - 1)


def pack_rims(field, sides):
    for s in range(4):
        for c in range(3):
            for y in range(0, CY, 8):
                ref, at = layer_at(field, s, 0, c, y)
                sides[s, c, pl.ds(y, 8), :] = ref[at]


def regroup(block, quantity):
    lane = lax.broadcasted_iota(jnp.int32, (32, LANES), 1)
    out = None
    for k in range(4):
        piece = block[32 * k : 32 * k + 32, :]
        turn = (32 * (k - quantity)) % LANES
        if turn:
            piece = pltpu.roll(piece, turn, 1)
        out = piece if out is None else jnp.where(lane >= 32 * k, piece, out)
    return out


def forward_kernel(
    state, lists,
    w0, w1, w2, table, take, give, third, slots, seen_obs,
    got, msg, sides, inbox, send, recv, list_send, list_recv, own,
):
    n_gx, n_gy, gx, gy = sizes()
    count = n_gx * n_gy
    me = gx * n_gy + gy
    barrier = pltpu.get_barrier_semaphore()

    def device(i):
        peer = lax.rem(me + i, count)
        return peer, (peer // n_gy, lax.rem(peer, n_gy))

    def hail(i, carry):
        pl.semaphore_signal(barrier, inc=1, device_id=device(i)[1], device_id_type=MESH)
        return carry

    lax.fori_loop(1, count, hail, 0)
    kind = lists[pl.ds(LANES, 32), :]
    tails = [kind]
    beam_dir = lists[pl.ds(LANES + 32, 8), :]
    for c in range(3):
        weight = jnp.zeros(kind.shape, jnp.float32)
        for b in range(BEAMS):
            weight = jnp.where(kind == float(b), beam_dir[c : c + 1, b : b + 1], weight)
        tails.append(weight)
    msg[:, 0, :] = lists[pl.ds(0, LANES), :].T
    msg[:, 1, :] = jnp.concatenate(tails, axis=0).T

    lane = lax.broadcasted_iota(jnp.int32, (CX, LANES), 1)
    for c in range(3):
        for y in range(0, CY, 4):
            t = [state[c, :, pl.ds(y * NZ + LANES * i, LANES)] for i in range(3)]
            planes = [
                t[0],
                pltpu.roll(jnp.where(lane >= 96, t[0], t[1]), 32, 1),
                pltpu.roll(jnp.where(lane >= 64, t[1], t[2]), 64, 1),
                pltpu.roll(t[2], 96, 1),
            ]
            for i, v in enumerate(planes):
                w0[c, y + 1 + i, pl.ds(TOP, CX), :] = jnp.where(lane < NZ, v, 0.0)
    pack_rims(w0, sides.at[0])
    clear_rims((w0, w1, w2))
    pl.semaphore_wait(barrier, count - 1)

    where = (n_gx, n_gy, gx, gy)
    copies = send_rims(sides.at[0], inbox.at[0], send.at[0], recv.at[0], *where)

    def post(i, carry):
        peer, target = device(i)
        pltpu.make_async_remote_copy(
            src_ref=msg.at[peer], dst_ref=got.at[me], send_sem=list_send, recv_sem=list_recv,
            device_id=target, device_id_type=MESH,
        ).start()
        return carry

    lax.fori_loop(1, count, post, 0)
    mine = pltpu.make_async_copy(msg.at[me], got.at[me], own)
    mine.start()

    keep = levels()

    def advance(src, dst):
        def body(y, r):
            for c, v in enumerate(step_block(src, y, r)):
                dst[c, y, pl.ds(r, 8), :] = jnp.where(keep, v, 0.0)
        return body

    cells = table.reshape(CX * CY * TILE, LANES)

    def tables(y, r):
        at = ((y - 1) * CX + (r - TOP)) * TILE
        spare = w1[2, y, pl.ds(r, 8), :]
        for c, v in enumerate(step_block(w2, y, r)):
            cells[pl.ds(at + c, 8, stride=TILE), :] = jnp.where(keep, v, pltpu.roll(spare, NZ - 32 * c, 1))
            cells[pl.ds(at + 3 + c, 8, stride=TILE), :] = w2[c, y, pl.ds(r, 8), :]
            if c < 2:
                cells[pl.ds(at + 6 + c, 8, stride=TILE), :] = w1[c, y, pl.ds(r, 8), :]

    def target(dst, s, c, y):
        if dst is not None:
            return layer_at(dst, s, 0, c, y)
        if s < 2:
            return cells, (pl.ds((y * CX + (CX - 1) * s) * TILE + c, 8, stride=CX * TILE), slice(None))
        return cells, (pl.ds(((CY - 1) * (s - 2) * CX + y) * TILE + c, 8, stride=TILE), slice(None))

    inside = inside_grid(*where)

    def meet_rims(src, dst, n):
        for s in range(4):
            for y in range(0, CY, 8):
                rows = pl.ds(y, 8)
                speed = sides[n, s, s // 2, rows, :]
                factor = HALF * (1.0 - speed) if s % 2 else HALF * (1.0 + speed)
                for c in range(3):
                    v = jnp.where(inside[s], inbox[n, OPPOSITE[s], c, rows, :], 0.0)
                    ref, at = layer_at(src, s, 1, c, y)
                    ref[at] = v
                    ref, at = target(dst, s, c, y)
                    ref[at] = ref[at] + factor * v

    for n, (src, dst, body) in enumerate(((w0, w1, advance(w0, w1)), (w1, w2, advance(w1, w2)), (w2, None, tables))):
        if n:
            pack_rims(src, sides.at[n])
            copies = send_rims(sides.at[n], inbox.at[n], send.at[n], recv.at[n], *where)
        over_tile(body)
        for copy in copies:
            copy.wait()
        meet_rims(src, dst, n)

    mine.wait()
    rest = pl.ds(0, count - 1)
    pltpu.make_async_remote_copy(
        src_ref=msg.at[rest], dst_ref=got.at[rest], send_sem=list_send, recv_sem=list_recv,
        device_id=device(1)[1], device_id_type=MESH,
    ).wait()
    g0, g1 = got[:, 0, :], got[:, 1, :]
    where_to = regroup(g0, 0).astype(jnp.int32)
    x = ((where_to >> 10) * 171) >> 9
    rem = where_to - x * (CY * NZ)
    y = ((rem >> 5) * 171) >> 9
    z = rem - y * NZ
    lane = lax.broadcasted_iota(jnp.int32, (32, LANES), 1)
    at = (y * CX + x) * LANES
    take[...] = at + ((lane - z) & (LANES - 1))
    give[...] = at * TILE + ((z - lane) & (LANES - 1))
    third[...] = (z >> 5).astype(jnp.float32)
    for j in range(4):
        slots[j] = regroup(g1, j)
    for n in range(STEPS):
        seen_obs[n] = regroup(g0, 1 + n)


def forward(state, lists):
    count = lists.shape[1]
    wide, table = f32(3, WIDE, ROWS, LANES), f32(CX * CY, TILE, LANES)
    codes = jax.ShapeDtypeStruct((32, LANES), jnp.int32)
    rim = pltpu.VMEM((STEPS, 4, 3, 32, LANES), jnp.float32)
    return pl.pallas_call(
        forward_kernel,
        out_shape=[
            wide, wide, wide, table, codes, codes, f32(32, LANES), f32(4, 32, LANES), f32(STEPS, 32, LANES),
        ],
        in_specs=[VMEM] * 2,
        out_specs=[VMEM] * 9,
        scratch_shapes=[
            pltpu.VMEM((count, 2, LANES), jnp.float32), pltpu.VMEM((count, 2, LANES), jnp.float32), rim, rim,
            pltpu.SemaphoreType.DMA((STEPS, 4)), pltpu.SemaphoreType.DMA((STEPS, 4)),
            pltpu.SemaphoreType.DMA, pltpu.SemaphoreType.DMA, pltpu.SemaphoreType.DMA,
        ],
        compiler_params=pltpu.CompilerParams(collective_id=0, has_side_effects=True, vmem_limit_bytes=24 * MIB),
        name="forward",
    )(state, lists)


def spare_lanes():
    lane = lax.broadcasted_iota(jnp.int32, (8, LANES), 1)
    row = lax.broadcasted_iota(jnp.int32, (8, LANES), 0)
    return jnp.where(row < 3, (lane + 32 * (row + 1)) & (LANES - 1), -1)


def same_list():
    a = lax.broadcasted_iota(jnp.int32, (LANES, LANES), 0) >> 5
    b = lax.broadcasted_iota(jnp.int32, (LANES, LANES), 1) >> 5
    return (a == b).astype(jnp.float32)


def diagonal():
    g = lax.broadcasted_iota(jnp.int32, (32, LANES), 0)
    lane = lax.broadcasted_iota(jnp.int32, (32, LANES), 1)
    return (lane & 31) == g


def list_sums(values):
    return jnp.dot(
        jnp.concatenate(values, axis=0), same_list(), precision=lax.Precision.HIGHEST,
        preferred_element_type=jnp.float32,
    )


def gather_kernel(
    take, table, third, slots, seen_obs,
    vals_a, vals_b, *rest,
):
    empty = rest[:COPIES]
    gather_body(take, table, third, slots, seen_obs, vals_a, vals_b, empty, *rest[COPIES:])


def gather_body(
    take, table, third, slots, seen_obs, vals_a, vals_b, empty,
    acc_a, acc_b, resid, part, half, inbox_a, inbox_b, send_a, recv_a, send_b, recv_b,
):
    gx, gy = lax.axis_index("gx"), lax.axis_index("gy")
    q = (gx // 4) * 4 + lax.rem(gy, 4)
    p = lax.rem(gx, 4) * 4 + gy // 4

    def near(d):
        to = lax.rem(q + d, 8)
        return ((to // 4) * 4 + lax.rem(gx, 4), (gy // 4) * 4 + lax.rem(to, 4))

    def far(d):
        to = lax.rem(p + d, 16)
        return ((gx // 4) * 4 + to // 4, lax.rem(to, 4) * 4 + lax.rem(gy, 4))

    barrier = pltpu.get_barrier_semaphore()
    for d in range(1, 8):
        pl.semaphore_signal(barrier, inc=1, device_id=near(d), device_id_type=MESH)
    for d in range(1, 16):
        pl.semaphore_signal(barrier, inc=1, device_id=far(d), device_id_type=MESH)

    vals_a[...] = jnp.zeros_like(vals_a)
    vals_b[...] = jnp.zeros_like(vals_b)
    part[...] = jnp.zeros_like(part)

    lane8 = lax.broadcasted_iota(jnp.int32, (8, LANES), 1)
    spare = spare_lanes()

    def pick(g, carry):
        a = jnp.zeros((8, LANES), jnp.float32)
        b = jnp.zeros((8, LANES), jnp.float32)
        for j in range(LANES):
            code = take[g, j]
            tile = pltpu.roll(table[code >> 7], code & (LANES - 1), 1)
            a = jnp.where(lane8 == j, tile, a)
            b = jnp.where(spare == j, tile, b)
        at = pl.multiple_of(g * 8, 8)
        acc_a[pl.ds(at, 8), :] = a
        acc_b[pl.ds(at, 8), :] = b
        return carry

    lax.fori_loop(0, 32, pick, 0)

    diag = diagonal()
    beam = slots[0]
    values = []
    for n in range(STEPS):
        base = (6, 3, 0)[n]
        got = [acc_a[pl.ds(base + c, 32, stride=8), :] for c in range(3 if n else 2)]
        if n == 0:
            ninth = jnp.zeros((32, LANES), jnp.float32)
            for k in range(3):
                piece = pltpu.roll(acc_b[pl.ds(k, 32, stride=8), :], 32 * (k + 1), 1)
                ninth = jnp.where(third[...] == float(k), piece, ninth)
            got.append(ninth)
        seen = sum(slots[1 + c] * got[c] for c in range(3))
        r = seen - seen_obs[n]
        resid[n] = r
        for b in range(BEAMS):
            values.append(jnp.where(beam == float(b), r, 0.0))
    sums = list_sums(values)
    for i in range(STEPS * BEAMS):
        block = jnp.where(diag, sums[32 * i : 32 * i + 32, :], 0.0)
        part[pl.ds(i, 1), :] = jnp.sum(block, axis=0, keepdims=True)
    pl.semaphore_wait(barrier, 22)

    blank = jnp.zeros((64, LANES), jnp.float32)

    def clear(i, carry):
        for ref in empty:
            ref[pl.ds(pl.multiple_of(i * 64, 64), 64), :] = blank
        return carry

    half_way = CX * CY * TILE // 128

    def spread(src, inbox, send, recv, where_to, peers, first):
        copies = []
        for d in range(1, peers):
            copy = pltpu.make_async_remote_copy(
                src_ref=src, dst_ref=inbox.at[d - 1], send_sem=send.at[d - 1], recv_sem=recv.at[d - 1],
                device_id=where_to(d), device_id_type=MESH,
            )
            copy.start()
            copies.append(copy)
        lax.fori_loop(first, first + half_way, clear, 0)
        for copy in copies:
            copy.wait()

    spread(part, inbox_a, send_a, recv_a, near, 8, 0)
    acc = part[...]
    for d in range(7):
        acc = acc + inbox_a[d]
    half[...] = acc
    spread(half, inbox_b, send_b, recv_b, far, 16, half_way)
    for d in range(15):
        acc = acc + inbox_b[d]

    total = acc * (1.0 / GATES)
    means = list_sums([jnp.where(diag, total[i : i + 1, :], 0.0) for i in range(STEPS * BEAMS)])
    for n in range(STEPS):
        at = 32 * BEAMS * n
        mean = jnp.zeros((32, LANES), jnp.float32)
        for b in range(BEAMS):
            mean = jnp.where(beam == float(b), means[at + 32 * b : at + 32 * b + 32, :], mean)
        misfit = jnp.where(beam >= 0.0, resid[n] - mean, 0.0)
        base = (6, 3, 0)[n]
        for c in range(3):
            if base + c < 8:
                vals_a[pl.ds(base + c, 32, stride=8), :] = slots[1 + c] * misfit
                continue
            for k in range(3):
                piece = jnp.where(third[...] == float(k), slots[1 + c] * misfit, 0.0)
                vals_b[pl.ds(k, 32, stride=8), :] = pltpu.roll(piece, NZ - 32 * k, 1)


def gather(take, table, third, slots, seen_obs):
    rows = pltpu.VMEM((256, LANES), jnp.float32)
    block = pltpu.VMEM((16, LANES), jnp.float32)
    return pl.pallas_call(
        gather_kernel,
        out_shape=[f32(256, LANES), f32(256, LANES)] + [f32(CX * CY * TILE, LANES)] * COPIES,
        in_specs=[SMEM] + [VMEM] * 4,
        out_specs=[VMEM] * (2 + COPIES),
        scratch_shapes=[
            rows, rows, pltpu.VMEM((STEPS, 32, LANES), jnp.float32), block, block,
            pltpu.VMEM((7, 16, LANES), jnp.float32), pltpu.VMEM((15, 16, LANES), jnp.float32),
            pltpu.SemaphoreType.DMA((7,)), pltpu.SemaphoreType.DMA((7,)),
            pltpu.SemaphoreType.DMA((15,)), pltpu.SemaphoreType.DMA((15,)),
        ],
        compiler_params=pltpu.CompilerParams(collective_id=1, has_side_effects=True, vmem_limit_bytes=16 * MIB),
        name="gather",
    )(take, table, third, slots, seen_obs)


def scatter_kernel(give, vals_a, vals_b, *rest):
    f3, f2, f1 = rest[COPIES : COPIES + 3]
    sums = rest[COPIES + 3 :]
    lane8 = lax.broadcasted_iota(jnp.int32, (8, LANES), 1)
    spare = spare_lanes()

    def place(g, carry):
        at = pl.multiple_of(g * 8, 8)
        va = vals_a[pl.ds(at, 8), :]
        vb = vals_b[pl.ds(at, 8), :]
        for j in range(LANES):
            code = give[g, j]
            to = pl.ds(pl.multiple_of(code >> 7, TILE), TILE)
            v = jnp.where(lane8 == j, va, jnp.where(spare == j, vb, 0.0))
            out = sums[j % COPIES]
            out[to, :] = out[to, :] + pltpu.roll(v, code & (LANES - 1), 1)
        return carry

    lax.fori_loop(0, 32, place, 0)
    keep = lane8 < NZ

    def unpack(y, carry):
        for r in range(0, CX, 8):
            rows = []
            for k in range(8):
                at = pl.ds((y * CX + r) * TILE + k, 8, stride=TILE)
                rows.append(sum(ref[at, :] for ref in sums))
            pieces = [pltpu.roll(rows[k], 32 * (k + 1), 1) for k in range(3)]
            ninth = jnp.where(lane8 < 32, pieces[0], jnp.where(lane8 < 64, pieces[1], pieces[2]))
            rows = [jnp.where(keep, v, 0.0) for v in rows[:3]] + rows[3:] + [jnp.where(keep, ninth, 0.0)]
            for i, out in enumerate((f3, f2, f1)):
                for c in range(3):
                    out[c, y, pl.ds(r, 8), :] = rows[3 * i + c]
        return carry

    lax.fori_loop(0, CY, unpack, 0)


def scatter(give, vals_a, vals_b, empty):
    table = f32(CX * CY * TILE, LANES)
    field = f32(3, CY, CX, LANES)
    return pl.pallas_call(
        scatter_kernel,
        out_shape=[field, field, field] + [table] * COPIES,
        in_specs=[SMEM] + [VMEM] * (2 + COPIES),
        out_specs=[VMEM] * (3 + COPIES),
        input_output_aliases={3 + i: 3 + i for i in range(COPIES)},
        compiler_params=pltpu.CompilerParams(vmem_limit_bytes=16 * MIB),
        name="scatter",
    )(give, vals_a, vals_b, *empty)[:3]


def adjoint_kernel(w0, w1, w2, f3, f2, f1, out, a3, a2, a1, sides, inbox, send, recv):
    n_gx, n_gy, gx, gy = sizes()
    where = (n_gx, n_gy, gx, gy)
    barrier = pltpu.get_barrier_semaphore()
    for target in (
        (lax.rem(gx + n_gx - 1, n_gx), gy), (lax.rem(gx + 1, n_gx), gy),
        (gx, lax.rem(gy + n_gy - 1, n_gy)), (gx, lax.rem(gy + 1, n_gy)),
    ):
        pl.semaphore_signal(barrier, inc=1, device_id=target, device_id_type=MESH)

    def fill(y, carry):
        for c in range(3):
            a3[c, y + 1, pl.ds(TOP, CX), :] = f3[c, y]
        return carry

    lax.fori_loop(0, CY, fill, 0)
    clear_rims((a3, a2, a1))
    keep = levels()
    inside = inside_grid(*where)

    def meet_rims(src, dst, n):
        for s in range(4):
            for y in range(0, CY, 8):
                ref, at = layer_at(src, s, 1, s // 2, y)
                factor = HALF * (1.0 + ref[at]) if s % 2 else HALF * (1.0 - ref[at])
                for c in range(3):
                    v = jnp.where(inside[s], inbox[n, OPPOSITE[s], c, pl.ds(y, 8), :], 0.0)
                    ref, at = layer_at(dst, s, 0, c, y)
                    ref[at] = ref[at] + factor * v

    def pull(src, adj, dst, force):
        def body(y, r):
            for c, v in enumerate(pull_block(src, adj, y, r)):
                v = jnp.where(keep, v, 0.0)
                if force is not None:
                    v = v + force[c, y - 1, pl.ds(r - TOP, 8), :]
                dst[c, y, pl.ds(r, 8), :] = v
        return body

    for n, (src, adj, dst, force) in enumerate(((w2, a3, a2, f2), (w1, a2, a1, f1), (w0, a1, a3, None))):
        body = pull(src, adj, dst, force)
        pack_rims(adj, sides.at[n])
        if n == 0:
            pl.semaphore_wait(barrier, 4)
        copies = send_rims(sides.at[n], inbox.at[n], send.at[n], recv.at[n], *where)
        over_tile(body)
        for copy in copies:
            copy.wait()
        meet_rims(src, dst, n)

    lane = lax.broadcasted_iota(jnp.int32, (CX, LANES), 1)
    for c in range(3):
        for y in range(0, CY, 4):
            v = [a3[c, y + 1 + i, pl.ds(TOP, CX), :] for i in range(4)]
            v = [v[0], pltpu.roll(v[1], 96, 1), pltpu.roll(v[2], 64, 1), pltpu.roll(v[3], 32, 1)]
            t = [
                jnp.where(lane < 96, v[0], v[1]),
                jnp.where(lane < 64, v[1], v[2]),
                jnp.where(lane < 32, v[2], v[3]),
            ]
            for i in range(3):
                out[c, :, pl.ds(y * NZ + LANES * i, LANES)] = t[i]


def adjoint(wides, fields):
    wide = pltpu.VMEM((3, WIDE, ROWS, LANES), jnp.float32)
    rim = pltpu.VMEM((STEPS, 4, 3, 32, LANES), jnp.float32)
    return pl.pallas_call(
        adjoint_kernel,
        out_shape=f32(3, CX, CY * NZ),
        in_specs=[VMEM] * 6,
        out_specs=VMEM,
        scratch_shapes=[wide] * 3 + [
            rim, rim, pltpu.SemaphoreType.DMA((STEPS, 4)), pltpu.SemaphoreType.DMA((STEPS, 4)),
        ],
        compiler_params=pltpu.CompilerParams(collective_id=2, has_side_effects=True, vmem_limit_bytes=24 * MIB),
        name="adjoint",
    )(*wides, *fields)


def local(initial_state, beam_dir, gate_obs, slot_beam, slot_cell):
    count = slot_cell.shape[1]
    capacity = slot_cell.shape[2]
    rows = 5 * capacity + 8

    def at_row(block, first):
        return jnp.pad(block, ((first, rows - first - block.shape[0]), (0, count - block.shape[1])))

    lists = (
        at_row(slot_cell[0].T.astype(jnp.float32), 0)
        + at_row(jnp.transpose(gate_obs[:, 0], (0, 2, 1)).reshape(-1, count), capacity)
        + at_row(slot_beam[0].T.astype(jnp.float32), 4 * capacity)
        + at_row(beam_dir, 5 * capacity)
    )
    w0, w1, w2, table, take, give, third, slots, seen_obs = forward(initial_state, lists)
    vals_a, vals_b, *empty = gather(take, table, third, slots, seen_obs)
    fields = scatter(give, vals_a, vals_b, empty)
    return adjoint((w0, w1, w2), fields)


def solution(mesh):
    in_specs = (
        P(None, "gx", "gy"),
        P(None, ("gx", "gy")),
        P(None, ("gx", "gy"), None, None),
        P(("gx", "gy"), None, None),
        P(("gx", "gy"), None, None),
    )
    out_specs = P(None, "gx", "gy")
    return jax.shard_map(local, mesh=mesh, in_specs=in_specs, out_specs=out_specs, check_vma=False)
```

```python
import jax
import jax.numpy as jnp
from jax import lax
from jax.experimental import pallas as pl
from jax.experimental.pallas import tpu as pltpu
from jax.sharding import PartitionSpec as P

NZ = 96
LANES = 128
GATES = 512
BEAMS = 4
STEPS = 3
TIME_STEP = 0.2
VISCOSITY = 0.5
HALF = 0.5 * TIME_STEP
CX = 32
CY = 32
TOP = 8
ROWS = CX + 2 * TOP
WIDE = CY + 2
COPIES = 4
TILE = 8
UNROLL = 4
MIB = 1024 * 1024
MESH = pl.DeviceIdType.MESH
VMEM = pl.BlockSpec(memory_space=pltpu.VMEM)
SMEM = pl.BlockSpec(memory_space=pltpu.SMEM)


def f32(*shape):
    return jax.ShapeDtypeStruct(shape, jnp.float32)


def sizes():
    return lax.axis_size("gx"), lax.axis_size("gy"), lax.axis_index("gx"), lax.axis_index("gy")


def shift_up(v):
    return pltpu.roll(v, LANES - 1, 1)


def shift_down(v):
    return pltpu.roll(v, 1, 1)


def levels():
    return lax.broadcasted_iota(jnp.int32, (8, LANES), 1) < NZ


def step_block(src, y, r):
    rows, fore, back = pl.ds(r, 8), pl.ds(r + 1, 8), pl.ds(r - 1, 8)
    centre = [src[c, y, rows, :] for c in range(3)]
    less = [1.0 - v for v in centre]
    more = [1.0 + v for v in centre]
    out = []
    for c in range(3):
        v = centre[c]
        total = src[c, y, fore, :] * less[0] + src[c, y, back, :] * more[0]
        total += src[c, y + 1, rows, :] * less[1] + src[c, y - 1, rows, :] * more[1]
        total += shift_up(v) * less[2] + shift_down(v) * more[2]
        out.append((1.0 - 6.0 * HALF) * v + HALF * total)
    return out


def pull_block(src, adj, y, r):
    rows, fore, back = pl.ds(r, 8), pl.ds(r + 1, 8), pl.ds(r - 1, 8)
    near = []
    for c in range(3):
        v = src[c, y, rows, :]
        near.append((src[c, y, fore, :], src[c, y, back, :], src[c, y + 1, rows, :], src[c, y - 1, rows, :],
                     shift_up(v), shift_down(v)))
    factors = [1.0 + near[0][0], 1.0 - near[0][1], 1.0 + near[1][2], 1.0 - near[1][3],
               1.0 + near[2][4], 1.0 - near[2][5]]
    a = [adj[c, y, rows, :] for c in range(3)]
    out = []
    for c in range(3):
        total = adj[c, y, fore, :] * factors[0] + adj[c, y, back, :] * factors[1]
        total += adj[c, y + 1, rows, :] * factors[2] + adj[c, y - 1, rows, :] * factors[3]
        total += shift_up(a[c]) * factors[4] + shift_down(a[c]) * factors[5]
        for k in range(3):
            total -= a[k] * (near[k][2 * c] - near[k][2 * c + 1])
        out.append((1.0 - 6.0 * HALF) * a[c] + HALF * total)
    return out


def send_rims(sides, inbox, send, recv, n_gx, n_gy, gx, gy):
    targets = (
        (lax.rem(gx + n_gx - 1, n_gx), gy), (lax.rem(gx + 1, n_gx), gy),
        (gx, lax.rem(gy + n_gy - 1, n_gy)), (gx, lax.rem(gy + 1, n_gy)),
    )
    copies = []
    for s in (2, 3, 0, 1):
        target = targets[s]
        copy = pltpu.make_async_remote_copy(
            src_ref=sides.at[s], dst_ref=inbox.at[s], send_sem=send.at[s], recv_sem=recv.at[s],
            device_id=target, device_id_type=MESH,
        )
        copy.start()
        copies.append(copy)
    return copies


def over_tile(body):
    def layer(y, carry):
        for r in range(TOP, TOP + CX, 8):
            body(y, r)
        return carry

    lax.fori_loop(1, CY + 1, layer, 0, unroll=UNROLL)


def clear_rims(fields):
    blank = jnp.zeros((8, LANES), jnp.float32)

    def layer(y, carry):
        for field in fields:
            for c in range(3):
                field[c, y, pl.ds(0, 8), :] = blank
                field[c, y, pl.ds(TOP + CX, 8), :] = blank
        return carry

    lax.fori_loop(1, CY + 1, layer, 0)
    for field in fields:
        for c in range(3):
            for y in (0, CY + 1):
                for r in range(TOP, TOP + CX, 8):
                    field[c, y, pl.ds(r, 8), :] = blank


def layer_at(field, side, depth, c, y):
    if side < 2:
        row = TOP - depth if side == 0 else TOP + CX - 1 + depth
        return field.reshape(3, WIDE * ROWS, LANES), (c, pl.ds((y + 1) * ROWS + row, 8, stride=ROWS), slice(None))
    return field, (c, 1 - depth if side == 2 else CY + depth, pl.ds(TOP + y, 8), slice(None))


OPPOSITE = (1, 0, 3, 2)


def inside_grid(n_gx, n_gy, gx, gy):
    return (gx > 0, gx < n_gx - 1, gy > 0, gy < n_gy - 1)


def pack_rims(field, sides):
    for s in range(4):
        for c in range(3):
            for y in range(0, CY, 8):
                ref, at = layer_at(field, s, 0, c, y)
                sides[s, c, pl.ds(y, 8), :] = ref[at]


def regroup(block, quantity):
    lane = lax.broadcasted_iota(jnp.int32, (32, LANES), 1)
    out = None
    for k in range(4):
        piece = block[32 * k : 32 * k + 32, :]
        turn = (32 * (k - quantity)) % LANES
        if turn:
            piece = pltpu.roll(piece, turn, 1)
        out = piece if out is None else jnp.where(lane >= 32 * k, piece, out)
    return out


def forward_kernel(
    state, lists,
    w0, w1, w2, table, take, give, third, slots, seen_obs,
    got, mid, msg, sides, inbox, send, recv, list_send, list_recv, own,
):
    n_gx, n_gy, gx, gy = sizes()
    barrier = pltpu.get_barrier_semaphore()

    def along_x(i):
        to = lax.rem(gx + i, n_gx)
        return to, (to, gy)

    def along_y(i):
        to = lax.rem(gy + i, n_gy)
        return to, (gx, to)

    def hail(line):
        def body(i, carry):
            pl.semaphore_signal(barrier, inc=1, device_id=line(i)[1], device_id_type=MESH)
            return carry
        return body

    lax.fori_loop(1, n_gx, hail(along_x), 0)
    lax.fori_loop(1, n_gy, hail(along_y), 0)
    lane = lax.broadcasted_iota(jnp.int32, (CX, LANES), 1)
    for c in range(3):
        for y in range(0, CY, 4):
            t = [state[c, :, pl.ds(y * NZ + LANES * i, LANES)] for i in range(3)]
            planes = [
                t[0],
                pltpu.roll(jnp.where(lane >= 96, t[0], t[1]), 32, 1),
                pltpu.roll(jnp.where(lane >= 64, t[1], t[2]), 64, 1),
                pltpu.roll(t[2], 96, 1),
            ]
            for i, v in enumerate(planes):
                w0[c, y + 1 + i, pl.ds(TOP, CX), :] = jnp.where(lane < NZ, v, 0.0)
    pack_rims(w0, sides.at[0])
    pl.semaphore_wait(barrier, n_gx + n_gy - 2)

    where = (n_gx, n_gy, gx, gy)
    copies = send_rims(sides.at[0], inbox.at[0], send.at[0], recv.at[0], *where)
    kind = lists[pl.ds(LANES, 32), :]
    tails = [kind]
    beam_dir = lists[pl.ds(LANES + 32, 8), :]
    for c in range(3):
        weight = jnp.zeros(kind.shape, jnp.float32)
        for b in range(BEAMS):
            weight = jnp.where(kind == float(b), beam_dir[c : c + 1, b : b + 1], weight)
        tails.append(weight)
    msg[:, :, 0, :] = lists[pl.ds(0, LANES), :].T.reshape(n_gx, n_gy, LANES)
    msg[:, :, 1, :] = jnp.concatenate(tails, axis=0).T.reshape(n_gx, n_gy, LANES)


    def post(src, dst, line, sems):
        def body(i, carry):
            to, target = line(i)
            pltpu.make_async_remote_copy(
                src_ref=src(to), dst_ref=dst, send_sem=list_send.at[sems], recv_sem=list_recv.at[sems],
                device_id=target, device_id_type=MESH,
            ).start()
            return carry
        return body

    def settle(src, dst, line, sems):
        pltpu.make_async_remote_copy(
            src_ref=src, dst_ref=dst, send_sem=list_send.at[sems], recv_sem=list_recv.at[sems],
            device_id=line(1)[1], device_id_type=MESH,
        ).wait()

    lax.fori_loop(1, n_gx, post(lambda to: msg.at[to], mid.at[gx], along_x, 0), 0)
    mine = pltpu.make_async_copy(msg.at[gx], mid.at[gx], own.at[0])
    mine.start()

    def forward_lists():
        mine.wait()
        rest = pl.ds(0, n_gx - 1)
        settle(msg.at[rest], mid.at[rest], along_x, 0)
        lax.fori_loop(1, n_gy, post(lambda to: mid.at[:, to], got.at[:, gy], along_y, 1), 0)
        copy = pltpu.make_async_copy(mid.at[:, gy], got.at[:, gy], own.at[1])
        copy.start()
        return copy

    clear_rims((w0, w1, w2))
    keep = levels()

    def advance(src, dst):
        def body(y, r):
            for c, v in enumerate(step_block(src, y, r)):
                dst[c, y, pl.ds(r, 8), :] = jnp.where(keep, v, 0.0)
        return body

    cells = table.reshape(CX * CY * TILE, LANES)

    def tables(y, r):
        at = ((y - 1) * CX + (r - TOP)) * TILE
        spare = w1[2, y, pl.ds(r, 8), :]
        for c, v in enumerate(step_block(w2, y, r)):
            cells[pl.ds(at + c, 8, stride=TILE), :] = jnp.where(keep, v, pltpu.roll(spare, NZ - 32 * c, 1))
            cells[pl.ds(at + 3 + c, 8, stride=TILE), :] = w2[c, y, pl.ds(r, 8), :]
            if c < 2:
                cells[pl.ds(at + 6 + c, 8, stride=TILE), :] = w1[c, y, pl.ds(r, 8), :]

    def target(dst, s, c, y):
        if dst is not None:
            return layer_at(dst, s, 0, c, y)
        if s < 2:
            return cells, (pl.ds((y * CX + (CX - 1) * s) * TILE + c, 8, stride=CX * TILE), slice(None))
        return cells, (pl.ds(((CY - 1) * (s - 2) * CX + y) * TILE + c, 8, stride=TILE), slice(None))

    inside = inside_grid(*where)

    def meet_rims(src, dst, n):
        for s in range(4):
            for y in range(0, CY, 8):
                rows = pl.ds(y, 8)
                speed = sides[n, s, s // 2, rows, :]
                factor = HALF * (1.0 - speed) if s % 2 else HALF * (1.0 + speed)
                for c in range(3):
                    v = jnp.where(inside[s], inbox[n, OPPOSITE[s], c, rows, :], 0.0)
                    ref, at = layer_at(src, s, 1, c, y)
                    ref[at] = v
                    ref, at = target(dst, s, c, y)
                    ref[at] = ref[at] + factor * v

    for n, (src, dst, body) in enumerate(((w0, w1, advance(w0, w1)), (w1, w2, advance(w1, w2)), (w2, None, tables))):
        if n:
            pack_rims(src, sides.at[n])
            copies = send_rims(sides.at[n], inbox.at[n], send.at[n], recv.at[n], *where)
        if n == 1:
            last = forward_lists()
        over_tile(body)
        for copy in copies:
            copy.wait()
        meet_rims(src, dst, n)

    last.wait()
    rest = pl.ds(0, n_gy - 1)
    settle(mid.at[:, rest], got.at[:, rest], along_y, 1)
    g0 = got[:, :, 0, :].reshape(LANES, LANES)
    g1 = got[:, :, 1, :].reshape(LANES, LANES)
    where_to = regroup(g0, 0).astype(jnp.int32)
    x = ((where_to >> 10) * 171) >> 9
    rem = where_to - x * (CY * NZ)
    y = ((rem >> 5) * 171) >> 9
    z = rem - y * NZ
    lane = lax.broadcasted_iota(jnp.int32, (32, LANES), 1)
    at = (y * CX + x) * LANES
    take[...] = at + ((lane - z) & (LANES - 1))
    give[...] = at * TILE + ((z - lane) & (LANES - 1))
    third[...] = (z >> 5).astype(jnp.float32)
    for j in range(4):
        slots[j] = regroup(g1, j)
    for n in range(STEPS):
        seen_obs[n] = regroup(g0, 1 + n)


def forward(state, lists):
    box = pltpu.VMEM((lax.axis_size("gx"), lax.axis_size("gy"), 2, LANES), jnp.float32)
    wide, table = f32(3, WIDE, ROWS, LANES), f32(CX * CY, TILE, LANES)
    codes = jax.ShapeDtypeStruct((32, LANES), jnp.int32)
    rim = pltpu.VMEM((STEPS, 4, 3, 32, LANES), jnp.float32)
    return pl.pallas_call(
        forward_kernel,
        out_shape=[
            wide, wide, wide, table, codes, codes, f32(32, LANES), f32(4, 32, LANES), f32(STEPS, 32, LANES),
        ],
        in_specs=[VMEM] * 2,
        out_specs=[VMEM] * 9,
        scratch_shapes=[
            box, box, box, rim, rim,
            pltpu.SemaphoreType.DMA((STEPS, 4)), pltpu.SemaphoreType.DMA((STEPS, 4)),
            pltpu.SemaphoreType.DMA((2,)), pltpu.SemaphoreType.DMA((2,)), pltpu.SemaphoreType.DMA((2,)),
        ],
        compiler_params=pltpu.CompilerParams(collective_id=0, has_side_effects=True, vmem_limit_bytes=24 * MIB),
        name="forward",
    )(state, lists)


def spare_lanes():
    lane = lax.broadcasted_iota(jnp.int32, (8, LANES), 1)
    row = lax.broadcasted_iota(jnp.int32, (8, LANES), 0)
    return jnp.where(row < 3, (lane + 32 * (row + 1)) & (LANES - 1), -1)


def same_list():
    a = lax.broadcasted_iota(jnp.int32, (LANES, LANES), 0) >> 5
    b = lax.broadcasted_iota(jnp.int32, (LANES, LANES), 1) >> 5
    return (a == b).astype(jnp.float32)


def diagonal():
    g = lax.broadcasted_iota(jnp.int32, (32, LANES), 0)
    lane = lax.broadcasted_iota(jnp.int32, (32, LANES), 1)
    return (lane & 31) == g


def list_sums(values):
    return jnp.dot(
        jnp.concatenate(values, axis=0), same_list(), precision=lax.Precision.HIGHEST,
        preferred_element_type=jnp.float32,
    )


def gather_kernel(
    take, table, third, slots, seen_obs,
    vals_a, vals_b, *rest,
):
    empty = rest[:COPIES]
    gather_body(take, table, third, slots, seen_obs, vals_a, vals_b, empty, *rest[COPIES:])


def gather_body(
    take, table, third, slots, seen_obs, vals_a, vals_b, empty,
    acc_a, acc_b, resid, part, half, inbox_a, inbox_b, send_a, recv_a, send_b, recv_b,
):
    gx, gy = lax.axis_index("gx"), lax.axis_index("gy")
    q = (gx // 4) * 4 + lax.rem(gy, 4)
    p = lax.rem(gx, 4) * 4 + gy // 4

    def near(d):
        to = lax.rem(q + d, 8)
        return ((to // 4) * 4 + lax.rem(gx, 4), (gy // 4) * 4 + lax.rem(to, 4))

    def far(d):
        to = lax.rem(p + d, 16)
        return ((gx // 4) * 4 + to // 4, lax.rem(to, 4) * 4 + lax.rem(gy, 4))

    barrier = pltpu.get_barrier_semaphore()
    for d in range(1, 8):
        pl.semaphore_signal(barrier, inc=1, device_id=near(d), device_id_type=MESH)
    for d in range(1, 16):
        pl.semaphore_signal(barrier, inc=1, device_id=far(d), device_id_type=MESH)

    vals_a[...] = jnp.zeros_like(vals_a)
    vals_b[...] = jnp.zeros_like(vals_b)
    part[...] = jnp.zeros_like(part)

    lane8 = lax.broadcasted_iota(jnp.int32, (8, LANES), 1)
    spare = spare_lanes()

    def pick(g, carry):
        a = jnp.zeros((8, LANES), jnp.float32)
        b = jnp.zeros((8, LANES), jnp.float32)
        for j in range(LANES):
            code = take[g, j]
            tile = pltpu.roll(table[code >> 7], code & (LANES - 1), 1)
            a = jnp.where(lane8 == j, tile, a)
            b = jnp.where(spare == j, tile, b)
        at = pl.multiple_of(g * 8, 8)
        acc_a[pl.ds(at, 8), :] = a
        acc_b[pl.ds(at, 8), :] = b
        return carry

    lax.fori_loop(0, 32, pick, 0, unroll=4)

    diag = diagonal()
    beam = slots[0]
    values = []
    for n in range(STEPS):
        base = (6, 3, 0)[n]
        got = [acc_a[pl.ds(base + c, 32, stride=8), :] for c in range(3 if n else 2)]
        if n == 0:
            ninth = jnp.zeros((32, LANES), jnp.float32)
            for k in range(3):
                piece = pltpu.roll(acc_b[pl.ds(k, 32, stride=8), :], 32 * (k + 1), 1)
                ninth = jnp.where(third[...] == float(k), piece, ninth)
            got.append(ninth)
        seen = sum(slots[1 + c] * got[c] for c in range(3))
        r = seen - seen_obs[n]
        resid[n] = r
        for b in range(BEAMS):
            values.append(jnp.where(beam == float(b), r, 0.0))
    sums = list_sums(values)
    for i in range(STEPS * BEAMS):
        block = jnp.where(diag, sums[32 * i : 32 * i + 32, :], 0.0)
        part[pl.ds(i, 1), :] = jnp.sum(block, axis=0, keepdims=True)
    pl.semaphore_wait(barrier, 22)

    blank = jnp.zeros((64, LANES), jnp.float32)

    def clear(i, carry):
        for ref in empty:
            ref[pl.ds(pl.multiple_of(i * 64, 64), 64), :] = blank
        return carry

    half_way = CX * CY * TILE // 128

    def spread(src, inbox, send, recv, where_to, peers, first):
        copies = []
        for d in range(1, peers):
            copy = pltpu.make_async_remote_copy(
                src_ref=src, dst_ref=inbox.at[d - 1], send_sem=send.at[d - 1], recv_sem=recv.at[d - 1],
                device_id=where_to(d), device_id_type=MESH,
            )
            copy.start()
            copies.append(copy)
        lax.fori_loop(first, first + half_way, clear, 0)
        for copy in copies:
            copy.wait()

    spread(part, inbox_a, send_a, recv_a, near, 8, 0)
    acc = part[...]
    for d in range(7):
        acc = acc + inbox_a[d]
    half[...] = acc
    spread(half, inbox_b, send_b, recv_b, far, 16, half_way)
    for d in range(15):
        acc = acc + inbox_b[d]

    total = acc * (1.0 / GATES)
    means = list_sums([jnp.where(diag, total[i : i + 1, :], 0.0) for i in range(STEPS * BEAMS)])
    for n in range(STEPS):
        at = 32 * BEAMS * n
        mean = jnp.zeros((32, LANES), jnp.float32)
        for b in range(BEAMS):
            mean = jnp.where(beam == float(b), means[at + 32 * b : at + 32 * b + 32, :], mean)
        misfit = jnp.where(beam >= 0.0, resid[n] - mean, 0.0)
        base = (6, 3, 0)[n]
        for c in range(3):
            if base + c < 8:
                vals_a[pl.ds(base + c, 32, stride=8), :] = slots[1 + c] * misfit
                continue
            for k in range(3):
                piece = jnp.where(third[...] == float(k), slots[1 + c] * misfit, 0.0)
                vals_b[pl.ds(k, 32, stride=8), :] = pltpu.roll(piece, NZ - 32 * k, 1)


def gather(take, table, third, slots, seen_obs):
    rows = pltpu.VMEM((256, LANES), jnp.float32)
    block = pltpu.VMEM((16, LANES), jnp.float32)
    return pl.pallas_call(
        gather_kernel,
        out_shape=[f32(256, LANES), f32(256, LANES)] + [f32(CX * CY * TILE, LANES)] * COPIES,
        in_specs=[SMEM] + [VMEM] * 4,
        out_specs=[VMEM] * (2 + COPIES),
        scratch_shapes=[
            rows, rows, pltpu.VMEM((STEPS, 32, LANES), jnp.float32), block, block,
            pltpu.VMEM((7, 16, LANES), jnp.float32), pltpu.VMEM((15, 16, LANES), jnp.float32),
            pltpu.SemaphoreType.DMA((7,)), pltpu.SemaphoreType.DMA((7,)),
            pltpu.SemaphoreType.DMA((15,)), pltpu.SemaphoreType.DMA((15,)),
        ],
        compiler_params=pltpu.CompilerParams(collective_id=1, has_side_effects=True, vmem_limit_bytes=16 * MIB),
        name="gather",
    )(take, table, third, slots, seen_obs)


def scatter_kernel(give, vals_a, vals_b, *rest):
    f3, f2, f1 = rest[COPIES : COPIES + 3]
    sums = rest[COPIES + 3 : -1]
    layer = rest[-1]
    lane8 = lax.broadcasted_iota(jnp.int32, (8, LANES), 1)
    spare = spare_lanes()

    def place(g, carry):
        at = pl.multiple_of(g * 8, 8)
        va = vals_a[pl.ds(at, 8), :]
        vb = vals_b[pl.ds(at, 8), :]
        for j in range(LANES):
            code = give[g, j]
            to = pl.ds(pl.multiple_of(code >> 7, TILE), TILE)
            v = jnp.where(lane8 == j, va, jnp.where(spare == j, vb, 0.0))
            out = sums[j % COPIES]
            out[to, :] = out[to, :] + pltpu.roll(v, code & (LANES - 1), 1)
        return carry

    lax.fori_loop(0, 32, place, 0, unroll=4)
    keep = lane8 < NZ

    def unpack(y, carry):
        first = pl.multiple_of(y * CX * TILE, CX * TILE)
        for x in range(CX):
            at = pl.ds(first + x * TILE, TILE)
            layer[pl.ds(x * TILE, TILE), :] = sum(ref[at, :] for ref in sums)
        for r in range(0, CX, 8):
            rows = [layer[pl.ds(r * TILE + k, 8, stride=TILE), :] for k in range(8)]
            pieces = [pltpu.roll(rows[k], 32 * (k + 1), 1) for k in range(3)]
            ninth = jnp.where(lane8 < 32, pieces[0], jnp.where(lane8 < 64, pieces[1], pieces[2]))
            rows = [jnp.where(keep, v, 0.0) for v in rows[:3]] + rows[3:] + [jnp.where(keep, ninth, 0.0)]
            for i, out in enumerate((f3, f2, f1)):
                for c in range(3):
                    out[c, y, pl.ds(r, 8), :] = rows[3 * i + c]
        return carry

    lax.fori_loop(0, CY, unpack, 0, unroll=4)


def scatter(give, vals_a, vals_b, empty):
    table = f32(CX * CY * TILE, LANES)
    field = f32(3, CY, CX, LANES)
    return pl.pallas_call(
        scatter_kernel,
        out_shape=[field, field, field] + [table] * COPIES,
        in_specs=[SMEM] + [VMEM] * (2 + COPIES),
        out_specs=[VMEM] * (3 + COPIES),
        scratch_shapes=[pltpu.VMEM((CX * TILE, LANES), jnp.float32)],
        input_output_aliases={3 + i: 3 + i for i in range(COPIES)},
        compiler_params=pltpu.CompilerParams(vmem_limit_bytes=16 * MIB),
        name="scatter",
    )(give, vals_a, vals_b, *empty)[:3]


def adjoint_kernel(w0, w1, w2, f3, f2, f1, out, a3, a2, a1, sides, inbox, send, recv):
    n_gx, n_gy, gx, gy = sizes()
    where = (n_gx, n_gy, gx, gy)
    barrier = pltpu.get_barrier_semaphore()
    for target in (
        (lax.rem(gx + n_gx - 1, n_gx), gy), (lax.rem(gx + 1, n_gx), gy),
        (gx, lax.rem(gy + n_gy - 1, n_gy)), (gx, lax.rem(gy + 1, n_gy)),
    ):
        pl.semaphore_signal(barrier, inc=1, device_id=target, device_id_type=MESH)

    def fill(y, carry):
        for c in range(3):
            a3[c, y + 1, pl.ds(TOP, CX), :] = f3[c, y]
        return carry

    lax.fori_loop(0, CY, fill, 0)
    keep = levels()
    inside = inside_grid(*where)

    def meet_rims(src, dst, n):
        for s in range(4):
            for y in range(0, CY, 8):
                ref, at = layer_at(src, s, 1, s // 2, y)
                factor = HALF * (1.0 + ref[at]) if s % 2 else HALF * (1.0 - ref[at])
                for c in range(3):
                    v = jnp.where(inside[s], inbox[n, OPPOSITE[s], c, pl.ds(y, 8), :], 0.0)
                    ref, at = layer_at(dst, s, 0, c, y)
                    ref[at] = ref[at] + factor * v

    def pull(src, adj, dst, force):
        def body(y, r):
            for c, v in enumerate(pull_block(src, adj, y, r)):
                v = jnp.where(keep, v, 0.0)
                if force is not None:
                    v = v + force[c, y - 1, pl.ds(r - TOP, 8), :]
                dst[c, y, pl.ds(r, 8), :] = v
        return body

    for n, (src, adj, dst, force) in enumerate(((w2, a3, a2, f2), (w1, a2, a1, f1), (w0, a1, a3, None))):
        body = pull(src, adj, dst, force)
        pack_rims(adj, sides.at[n])
        if n == 0:
            pl.semaphore_wait(barrier, 4)
        copies = send_rims(sides.at[n], inbox.at[n], send.at[n], recv.at[n], *where)
        if n == 0:
            clear_rims((a3, a2, a1))
        over_tile(body)
        for copy in copies:
            copy.wait()
        meet_rims(src, dst, n)

    lane = lax.broadcasted_iota(jnp.int32, (CX, LANES), 1)
    for c in range(3):
        for y in range(0, CY, 4):
            v = [a3[c, y + 1 + i, pl.ds(TOP, CX), :] for i in range(4)]
            v = [v[0], pltpu.roll(v[1], 96, 1), pltpu.roll(v[2], 64, 1), pltpu.roll(v[3], 32, 1)]
            t = [
                jnp.where(lane < 96, v[0], v[1]),
                jnp.where(lane < 64, v[1], v[2]),
                jnp.where(lane < 32, v[2], v[3]),
            ]
            for i in range(3):
                out[c, :, pl.ds(y * NZ + LANES * i, LANES)] = t[i]


def adjoint(wides, fields):
    wide = pltpu.VMEM((3, WIDE, ROWS, LANES), jnp.float32)
    rim = pltpu.VMEM((STEPS, 4, 3, 32, LANES), jnp.float32)
    return pl.pallas_call(
        adjoint_kernel,
        out_shape=f32(3, CX, CY * NZ),
        in_specs=[VMEM] * 6,
        out_specs=VMEM,
        scratch_shapes=[wide] * 3 + [
            rim, rim, pltpu.SemaphoreType.DMA((STEPS, 4)), pltpu.SemaphoreType.DMA((STEPS, 4)),
        ],
        compiler_params=pltpu.CompilerParams(collective_id=2, has_side_effects=True, vmem_limit_bytes=24 * MIB),
        name="adjoint",
    )(*wides, *fields)


def local(initial_state, beam_dir, gate_obs, slot_beam, slot_cell):
    count = slot_cell.shape[1]
    capacity = slot_cell.shape[2]
    rows = 5 * capacity + 8

    def at_row(block, first):
        return jnp.pad(block, ((first, rows - first - block.shape[0]), (0, count - block.shape[1])))

    lists = (
        at_row(slot_cell[0].T.astype(jnp.float32), 0)
        + at_row(jnp.transpose(gate_obs[:, 0], (0, 2, 1)).reshape(-1, count), capacity)
        + at_row(slot_beam[0].T.astype(jnp.float32), 4 * capacity)
        + at_row(beam_dir, 5 * capacity)
    )
    w0, w1, w2, table, take, give, third, slots, seen_obs = forward(initial_state, lists)
    vals_a, vals_b, *empty = gather(take, table, third, slots, seen_obs)
    fields = scatter(give, vals_a, vals_b, empty)
    return adjoint((w0, w1, w2), fields)


def solution(mesh):
    in_specs = (
        P(None, "gx", "gy"),
        P(None, ("gx", "gy")),
        P(None, ("gx", "gy"), None, None),
        P(("gx", "gy"), None, None),
        P(("gx", "gy"), None, None),
    )
    out_specs = P(None, "gx", "gy")
    return jax.shard_map(local, mesh=mesh, in_specs=in_specs, out_specs=out_specs, check_vma=False)
```

```python
import jax
import jax.numpy as jnp
from jax import lax
from jax.experimental import pallas as pl
from jax.experimental.pallas import tpu as pltpu
from jax.sharding import PartitionSpec as P

NZ = 96
LANES = 128
GATES = 512
BEAMS = 4
STEPS = 3
TIME_STEP = 0.2
VISCOSITY = 0.5
HALF = 0.5 * TIME_STEP
CX = 32
CY = 32
TOP = 8
ROWS = CX + 2 * TOP
WIDE = CY + 2
COPIES = 4
TILE = 8
UNROLL = 4
MIB = 1024 * 1024
MESH = pl.DeviceIdType.MESH
VMEM = pl.BlockSpec(memory_space=pltpu.VMEM)
SMEM = pl.BlockSpec(memory_space=pltpu.SMEM)


def f32(*shape):
    return jax.ShapeDtypeStruct(shape, jnp.float32)


def sizes():
    return lax.axis_size("gx"), lax.axis_size("gy"), lax.axis_index("gx"), lax.axis_index("gy")


def shift_up(v):
    return pltpu.roll(v, LANES - 1, 1)


def shift_down(v):
    return pltpu.roll(v, 1, 1)


def levels():
    return lax.broadcasted_iota(jnp.int32, (8, LANES), 1) < NZ


def step_block(src, y, r):
    rows, fore, back = pl.ds(r, 8), pl.ds(r + 1, 8), pl.ds(r - 1, 8)
    centre = [src[c, y, rows, :] for c in range(3)]
    less = [1.0 - v for v in centre]
    more = [1.0 + v for v in centre]
    out = []
    for c in range(3):
        v = centre[c]
        total = src[c, y, fore, :] * less[0] + src[c, y, back, :] * more[0]
        total += src[c, y + 1, rows, :] * less[1] + src[c, y - 1, rows, :] * more[1]
        total += shift_up(v) * less[2] + shift_down(v) * more[2]
        out.append((1.0 - 6.0 * HALF) * v + HALF * total)
    return out


def pull_block(src, adj, y, r):
    rows, fore, back = pl.ds(r, 8), pl.ds(r + 1, 8), pl.ds(r - 1, 8)
    near = []
    for c in range(3):
        v = src[c, y, rows, :]
        near.append((src[c, y, fore, :], src[c, y, back, :], src[c, y + 1, rows, :], src[c, y - 1, rows, :],
                     shift_up(v), shift_down(v)))
    factors = [1.0 + near[0][0], 1.0 - near[0][1], 1.0 + near[1][2], 1.0 - near[1][3],
               1.0 + near[2][4], 1.0 - near[2][5]]
    a = [adj[c, y, rows, :] for c in range(3)]
    out = []
    for c in range(3):
        total = adj[c, y, fore, :] * factors[0] + adj[c, y, back, :] * factors[1]
        total += adj[c, y + 1, rows, :] * factors[2] + adj[c, y - 1, rows, :] * factors[3]
        total += shift_up(a[c]) * factors[4] + shift_down(a[c]) * factors[5]
        for k in range(3):
            total -= a[k] * (near[k][2 * c] - near[k][2 * c + 1])
        out.append((1.0 - 6.0 * HALF) * a[c] + HALF * total)
    return out


def send_rims(sides, inbox, send, recv, n_gx, n_gy, gx, gy):
    targets = (
        (lax.rem(gx + n_gx - 1, n_gx), gy), (lax.rem(gx + 1, n_gx), gy),
        (gx, lax.rem(gy + n_gy - 1, n_gy)), (gx, lax.rem(gy + 1, n_gy)),
    )
    copies = []
    for s in (2, 3, 0, 1):
        target = targets[s]
        copy = pltpu.make_async_remote_copy(
            src_ref=sides.at[s], dst_ref=inbox.at[s], send_sem=send.at[s], recv_sem=recv.at[s],
            device_id=target, device_id_type=MESH,
        )
        copy.start()
        copies.append(copy)
    return copies


def over_tile(body):
    def layer(y, carry):
        for r in range(TOP, TOP + CX, 8):
            body(y, r)
        return carry

    lax.fori_loop(1, CY + 1, layer, 0, unroll=UNROLL)


def clear_rims(fields):
    blank = jnp.zeros((8, LANES), jnp.float32)

    def layer(y, carry):
        for field in fields:
            for c in range(3):
                field[c, y, pl.ds(0, 8), :] = blank
                field[c, y, pl.ds(TOP + CX, 8), :] = blank
        return carry

    lax.fori_loop(1, CY + 1, layer, 0)
    for field in fields:
        for c in range(3):
            for y in (0, CY + 1):
                for r in range(TOP, TOP + CX, 8):
                    field[c, y, pl.ds(r, 8), :] = blank


def layer_at(field, side, depth, c, y):
    if side < 2:
        row = TOP - depth if side == 0 else TOP + CX - 1 + depth
        return field.reshape(3, WIDE * ROWS, LANES), (c, pl.ds((y + 1) * ROWS + row, 8, stride=ROWS), slice(None))
    return field, (c, 1 - depth if side == 2 else CY + depth, pl.ds(TOP + y, 8), slice(None))


OPPOSITE = (1, 0, 3, 2)


def inside_grid(n_gx, n_gy, gx, gy):
    return (gx > 0, gx < n_gx - 1, gy > 0, gy < n_gy - 1)


def pack_rims(field, sides):
    keep = levels()
    for s in range(4):
        for c in range(3):
            v = []
            for y in range(0, CY, 8):
                ref, at = layer_at(field, s, 0, c, y)
                v.append(ref[at])
            for k in range(3):
                sides[s, c, pl.ds(8 * k, 8), :] = jnp.where(keep, v[k], pltpu.roll(v[3], NZ - 32 * k, 1))


def rim_rows(inbox, side, c, inside):
    lane = lax.broadcasted_iota(jnp.int32, (8, LANES), 1)
    p = [inbox[side, c, pl.ds(8 * k, 8), :] for k in range(3)]
    q = [pltpu.roll(p[k], 32 * (k + 1), 1) for k in range(3)]
    p.append(jnp.where(lane < 32, q[0], jnp.where(lane < 64, q[1], q[2])))
    return [jnp.where((lane < NZ) & inside, v, 0.0) for v in p]


def regroup(block, quantity):
    lane = lax.broadcasted_iota(jnp.int32, (32, LANES), 1)
    out = None
    for k in range(4):
        piece = block[32 * k : 32 * k + 32, :]
        turn = (32 * (k - quantity)) % LANES
        if turn:
            piece = pltpu.roll(piece, turn, 1)
        out = piece if out is None else jnp.where(lane >= 32 * k, piece, out)
    return out


def forward_kernel(
    state, lists,
    w0, w1, w2, table, take, give, third, slots, seen_obs,
    got, mid, msg, sides, inbox, send, recv, list_send, list_recv, own,
):
    n_gx, n_gy, gx, gy = sizes()
    barrier = pltpu.get_barrier_semaphore()

    def along_x(i):
        to = lax.rem(gx + i, n_gx)
        return to, (to, gy)

    def along_y(i):
        to = lax.rem(gy + i, n_gy)
        return to, (gx, to)

    def hail(line):
        def body(i, carry):
            pl.semaphore_signal(barrier, inc=1, device_id=line(i)[1], device_id_type=MESH)
            return carry
        return body

    lax.fori_loop(1, n_gx, hail(along_x), 0)
    lax.fori_loop(1, n_gy, hail(along_y), 0)
    lane = lax.broadcasted_iota(jnp.int32, (CX, LANES), 1)
    for c in range(3):
        for y in range(0, CY, 4):
            t = [state[c, :, pl.ds(y * NZ + LANES * i, LANES)] for i in range(3)]
            planes = [
                t[0],
                pltpu.roll(jnp.where(lane >= 96, t[0], t[1]), 32, 1),
                pltpu.roll(jnp.where(lane >= 64, t[1], t[2]), 64, 1),
                pltpu.roll(t[2], 96, 1),
            ]
            for i, v in enumerate(planes):
                w0[c, y + 1 + i, pl.ds(TOP, CX), :] = jnp.where(lane < NZ, v, 0.0)
    pack_rims(w0, sides.at[0])
    pl.semaphore_wait(barrier, n_gx + n_gy - 2)

    where = (n_gx, n_gy, gx, gy)
    copies = send_rims(sides.at[0], inbox.at[0], send.at[0], recv.at[0], *where)
    kind = lists[pl.ds(LANES, 32), :]
    tails = [kind]
    beam_dir = lists[pl.ds(LANES + 32, 8), :]
    for c in range(3):
        weight = jnp.zeros(kind.shape, jnp.float32)
        for b in range(BEAMS):
            weight = jnp.where(kind == float(b), beam_dir[c : c + 1, b : b + 1], weight)
        tails.append(weight)
    msg[:, :, 0, :] = lists[pl.ds(0, LANES), :].T.reshape(n_gx, n_gy, LANES)
    msg[:, :, 1, :] = jnp.concatenate(tails, axis=0).T.reshape(n_gx, n_gy, LANES)


    def post(src, dst, line, sems):
        def body(i, carry):
            to, target = line(i)
            pltpu.make_async_remote_copy(
                src_ref=src(to), dst_ref=dst, send_sem=list_send.at[sems], recv_sem=list_recv.at[sems],
                device_id=target, device_id_type=MESH,
            ).start()
            return carry
        return body

    def settle(src, dst, line, sems):
        pltpu.make_async_remote_copy(
            src_ref=src, dst_ref=dst, send_sem=list_send.at[sems], recv_sem=list_recv.at[sems],
            device_id=line(1)[1], device_id_type=MESH,
        ).wait()

    lax.fori_loop(1, n_gx, post(lambda to: msg.at[to], mid.at[gx], along_x, 0), 0)
    mine = pltpu.make_async_copy(msg.at[gx], mid.at[gx], own.at[0])
    mine.start()

    def forward_lists():
        mine.wait()
        rest = pl.ds(0, n_gx - 1)
        settle(msg.at[rest], mid.at[rest], along_x, 0)
        lax.fori_loop(1, n_gy, post(lambda to: mid.at[:, to], got.at[:, gy], along_y, 1), 0)
        copy = pltpu.make_async_copy(mid.at[:, gy], got.at[:, gy], own.at[1])
        copy.start()
        return copy

    clear_rims((w0, w1, w2))
    keep = levels()

    def advance(src, dst):
        def body(y, r):
            for c, v in enumerate(step_block(src, y, r)):
                dst[c, y, pl.ds(r, 8), :] = jnp.where(keep, v, 0.0)
        return body

    cells = table.reshape(CX * CY * TILE, LANES)

    def tables(y, r):
        at = ((y - 1) * CX + (r - TOP)) * TILE
        spare = w1[2, y, pl.ds(r, 8), :]
        for c, v in enumerate(step_block(w2, y, r)):
            cells[pl.ds(at + c, 8, stride=TILE), :] = jnp.where(keep, v, pltpu.roll(spare, NZ - 32 * c, 1))
            cells[pl.ds(at + 3 + c, 8, stride=TILE), :] = w2[c, y, pl.ds(r, 8), :]
            if c < 2:
                cells[pl.ds(at + 6 + c, 8, stride=TILE), :] = w1[c, y, pl.ds(r, 8), :]

    def target(dst, s, c, y):
        if dst is not None:
            return layer_at(dst, s, 0, c, y)
        if s < 2:
            return cells, (pl.ds((y * CX + (CX - 1) * s) * TILE + c, 8, stride=CX * TILE), slice(None))
        return cells, (pl.ds(((CY - 1) * (s - 2) * CX + y) * TILE + c, 8, stride=TILE), slice(None))

    inside = inside_grid(*where)

    def meet_rims(src, dst, n):
        for s in range(4):
            factors = []
            for y in range(0, CY, 8):
                ref, at = layer_at(src, s, 0, s // 2, y)
                factors.append(HALF * (1.0 - ref[at]) if s % 2 else HALF * (1.0 + ref[at]))
            for c in range(3):
                for i, v in enumerate(rim_rows(inbox.at[n], OPPOSITE[s], c, inside[s])):
                    ref, at = layer_at(src, s, 1, c, 8 * i)
                    ref[at] = v
                    ref, at = target(dst, s, c, 8 * i)
                    ref[at] = ref[at] + factors[i] * v

    for n, (src, dst, body) in enumerate(((w0, w1, advance(w0, w1)), (w1, w2, advance(w1, w2)), (w2, None, tables))):
        if n:
            pack_rims(src, sides.at[n])
            copies = send_rims(sides.at[n], inbox.at[n], send.at[n], recv.at[n], *where)
        if n == 1:
            last = forward_lists()
        over_tile(body)
        for copy in copies:
            copy.wait()
        meet_rims(src, dst, n)

    last.wait()
    rest = pl.ds(0, n_gy - 1)
    settle(mid.at[:, rest], got.at[:, rest], along_y, 1)
    g0 = got[:, :, 0, :].reshape(LANES, LANES)
    g1 = got[:, :, 1, :].reshape(LANES, LANES)
    where_to = regroup(g0, 0).astype(jnp.int32)
    x = ((where_to >> 10) * 171) >> 9
    rem = where_to - x * (CY * NZ)
    y = ((rem >> 5) * 171) >> 9
    z = rem - y * NZ
    lane = lax.broadcasted_iota(jnp.int32, (32, LANES), 1)
    at = (y * CX + x) * LANES
    take[...] = at + ((lane - z) & (LANES - 1))
    give[...] = at * TILE + ((z - lane) & (LANES - 1))
    third[...] = (z >> 5).astype(jnp.float32)
    for j in range(4):
        slots[j] = regroup(g1, j)
    for n in range(STEPS):
        seen_obs[n] = regroup(g0, 1 + n)


def forward(state, lists):
    box = pltpu.VMEM((lax.axis_size("gx"), lax.axis_size("gy"), 2, LANES), jnp.float32)
    wide, table = f32(3, WIDE, ROWS, LANES), f32(CX * CY, TILE, LANES)
    codes = jax.ShapeDtypeStruct((32, LANES), jnp.int32)
    rim = pltpu.VMEM((STEPS, 4, 3, 24, LANES), jnp.float32)
    return pl.pallas_call(
        forward_kernel,
        out_shape=[
            wide, wide, wide, table, codes, codes, f32(32, LANES), f32(4, 32, LANES), f32(STEPS, 32, LANES),
        ],
        in_specs=[VMEM] * 2,
        out_specs=[VMEM] * 9,
        scratch_shapes=[
            box, box, box, rim, rim,
            pltpu.SemaphoreType.DMA((STEPS, 4)), pltpu.SemaphoreType.DMA((STEPS, 4)),
            pltpu.SemaphoreType.DMA((2,)), pltpu.SemaphoreType.DMA((2,)), pltpu.SemaphoreType.DMA((2,)),
        ],
        compiler_params=pltpu.CompilerParams(collective_id=0, has_side_effects=True, vmem_limit_bytes=24 * MIB),
        name="forward",
    )(state, lists)


def spare_lanes():
    lane = lax.broadcasted_iota(jnp.int32, (8, LANES), 1)
    row = lax.broadcasted_iota(jnp.int32, (8, LANES), 0)
    return jnp.where(row < 3, (lane + 32 * (row + 1)) & (LANES - 1), -1)


def same_list():
    a = lax.broadcasted_iota(jnp.int32, (LANES, LANES), 0) >> 5
    b = lax.broadcasted_iota(jnp.int32, (LANES, LANES), 1) >> 5
    return (a == b).astype(jnp.float32)


def diagonal():
    g = lax.broadcasted_iota(jnp.int32, (32, LANES), 0)
    lane = lax.broadcasted_iota(jnp.int32, (32, LANES), 1)
    return (lane & 31) == g


def list_sums(values):
    return jnp.dot(
        jnp.concatenate(values, axis=0), same_list(), precision=lax.Precision.HIGHEST,
        preferred_element_type=jnp.float32,
    )


def gather_kernel(
    take, table, third, slots, seen_obs,
    vals_a, vals_b, *rest,
):
    empty = rest[:COPIES]
    gather_body(take, table, third, slots, seen_obs, vals_a, vals_b, empty, *rest[COPIES:])


def gather_body(
    take, table, third, slots, seen_obs, vals_a, vals_b, empty,
    acc_a, acc_b, resid, part, half, inbox_a, inbox_b, send_a, recv_a, send_b, recv_b,
):
    gx, gy = lax.axis_index("gx"), lax.axis_index("gy")
    q = (gx // 4) * 4 + lax.rem(gy, 4)
    p = lax.rem(gx, 4) * 4 + gy // 4

    def near(d):
        to = lax.rem(q + d, 8)
        return ((to // 4) * 4 + lax.rem(gx, 4), (gy // 4) * 4 + lax.rem(to, 4))

    def far(d):
        to = lax.rem(p + d, 16)
        return ((gx // 4) * 4 + to // 4, lax.rem(to, 4) * 4 + lax.rem(gy, 4))

    barrier = pltpu.get_barrier_semaphore()
    for d in range(1, 8):
        pl.semaphore_signal(barrier, inc=1, device_id=near(d), device_id_type=MESH)
    for d in range(1, 16):
        pl.semaphore_signal(barrier, inc=1, device_id=far(d), device_id_type=MESH)

    vals_a[...] = jnp.zeros_like(vals_a)
    vals_b[...] = jnp.zeros_like(vals_b)

    lane8 = lax.broadcasted_iota(jnp.int32, (8, LANES), 1)
    spare = spare_lanes()

    def pick(g, carry):
        a = jnp.zeros((8, LANES), jnp.float32)
        b = jnp.zeros((8, LANES), jnp.float32)
        for j in range(LANES):
            code = take[g, j]
            tile = pltpu.roll(table[code >> 7], code & (LANES - 1), 1)
            a = jnp.where(lane8 == j, tile, a)
            b = jnp.where(spare == j, tile, b)
        at = pl.multiple_of(g * 8, 8)
        acc_a[pl.ds(at, 8), :] = a
        acc_b[pl.ds(at, 8), :] = b
        return carry

    lax.fori_loop(0, 32, pick, 0, unroll=4)

    diag = diagonal()
    beam = slots[0]
    values = []
    for n in range(STEPS):
        base = (6, 3, 0)[n]
        got = [acc_a[pl.ds(base + c, 32, stride=8), :] for c in range(3 if n else 2)]
        if n == 0:
            ninth = jnp.zeros((32, LANES), jnp.float32)
            for k in range(3):
                piece = pltpu.roll(acc_b[pl.ds(k, 32, stride=8), :], 32 * (k + 1), 1)
                ninth = jnp.where(third[...] == float(k), piece, ninth)
            got.append(ninth)
        seen = sum(slots[1 + c] * got[c] for c in range(3))
        r = seen - seen_obs[n]
        resid[n] = r
        for b in range(BEAMS):
            values.append(jnp.where(beam == float(b), r, 0.0))
    sums = list_sums(values)
    for i in range(STEPS * BEAMS):
        block = jnp.where(diag, sums[32 * i : 32 * i + 32, :], 0.0)
        part[i // BEAMS, pl.ds(i % BEAMS, 1), :] = jnp.sum(block, axis=0, keepdims=True)
    pl.semaphore_wait(barrier, 22)

    blank = jnp.zeros((64, LANES), jnp.float32)

    def clear(i, carry):
        for ref in empty:
            ref[pl.ds(pl.multiple_of(i * 64, 64), 64), :] = blank
        return carry

    half_way = CX * CY * TILE // 128

    def spread(src, inbox, send, recv, where_to, peers, first):
        copies = []
        for d in range(1, peers):
            copy = pltpu.make_async_remote_copy(
                src_ref=src, dst_ref=inbox.at[d - 1], send_sem=send.at[d - 1], recv_sem=recv.at[d - 1],
                device_id=where_to(d), device_id_type=MESH,
            )
            copy.start()
            copies.append(copy)
        lax.fori_loop(first, first + half_way, clear, 0)
        for copy in copies:
            copy.wait()

    spread(part, inbox_a, send_a, recv_a, near, 8, 0)
    acc = part[...]
    for d in range(7):
        acc = acc + inbox_a[d]
    half[...] = acc
    spread(half, inbox_b, send_b, recv_b, far, 16, half_way)
    for d in range(15):
        acc = acc + inbox_b[d]

    total = acc * (1.0 / GATES)
    means = list_sums([jnp.where(diag, total[i // BEAMS, i % BEAMS : i % BEAMS + 1, :], 0.0) for i in range(STEPS * BEAMS)])
    for n in range(STEPS):
        at = 32 * BEAMS * n
        mean = jnp.zeros((32, LANES), jnp.float32)
        for b in range(BEAMS):
            mean = jnp.where(beam == float(b), means[at + 32 * b : at + 32 * b + 32, :], mean)
        misfit = jnp.where(beam >= 0.0, resid[n] - mean, 0.0)
        base = (6, 3, 0)[n]
        for c in range(3):
            if base + c < 8:
                vals_a[pl.ds(base + c, 32, stride=8), :] = slots[1 + c] * misfit
                continue
            for k in range(3):
                piece = jnp.where(third[...] == float(k), slots[1 + c] * misfit, 0.0)
                vals_b[pl.ds(k, 32, stride=8), :] = pltpu.roll(piece, NZ - 32 * k, 1)


def gather(take, table, third, slots, seen_obs):
    rows = pltpu.VMEM((256, LANES), jnp.float32)
    block = pltpu.VMEM((STEPS, BEAMS, LANES), jnp.float32)
    return pl.pallas_call(
        gather_kernel,
        out_shape=[f32(256, LANES), f32(256, LANES)] + [f32(CX * CY * TILE, LANES)] * COPIES,
        in_specs=[SMEM] + [VMEM] * 4,
        out_specs=[VMEM] * (2 + COPIES),
        scratch_shapes=[
            rows, rows, pltpu.VMEM((STEPS, 32, LANES), jnp.float32), block, block,
            pltpu.VMEM((7, STEPS, BEAMS, LANES), jnp.float32), pltpu.VMEM((15, STEPS, BEAMS, LANES), jnp.float32),
            pltpu.SemaphoreType.DMA((7,)), pltpu.SemaphoreType.DMA((7,)),
            pltpu.SemaphoreType.DMA((15,)), pltpu.SemaphoreType.DMA((15,)),
        ],
        compiler_params=pltpu.CompilerParams(collective_id=1, has_side_effects=True, vmem_limit_bytes=16 * MIB),
        name="gather",
    )(take, table, third, slots, seen_obs)


def scatter_kernel(give, vals_a, vals_b, *rest):
    f3, f2, f1 = rest[COPIES : COPIES + 3]
    sums = rest[COPIES + 3 : -1]
    layer = rest[-1]
    lane8 = lax.broadcasted_iota(jnp.int32, (8, LANES), 1)
    spare = spare_lanes()

    def place(g, carry):
        at = pl.multiple_of(g * 8, 8)
        va = vals_a[pl.ds(at, 8), :]
        vb = vals_b[pl.ds(at, 8), :]
        for j in range(LANES):
            code = give[g, j]
            to = pl.ds(pl.multiple_of(code >> 7, TILE), TILE)
            v = jnp.where(lane8 == j, va, jnp.where(spare == j, vb, 0.0))
            out = sums[j % COPIES]
            out[to, :] = out[to, :] + pltpu.roll(v, code & (LANES - 1), 1)
        return carry

    lax.fori_loop(0, 32, place, 0, unroll=4)
    keep = lane8 < NZ

    def unpack(y, carry):
        first = pl.multiple_of(y * CX * TILE, CX * TILE)
        for x in range(CX):
            at = pl.ds(first + x * TILE, TILE)
            layer[pl.ds(x * TILE, TILE), :] = sum(ref[at, :] for ref in sums)
        for r in range(0, CX, 8):
            rows = [layer[pl.ds(r * TILE + k, 8, stride=TILE), :] for k in range(8)]
            pieces = [pltpu.roll(rows[k], 32 * (k + 1), 1) for k in range(3)]
            ninth = jnp.where(lane8 < 32, pieces[0], jnp.where(lane8 < 64, pieces[1], pieces[2]))
            rows = [jnp.where(keep, v, 0.0) for v in rows[:3]] + rows[3:] + [jnp.where(keep, ninth, 0.0)]
            for i, out in enumerate((f3, f2, f1)):
                for c in range(3):
                    out[c, y, pl.ds(r, 8), :] = rows[3 * i + c]
        return carry

    lax.fori_loop(0, CY, unpack, 0, unroll=4)


def scatter(give, vals_a, vals_b, empty):
    table = f32(CX * CY * TILE, LANES)
    field = f32(3, CY, CX, LANES)
    return pl.pallas_call(
        scatter_kernel,
        out_shape=[field, field, field] + [table] * COPIES,
        in_specs=[SMEM] + [VMEM] * (2 + COPIES),
        out_specs=[VMEM] * (3 + COPIES),
        scratch_shapes=[pltpu.VMEM((CX * TILE, LANES), jnp.float32)],
        input_output_aliases={3 + i: 3 + i for i in range(COPIES)},
        compiler_params=pltpu.CompilerParams(vmem_limit_bytes=16 * MIB),
        name="scatter",
    )(give, vals_a, vals_b, *empty)[:3]


def adjoint_kernel(w0, w1, w2, f3, f2, f1, out, a3, a2, a1, sides, inbox, send, recv):
    n_gx, n_gy, gx, gy = sizes()
    where = (n_gx, n_gy, gx, gy)
    barrier = pltpu.get_barrier_semaphore()
    for target in (
        (lax.rem(gx + n_gx - 1, n_gx), gy), (lax.rem(gx + 1, n_gx), gy),
        (gx, lax.rem(gy + n_gy - 1, n_gy)), (gx, lax.rem(gy + 1, n_gy)),
    ):
        pl.semaphore_signal(barrier, inc=1, device_id=target, device_id_type=MESH)

    def fill(y, carry):
        for c in range(3):
            a3[c, y + 1, pl.ds(TOP, CX), :] = f3[c, y]
        return carry

    lax.fori_loop(0, CY, fill, 0)
    keep = levels()
    inside = inside_grid(*where)

    def meet_rims(src, dst, n):
        for s in range(4):
            factors = []
            for y in range(0, CY, 8):
                ref, at = layer_at(src, s, 1, s // 2, y)
                factors.append(HALF * (1.0 + ref[at]) if s % 2 else HALF * (1.0 - ref[at]))
            for c in range(3):
                for i, v in enumerate(rim_rows(inbox.at[n], OPPOSITE[s], c, inside[s])):
                    ref, at = layer_at(dst, s, 0, c, 8 * i)
                    ref[at] = ref[at] + factors[i] * v

    def pull(src, adj, dst, force):
        def body(y, r):
            for c, v in enumerate(pull_block(src, adj, y, r)):
                v = jnp.where(keep, v, 0.0)
                if force is not None:
                    v = v + force[c, y - 1, pl.ds(r - TOP, 8), :]
                dst[c, y, pl.ds(r, 8), :] = v
        return body

    for n, (src, adj, dst, force) in enumerate(((w2, a3, a2, f2), (w1, a2, a1, f1), (w0, a1, a3, None))):
        body = pull(src, adj, dst, force)
        pack_rims(adj, sides.at[n])
        if n == 0:
            pl.semaphore_wait(barrier, 4)
        copies = send_rims(sides.at[n], inbox.at[n], send.at[n], recv.at[n], *where)
        if n == 0:
            clear_rims((a3, a2, a1))
        over_tile(body)
        for copy in copies:
            copy.wait()
        meet_rims(src, dst, n)

    lane = lax.broadcasted_iota(jnp.int32, (CX, LANES), 1)
    for c in range(3):
        for y in range(0, CY, 4):
            v = [a3[c, y + 1 + i, pl.ds(TOP, CX), :] for i in range(4)]
            v = [v[0], pltpu.roll(v[1], 96, 1), pltpu.roll(v[2], 64, 1), pltpu.roll(v[3], 32, 1)]
            t = [
                jnp.where(lane < 96, v[0], v[1]),
                jnp.where(lane < 64, v[1], v[2]),
                jnp.where(lane < 32, v[2], v[3]),
            ]
            for i in range(3):
                out[c, :, pl.ds(y * NZ + LANES * i, LANES)] = t[i]


def adjoint(wides, fields):
    wide = pltpu.VMEM((3, WIDE, ROWS, LANES), jnp.float32)
    rim = pltpu.VMEM((STEPS, 4, 3, 24, LANES), jnp.float32)
    return pl.pallas_call(
        adjoint_kernel,
        out_shape=f32(3, CX, CY * NZ),
        in_specs=[VMEM] * 6,
        out_specs=VMEM,
        scratch_shapes=[wide] * 3 + [
            rim, rim, pltpu.SemaphoreType.DMA((STEPS, 4)), pltpu.SemaphoreType.DMA((STEPS, 4)),
        ],
        compiler_params=pltpu.CompilerParams(collective_id=2, has_side_effects=True, vmem_limit_bytes=24 * MIB),
        name="adjoint",
    )(*wides, *fields)


def local(initial_state, beam_dir, gate_obs, slot_beam, slot_cell):
    count = slot_cell.shape[1]
    capacity = slot_cell.shape[2]
    rows = 5 * capacity + 8

    def at_row(block, first):
        return jnp.pad(block, ((first, rows - first - block.shape[0]), (0, count - block.shape[1])))

    lists = (
        (at_row(slot_cell[0].T, 0) + at_row(slot_beam[0].T, 4 * capacity)).astype(jnp.float32)
        + at_row(jnp.transpose(gate_obs[:, 0], (0, 2, 1)).reshape(-1, count), capacity)
        + at_row(beam_dir, 5 * capacity)
    )
    w0, w1, w2, table, take, give, third, slots, seen_obs = forward(initial_state, lists)
    vals_a, vals_b, *empty = gather(take, table, third, slots, seen_obs)
    fields = scatter(give, vals_a, vals_b, empty)
    return adjoint((w0, w1, w2), fields)


def solution(mesh):
    in_specs = (
        P(None, "gx", "gy"),
        P(None, ("gx", "gy")),
        P(None, ("gx", "gy"), None, None),
        P(("gx", "gy"), None, None),
        P(("gx", "gy"), None, None),
    )
    out_specs = P(None, "gx", "gy")
    return jax.shard_map(local, mesh=mesh, in_specs=in_specs, out_specs=out_specs, check_vma=False)
```

```python
import jax
import jax.numpy as jnp
from jax import lax
from jax.experimental import pallas as pl
from jax.experimental.pallas import tpu as pltpu
from jax.sharding import PartitionSpec as P

NZ = 96
LANES = 128
GATES = 512
BEAMS = 4
STEPS = 3
TIME_STEP = 0.2
VISCOSITY = 0.5
HALF = 0.5 * TIME_STEP
CX = 32
CY = 32
TOP = 8
ROWS = CX + 2 * TOP
WIDE = CY + 2
COPIES = 4
TILE = 8
UNROLL = 4
MIB = 1024 * 1024
MESH = pl.DeviceIdType.MESH
VMEM = pl.BlockSpec(memory_space=pltpu.VMEM)
SMEM = pl.BlockSpec(memory_space=pltpu.SMEM)


def f32(*shape):
    return jax.ShapeDtypeStruct(shape, jnp.float32)


def sizes():
    return lax.axis_size("gx"), lax.axis_size("gy"), lax.axis_index("gx"), lax.axis_index("gy")


def shift_up(v):
    return pltpu.roll(v, LANES - 1, 1)


def shift_down(v):
    return pltpu.roll(v, 1, 1)


def levels():
    return lax.broadcasted_iota(jnp.int32, (8, LANES), 1) < NZ


def step_block(src, y, r):
    rows, fore, back = pl.ds(r, 8), pl.ds(r + 1, 8), pl.ds(r - 1, 8)
    centre = [src[c, y, rows, :] for c in range(3)]
    less = [1.0 - v for v in centre]
    more = [1.0 + v for v in centre]
    out = []
    for c in range(3):
        v = centre[c]
        total = src[c, y, fore, :] * less[0] + src[c, y, back, :] * more[0]
        total += src[c, y + 1, rows, :] * less[1] + src[c, y - 1, rows, :] * more[1]
        total += shift_up(v) * less[2] + shift_down(v) * more[2]
        out.append((1.0 - 6.0 * HALF) * v + HALF * total)
    return out


def pull_block(src, adj, y, r):
    rows, fore, back = pl.ds(r, 8), pl.ds(r + 1, 8), pl.ds(r - 1, 8)
    near = []
    for c in range(3):
        v = src[c, y, rows, :]
        near.append((src[c, y, fore, :], src[c, y, back, :], src[c, y + 1, rows, :], src[c, y - 1, rows, :],
                     shift_up(v), shift_down(v)))
    factors = [1.0 + near[0][0], 1.0 - near[0][1], 1.0 + near[1][2], 1.0 - near[1][3],
               1.0 + near[2][4], 1.0 - near[2][5]]
    a = [adj[c, y, rows, :] for c in range(3)]
    out = []
    for c in range(3):
        total = adj[c, y, fore, :] * factors[0] + adj[c, y, back, :] * factors[1]
        total += adj[c, y + 1, rows, :] * factors[2] + adj[c, y - 1, rows, :] * factors[3]
        total += shift_up(a[c]) * factors[4] + shift_down(a[c]) * factors[5]
        for k in range(3):
            total -= a[k] * (near[k][2 * c] - near[k][2 * c + 1])
        out.append((1.0 - 6.0 * HALF) * a[c] + HALF * total)
    return out


def send_rims(sides, inbox, send, recv, n_gx, n_gy, gx, gy):
    targets = (
        (lax.rem(gx + n_gx - 1, n_gx), gy), (lax.rem(gx + 1, n_gx), gy),
        (gx, lax.rem(gy + n_gy - 1, n_gy)), (gx, lax.rem(gy + 1, n_gy)),
    )
    copies = []
    for s in (2, 3, 0, 1):
        target = targets[s]
        copy = pltpu.make_async_remote_copy(
            src_ref=sides.at[s], dst_ref=inbox.at[s], send_sem=send.at[s], recv_sem=recv.at[s],
            device_id=target, device_id_type=MESH,
        )
        copy.start()
        copies.append(copy)
    return copies


def over_tile(body):
    def layer(y, carry):
        for r in range(TOP, TOP + CX, 8):
            body(y, r)
        return carry

    lax.fori_loop(1, CY + 1, layer, 0, unroll=UNROLL)


def clear_rims(fields):
    blank = jnp.zeros((8, LANES), jnp.float32)

    def layer(y, carry):
        for field in fields:
            for c in range(3):
                field[c, y, pl.ds(0, 8), :] = blank
                field[c, y, pl.ds(TOP + CX, 8), :] = blank
        return carry

    lax.fori_loop(1, CY + 1, layer, 0)
    for field in fields:
        for c in range(3):
            for y in (0, CY + 1):
                for r in range(TOP, TOP + CX, 8):
                    field[c, y, pl.ds(r, 8), :] = blank


def layer_at(field, side, depth, c, y):
    if side < 2:
        row = TOP - depth if side == 0 else TOP + CX - 1 + depth
        return field.reshape(3, WIDE * ROWS, LANES), (c, pl.ds((y + 1) * ROWS + row, 8, stride=ROWS), slice(None))
    return field, (c, 1 - depth if side == 2 else CY + depth, pl.ds(TOP + y, 8), slice(None))


OPPOSITE = (1, 0, 3, 2)


def inside_grid(n_gx, n_gy, gx, gy):
    return (gx > 0, gx < n_gx - 1, gy > 0, gy < n_gy - 1)


def pack_rims(field, sides):
    keep = levels()
    for s in range(4):
        for c in range(3):
            v = []
            for y in range(0, CY, 8):
                ref, at = layer_at(field, s, 0, c, y)
                v.append(ref[at])
            for k in range(3):
                sides[s, c, pl.ds(8 * k, 8), :] = jnp.where(keep, v[k], pltpu.roll(v[3], NZ - 32 * k, 1))


def rim_rows(inbox, side, c, inside):
    lane = lax.broadcasted_iota(jnp.int32, (8, LANES), 1)
    p = [inbox[side, c, pl.ds(8 * k, 8), :] for k in range(3)]
    q = [pltpu.roll(p[k], 32 * (k + 1), 1) for k in range(3)]
    p.append(jnp.where(lane < 32, q[0], jnp.where(lane < 64, q[1], q[2])))
    return [jnp.where((lane < NZ) & inside, v, 0.0) for v in p]


def regroup(block, quantity):
    lane = lax.broadcasted_iota(jnp.int32, (32, LANES), 1)
    out = None
    for k in range(4):
        piece = block[32 * k : 32 * k + 32, :]
        turn = (32 * (k - quantity)) % LANES
        if turn:
            piece = pltpu.roll(piece, turn, 1)
        out = piece if out is None else jnp.where(lane >= 32 * k, piece, out)
    return out


def forward_kernel(
    state_in, cell_in, obs_in, beam_in, dir_in,
    w0, w1, w2, table, take, give, third, slots, seen_obs,
    state, cell, obs, beam, beam_dir, load, got, mid, msg, sides, inbox, send, recv, list_send, list_recv, own,
):
    n_gx, n_gy, gx, gy = sizes()
    barrier = pltpu.get_barrier_semaphore()
    loads = []
    pairs = ((state_in, state), (cell_in, cell), (obs_in, obs), (beam_in, beam), (dir_in, beam_dir))
    for i, (src, dst) in enumerate(pairs):
        loads.append(pltpu.make_async_copy(src, dst, load.at[i]))
        loads[-1].start()

    def along_x(i):
        to = lax.rem(gx + i, n_gx)
        return to, (to, gy)

    def along_y(i):
        to = lax.rem(gy + i, n_gy)
        return to, (gx, to)

    def hail(line):
        def body(i, carry):
            pl.semaphore_signal(barrier, inc=1, device_id=line(i)[1], device_id_type=MESH)
            return carry
        return body

    lax.fori_loop(1, n_gx, hail(along_x), 0)
    lax.fori_loop(1, n_gy, hail(along_y), 0)
    for copy in loads:
        copy.wait()
    lane = lax.broadcasted_iota(jnp.int32, (CX, LANES), 1)
    for c in range(3):
        for y in range(0, CY, 4):
            t = [state[c, :, pl.ds(y * NZ + LANES * i, LANES)] for i in range(3)]
            planes = [
                t[0],
                pltpu.roll(jnp.where(lane >= 96, t[0], t[1]), 32, 1),
                pltpu.roll(jnp.where(lane >= 64, t[1], t[2]), 64, 1),
                pltpu.roll(t[2], 96, 1),
            ]
            for i, v in enumerate(planes):
                w0[c, y + 1 + i, pl.ds(TOP, CX), :] = jnp.where(lane < NZ, v, 0.0)
    pack_rims(w0, sides.at[0])
    pl.semaphore_wait(barrier, n_gx + n_gy - 2)

    where = (n_gx, n_gy, gx, gy)
    copies = send_rims(sides.at[0], inbox.at[0], send.at[0], recv.at[0], *where)
    kind = beam[...]
    heads = [cell[...].astype(jnp.float32), obs[0], obs[1], obs[2]]
    tails = [kind.astype(jnp.float32)]
    for c in range(3):
        weight = jnp.zeros(kind.shape, jnp.float32)
        for b in range(BEAMS):
            weight = jnp.where(kind == b, beam_dir[c, b], weight)
        tails.append(weight)
    msg[:, :, 0, :] = jnp.concatenate(heads, axis=0).T.reshape(n_gx, n_gy, LANES)
    msg[:, :, 1, :] = jnp.concatenate(tails, axis=0).T.reshape(n_gx, n_gy, LANES)


    def post(src, dst, line, sems):
        def body(i, carry):
            to, target = line(i)
            pltpu.make_async_remote_copy(
                src_ref=src(to), dst_ref=dst, send_sem=list_send.at[sems], recv_sem=list_recv.at[sems],
                device_id=target, device_id_type=MESH,
            ).start()
            return carry
        return body

    def settle(src, dst, line, sems):
        pltpu.make_async_remote_copy(
            src_ref=src, dst_ref=dst, send_sem=list_send.at[sems], recv_sem=list_recv.at[sems],
            device_id=line(1)[1], device_id_type=MESH,
        ).wait()

    lax.fori_loop(1, n_gx, post(lambda to: msg.at[to], mid.at[gx], along_x, 0), 0)
    mine = pltpu.make_async_copy(msg.at[gx], mid.at[gx], own.at[0])
    mine.start()

    def forward_lists():
        mine.wait()
        rest = pl.ds(0, n_gx - 1)
        settle(msg.at[rest], mid.at[rest], along_x, 0)
        lax.fori_loop(1, n_gy, post(lambda to: mid.at[:, to], got.at[:, gy], along_y, 1), 0)
        copy = pltpu.make_async_copy(mid.at[:, gy], got.at[:, gy], own.at[1])
        copy.start()
        return copy

    clear_rims((w0, w1, w2))
    keep = levels()

    def advance(src, dst):
        def body(y, r):
            for c, v in enumerate(step_block(src, y, r)):
                dst[c, y, pl.ds(r, 8), :] = jnp.where(keep, v, 0.0)
        return body

    cells = table.reshape(CX * CY * TILE, LANES)

    def tables(y, r):
        at = ((y - 1) * CX + (r - TOP)) * TILE
        spare = w1[2, y, pl.ds(r, 8), :]
        for c, v in enumerate(step_block(w2, y, r)):
            cells[pl.ds(at + c, 8, stride=TILE), :] = jnp.where(keep, v, pltpu.roll(spare, NZ - 32 * c, 1))
            cells[pl.ds(at + 3 + c, 8, stride=TILE), :] = w2[c, y, pl.ds(r, 8), :]
            if c < 2:
                cells[pl.ds(at + 6 + c, 8, stride=TILE), :] = w1[c, y, pl.ds(r, 8), :]

    def target(dst, s, c, y):
        if dst is not None:
            return layer_at(dst, s, 0, c, y)
        if s < 2:
            return cells, (pl.ds((y * CX + (CX - 1) * s) * TILE + c, 8, stride=CX * TILE), slice(None))
        return cells, (pl.ds(((CY - 1) * (s - 2) * CX + y) * TILE + c, 8, stride=TILE), slice(None))

    inside = inside_grid(*where)

    def meet_rims(src, dst, n):
        for s in range(4):
            factors = []
            for y in range(0, CY, 8):
                ref, at = layer_at(src, s, 0, s // 2, y)
                factors.append(HALF * (1.0 - ref[at]) if s % 2 else HALF * (1.0 + ref[at]))
            for c in range(3):
                for i, v in enumerate(rim_rows(inbox.at[n], OPPOSITE[s], c, inside[s])):
                    ref, at = layer_at(src, s, 1, c, 8 * i)
                    ref[at] = v
                    ref, at = target(dst, s, c, 8 * i)
                    ref[at] = ref[at] + factors[i] * v

    for n, (src, dst, body) in enumerate(((w0, w1, advance(w0, w1)), (w1, w2, advance(w1, w2)), (w2, None, tables))):
        if n:
            pack_rims(src, sides.at[n])
            copies = send_rims(sides.at[n], inbox.at[n], send.at[n], recv.at[n], *where)
        if n == 1:
            last = forward_lists()
        over_tile(body)
        for copy in copies:
            copy.wait()
        meet_rims(src, dst, n)

    last.wait()
    rest = pl.ds(0, n_gy - 1)
    settle(mid.at[:, rest], got.at[:, rest], along_y, 1)
    g0 = got[:, :, 0, :].reshape(LANES, LANES)
    g1 = got[:, :, 1, :].reshape(LANES, LANES)
    where_to = regroup(g0, 0).astype(jnp.int32)
    x = ((where_to >> 10) * 171) >> 9
    rem = where_to - x * (CY * NZ)
    y = ((rem >> 5) * 171) >> 9
    z = rem - y * NZ
    lane = lax.broadcasted_iota(jnp.int32, (32, LANES), 1)
    at = (y * CX + x) * LANES
    take[...] = at + ((lane - z) & (LANES - 1))
    give[...] = at * TILE + ((z - lane) & (LANES - 1))
    third[...] = (z >> 5).astype(jnp.float32)
    for j in range(4):
        slots[j] = regroup(g1, j)
    for n in range(STEPS):
        seen_obs[n] = regroup(g0, 1 + n)


def forward(*inputs):
    box = pltpu.VMEM((lax.axis_size("gx"), lax.axis_size("gy"), 2, LANES), jnp.float32)
    wide, table = f32(3, WIDE, ROWS, LANES), f32(CX * CY, TILE, LANES)
    codes = jax.ShapeDtypeStruct((32, LANES), jnp.int32)
    rim = pltpu.VMEM((STEPS, 4, 3, 24, LANES), jnp.float32)
    return pl.pallas_call(
        forward_kernel,
        out_shape=[
            wide, wide, wide, table, codes, codes, f32(32, LANES), f32(4, 32, LANES), f32(STEPS, 32, LANES),
        ],
        in_specs=[pl.BlockSpec(memory_space=pltpu.HBM)] * 5,
        out_specs=[VMEM] * 9,
        scratch_shapes=[
            *[pltpu.VMEM(v.shape, v.dtype) for v in inputs[:4]], pltpu.SMEM(inputs[4].shape, jnp.float32),
            pltpu.SemaphoreType.DMA((5,)),
            box, box, box, rim, rim,
            pltpu.SemaphoreType.DMA((STEPS, 4)), pltpu.SemaphoreType.DMA((STEPS, 4)),
            pltpu.SemaphoreType.DMA((2,)), pltpu.SemaphoreType.DMA((2,)), pltpu.SemaphoreType.DMA((2,)),
        ],
        compiler_params=pltpu.CompilerParams(collective_id=0, has_side_effects=True, vmem_limit_bytes=24 * MIB),
        name="forward",
    )(*[pltpu.with_memory_space_constraint(v, pltpu.HBM) for v in inputs])


def spare_lanes():
    lane = lax.broadcasted_iota(jnp.int32, (8, LANES), 1)
    row = lax.broadcasted_iota(jnp.int32, (8, LANES), 0)
    return jnp.where(row < 3, (lane + 32 * (row + 1)) & (LANES - 1), -1)


def same_list():
    a = lax.broadcasted_iota(jnp.int32, (LANES, LANES), 0) >> 5
    b = lax.broadcasted_iota(jnp.int32, (LANES, LANES), 1) >> 5
    return (a == b).astype(jnp.float32)


def diagonal():
    g = lax.broadcasted_iota(jnp.int32, (32, LANES), 0)
    lane = lax.broadcasted_iota(jnp.int32, (32, LANES), 1)
    return (lane & 31) == g


def list_sums(values):
    return jnp.dot(
        jnp.concatenate(values, axis=0), same_list(), precision=lax.Precision.HIGHEST,
        preferred_element_type=jnp.float32,
    )


def gather_kernel(
    take, table, third, slots, seen_obs,
    vals_a, vals_b, *rest,
):
    empty = rest[:COPIES]
    gather_body(take, table, third, slots, seen_obs, vals_a, vals_b, empty, *rest[COPIES:])


def gather_body(
    take, table, third, slots, seen_obs, vals_a, vals_b, empty,
    acc_a, acc_b, resid, part, half, inbox_a, inbox_b, send_a, recv_a, send_b, recv_b,
):
    gx, gy = lax.axis_index("gx"), lax.axis_index("gy")
    q = (gx // 4) * 4 + lax.rem(gy, 4)
    p = lax.rem(gx, 4) * 4 + gy // 4

    def near(d):
        to = lax.rem(q + d, 8)
        return ((to // 4) * 4 + lax.rem(gx, 4), (gy // 4) * 4 + lax.rem(to, 4))

    def far(d):
        to = lax.rem(p + d, 16)
        return ((gx // 4) * 4 + to // 4, lax.rem(to, 4) * 4 + lax.rem(gy, 4))

    barrier = pltpu.get_barrier_semaphore()
    for d in range(1, 8):
        pl.semaphore_signal(barrier, inc=1, device_id=near(d), device_id_type=MESH)
    for d in range(1, 16):
        pl.semaphore_signal(barrier, inc=1, device_id=far(d), device_id_type=MESH)

    vals_a[...] = jnp.zeros_like(vals_a)
    vals_b[...] = jnp.zeros_like(vals_b)

    lane8 = lax.broadcasted_iota(jnp.int32, (8, LANES), 1)
    spare = spare_lanes()

    def pick(g, carry):
        a = jnp.zeros((8, LANES), jnp.float32)
        b = jnp.zeros((8, LANES), jnp.float32)
        for j in range(LANES):
            code = take[g, j]
            tile = pltpu.roll(table[code >> 7], code & (LANES - 1), 1)
            a = jnp.where(lane8 == j, tile, a)
            b = jnp.where(spare == j, tile, b)
        at = pl.multiple_of(g * 8, 8)
        acc_a[pl.ds(at, 8), :] = a
        acc_b[pl.ds(at, 8), :] = b
        return carry

    lax.fori_loop(0, 32, pick, 0, unroll=4)

    diag = diagonal()
    beam = slots[0]
    values = []
    for n in range(STEPS):
        base = (6, 3, 0)[n]
        got = [acc_a[pl.ds(base + c, 32, stride=8), :] for c in range(3 if n else 2)]
        if n == 0:
            ninth = jnp.zeros((32, LANES), jnp.float32)
            for k in range(3):
                piece = pltpu.roll(acc_b[pl.ds(k, 32, stride=8), :], 32 * (k + 1), 1)
                ninth = jnp.where(third[...] == float(k), piece, ninth)
            got.append(ninth)
        seen = sum(slots[1 + c] * got[c] for c in range(3))
        r = seen - seen_obs[n]
        resid[n] = r
        for b in range(BEAMS):
            values.append(jnp.where(beam == float(b), r, 0.0))
    sums = list_sums(values)
    for i in range(STEPS * BEAMS):
        block = jnp.where(diag, sums[32 * i : 32 * i + 32, :], 0.0)
        part[i // BEAMS, pl.ds(i % BEAMS, 1), :] = jnp.sum(block, axis=0, keepdims=True)
    pl.semaphore_wait(barrier, 22)

    blank = jnp.zeros((64, LANES), jnp.float32)

    def clear(i, carry):
        for ref in empty:
            ref[pl.ds(pl.multiple_of(i * 64, 64), 64), :] = blank
        return carry

    half_way = CX * CY * TILE // 128

    def spread(src, inbox, send, recv, where_to, peers, first):
        copies = []
        for d in range(1, peers):
            copy = pltpu.make_async_remote_copy(
                src_ref=src, dst_ref=inbox.at[d - 1], send_sem=send.at[d - 1], recv_sem=recv.at[d - 1],
                device_id=where_to(d), device_id_type=MESH,
            )
            copy.start()
            copies.append(copy)
        lax.fori_loop(first, first + half_way, clear, 0)
        for copy in copies:
            copy.wait()

    spread(part, inbox_a, send_a, recv_a, near, 8, 0)
    acc = part[...]
    for d in range(7):
        acc = acc + inbox_a[d]
    half[...] = acc
    spread(half, inbox_b, send_b, recv_b, far, 16, half_way)
    for d in range(15):
        acc = acc + inbox_b[d]

    total = acc * (1.0 / GATES)
    means = list_sums([jnp.where(diag, total[i // BEAMS, i % BEAMS : i % BEAMS + 1, :], 0.0) for i in range(STEPS * BEAMS)])
    for n in range(STEPS):
        at = 32 * BEAMS * n
        mean = jnp.zeros((32, LANES), jnp.float32)
        for b in range(BEAMS):
            mean = jnp.where(beam == float(b), means[at + 32 * b : at + 32 * b + 32, :], mean)
        misfit = jnp.where(beam >= 0.0, resid[n] - mean, 0.0)
        base = (6, 3, 0)[n]
        for c in range(3):
            if base + c < 8:
                vals_a[pl.ds(base + c, 32, stride=8), :] = slots[1 + c] * misfit
                continue
            for k in range(3):
                piece = jnp.where(third[...] == float(k), slots[1 + c] * misfit, 0.0)
                vals_b[pl.ds(k, 32, stride=8), :] = pltpu.roll(piece, NZ - 32 * k, 1)


def gather(take, table, third, slots, seen_obs):
    rows = pltpu.VMEM((256, LANES), jnp.float32)
    block = pltpu.VMEM((STEPS, BEAMS, LANES), jnp.float32)
    return pl.pallas_call(
        gather_kernel,
        out_shape=[f32(256, LANES), f32(256, LANES)] + [f32(CX * CY * TILE, LANES)] * COPIES,
        in_specs=[SMEM] + [VMEM] * 4,
        out_specs=[VMEM] * (2 + COPIES),
        scratch_shapes=[
            rows, rows, pltpu.VMEM((STEPS, 32, LANES), jnp.float32), block, block,
            pltpu.VMEM((7, STEPS, BEAMS, LANES), jnp.float32), pltpu.VMEM((15, STEPS, BEAMS, LANES), jnp.float32),
            pltpu.SemaphoreType.DMA((7,)), pltpu.SemaphoreType.DMA((7,)),
            pltpu.SemaphoreType.DMA((15,)), pltpu.SemaphoreType.DMA((15,)),
        ],
        compiler_params=pltpu.CompilerParams(collective_id=1, has_side_effects=True, vmem_limit_bytes=16 * MIB),
        name="gather",
    )(take, table, third, slots, seen_obs)


def scatter_kernel(give, vals_a, vals_b, *rest):
    f3, f2, f1 = rest[COPIES : COPIES + 3]
    sums = rest[COPIES + 3 : -1]
    layer = rest[-1]
    lane8 = lax.broadcasted_iota(jnp.int32, (8, LANES), 1)
    spare = spare_lanes()

    def place(g, carry):
        at = pl.multiple_of(g * 8, 8)
        va = vals_a[pl.ds(at, 8), :]
        vb = vals_b[pl.ds(at, 8), :]
        for j in range(LANES):
            code = give[g, j]
            to = pl.ds(pl.multiple_of(code >> 7, TILE), TILE)
            v = jnp.where(lane8 == j, va, jnp.where(spare == j, vb, 0.0))
            out = sums[j % COPIES]
            out[to, :] = out[to, :] + pltpu.roll(v, code & (LANES - 1), 1)
        return carry

    lax.fori_loop(0, 32, place, 0, unroll=4)
    keep = lane8 < NZ

    def unpack(y, carry):
        first = pl.multiple_of(y * CX * TILE, CX * TILE)
        for x in range(CX):
            at = pl.ds(first + x * TILE, TILE)
            layer[pl.ds(x * TILE, TILE), :] = sum(ref[at, :] for ref in sums)
        for r in range(0, CX, 8):
            rows = [layer[pl.ds(r * TILE + k, 8, stride=TILE), :] for k in range(8)]
            pieces = [pltpu.roll(rows[k], 32 * (k + 1), 1) for k in range(3)]
            ninth = jnp.where(lane8 < 32, pieces[0], jnp.where(lane8 < 64, pieces[1], pieces[2]))
            rows = [jnp.where(keep, v, 0.0) for v in rows[:3]] + rows[3:] + [jnp.where(keep, ninth, 0.0)]
            for i, out in enumerate((f3, f2, f1)):
                for c in range(3):
                    out[c, y, pl.ds(r, 8), :] = rows[3 * i + c]
        return carry

    lax.fori_loop(0, CY, unpack, 0, unroll=4)


def scatter(give, vals_a, vals_b, empty):
    table = f32(CX * CY * TILE, LANES)
    field = f32(3, CY, CX, LANES)
    return pl.pallas_call(
        scatter_kernel,
        out_shape=[field, field, field] + [table] * COPIES,
        in_specs=[SMEM] + [VMEM] * (2 + COPIES),
        out_specs=[VMEM] * (3 + COPIES),
        scratch_shapes=[pltpu.VMEM((CX * TILE, LANES), jnp.float32)],
        input_output_aliases={3 + i: 3 + i for i in range(COPIES)},
        compiler_params=pltpu.CompilerParams(vmem_limit_bytes=16 * MIB),
        name="scatter",
    )(give, vals_a, vals_b, *empty)[:3]


def adjoint_kernel(w0, w1, w2, f3, f2, f1, out, a3, a2, a1, sides, inbox, send, recv):
    n_gx, n_gy, gx, gy = sizes()
    where = (n_gx, n_gy, gx, gy)
    barrier = pltpu.get_barrier_semaphore()
    for target in (
        (lax.rem(gx + n_gx - 1, n_gx), gy), (lax.rem(gx + 1, n_gx), gy),
        (gx, lax.rem(gy + n_gy - 1, n_gy)), (gx, lax.rem(gy + 1, n_gy)),
    ):
        pl.semaphore_signal(barrier, inc=1, device_id=target, device_id_type=MESH)

    def fill(y, carry):
        for c in range(3):
            a3[c, y + 1, pl.ds(TOP, CX), :] = f3[c, y]
        return carry

    lax.fori_loop(0, CY, fill, 0)
    keep = levels()
    inside = inside_grid(*where)

    def meet_rims(src, dst, n):
        for s in range(4):
            factors = []
            for y in range(0, CY, 8):
                ref, at = layer_at(src, s, 1, s // 2, y)
                factors.append(HALF * (1.0 + ref[at]) if s % 2 else HALF * (1.0 - ref[at]))
            for c in range(3):
                for i, v in enumerate(rim_rows(inbox.at[n], OPPOSITE[s], c, inside[s])):
                    ref, at = layer_at(dst, s, 0, c, 8 * i)
                    ref[at] = ref[at] + factors[i] * v

    def pull(src, adj, dst, force):
        def body(y, r):
            for c, v in enumerate(pull_block(src, adj, y, r)):
                v = jnp.where(keep, v, 0.0)
                if force is not None:
                    v = v + force[c, y - 1, pl.ds(r - TOP, 8), :]
                dst[c, y, pl.ds(r, 8), :] = v
        return body

    for n, (src, adj, dst, force) in enumerate(((w2, a3, a2, f2), (w1, a2, a1, f1), (w0, a1, a3, None))):
        body = pull(src, adj, dst, force)
        pack_rims(adj, sides.at[n])
        if n == 0:
            pl.semaphore_wait(barrier, 4)
        copies = send_rims(sides.at[n], inbox.at[n], send.at[n], recv.at[n], *where)
        if n == 0:
            clear_rims((a3, a2, a1))
        over_tile(body)
        for copy in copies:
            copy.wait()
        meet_rims(src, dst, n)

    lane = lax.broadcasted_iota(jnp.int32, (CX, LANES), 1)
    for c in range(3):
        for y in range(0, CY, 4):
            v = [a3[c, y + 1 + i, pl.ds(TOP, CX), :] for i in range(4)]
            v = [v[0], pltpu.roll(v[1], 96, 1), pltpu.roll(v[2], 64, 1), pltpu.roll(v[3], 32, 1)]
            t = [
                jnp.where(lane < 96, v[0], v[1]),
                jnp.where(lane < 64, v[1], v[2]),
                jnp.where(lane < 32, v[2], v[3]),
            ]
            for i in range(3):
                out[c, :, pl.ds(y * NZ + LANES * i, LANES)] = t[i]


def adjoint(wides, fields):
    wide = pltpu.VMEM((3, WIDE, ROWS, LANES), jnp.float32)
    rim = pltpu.VMEM((STEPS, 4, 3, 24, LANES), jnp.float32)
    return pl.pallas_call(
        adjoint_kernel,
        out_shape=f32(3, CX, CY * NZ),
        in_specs=[VMEM] * 6,
        out_specs=VMEM,
        scratch_shapes=[wide] * 3 + [
            rim, rim, pltpu.SemaphoreType.DMA((STEPS, 4)), pltpu.SemaphoreType.DMA((STEPS, 4)),
        ],
        compiler_params=pltpu.CompilerParams(collective_id=2, has_side_effects=True, vmem_limit_bytes=24 * MIB),
        name="adjoint",
    )(*wides, *fields)


def local(initial_state, beam_dir, gate_obs, slot_beam, slot_cell):
    w0, w1, w2, table, take, give, third, slots, seen_obs = forward(
        initial_state, slot_cell[0].T, jnp.transpose(gate_obs[:, 0], (0, 2, 1)), slot_beam[0].T, beam_dir
    )
    vals_a, vals_b, *empty = gather(take, table, third, slots, seen_obs)
    fields = scatter(give, vals_a, vals_b, empty)
    return adjoint((w0, w1, w2), fields)


def solution(mesh):
    in_specs = (
        P(None, "gx", "gy"),
        P(None, ("gx", "gy")),
        P(None, ("gx", "gy"), None, None),
        P(("gx", "gy"), None, None),
        P(("gx", "gy"), None, None),
    )
    out_specs = P(None, "gx", "gy")
    return jax.shard_map(local, mesh=mesh, in_specs=in_specs, out_specs=out_specs, check_vma=False)
```
